32 devices in a mesh: wide: 8 (over z, y), narrow: 4 (over x, core).
Axes of the slice: x: 2, y: 2, z: 4, core: 2. Of those that a mesh axis runs over, the one named last changes fastest.
Arguments:
- tokens: bfloat16 [64, 600, 768], P(('wide', 'narrow')), may hold values from -6 to 6
- lengths: int32 [64], P(('wide', 'narrow')), may hold values from 256 to 600, as said below
- blocks: int32 [64, 600], P(('wide', 'narrow')), may hold values from 0 to 4, never falling along the last dimension, each value on 1 to 300 neighbouring positions
- ln1_gain: bfloat16 [768], P(('wide', 'narrow')), may hold values from 0.25 to 1.75
- ln1_bias: bfloat16 [768], P(('wide', 'narrow')), may hold values from -1.75 to 1.75
- qkv_weight: bfloat16 [768, 2304], P(('wide', 'narrow')), may hold values from -0.3125 to 0.3125
- qv_bias: bfloat16 [1536], P(('wide', 'narrow')), may hold values from -1.75 to 1.75
- out_weight: bfloat16 [768, 768], P(('wide', 'narrow')), may hold values from -1.25 to 1.25
- out_bias: bfloat16 [768], P(('wide', 'narrow')), may hold values from -1.75 to 1.75
- ln2_gain: bfloat16 [768], P(('wide', 'narrow')), may hold values from 0.25 to 1.75
- ln2_bias: bfloat16 [768], P(('wide', 'narrow')), may hold values from -1.75 to 1.75
- up_weight: bfloat16 [768, 3072], P(('wide', 'narrow')), may hold values from -0.21875 to 0.21875
- up_bias: bfloat16 [3072], P(('wide', 'narrow')), may hold values from -1.75 to 1.75
- down_weight: bfloat16 [3072, 768], P(('wide', 'narrow')), may hold values from -0.109375 to 0.109375
- down_bias: bfloat16 [768], P(('wide', 'narrow')), may hold values from -1.75 to 1.75
- cotangent: bfloat16 [64, 600, 768], P(('wide', 'narrow')), may hold values from -12 to 12
Outputs:
- output: bfloat16 [64, 600, 768], P(('wide', 'narrow'))
- input_grad: float32 [64, 600, 768], P(('wide', 'narrow'))
- ln1_gain_grad: float32 [768], P(('wide', 'narrow'))
- ln1_bias_grad: float32 [768], P(('wide', 'narrow'))
- qkv_weight_grad: float32 [768, 2304], P(('wide', 'narrow'))
- qv_bias_grad: float32 [1536], P(('wide', 'narrow'))
- out_weight_grad: float32 [768, 768], P(('wide', 'narrow'))
- out_bias_grad: float32 [768], P(('wide', 'narrow'))
- ln2_gain_grad: float32 [768], P(('wide', 'narrow'))
- ln2_bias_grad: float32 [768], P(('wide', 'narrow'))
- up_weight_grad: float32 [768, 3072], P(('wide', 'narrow'))
- up_bias_grad: float32 [3072], P(('wide', 'narrow'))
- down_weight_grad: float32 [3072, 768], P(('wide', 'narrow'))
- down_bias_grad: float32 [768], P(('wide', 'narrow'))
The draws below stay inside these ranges and needn't reach their ends.
Inputs may be any that keep to these rules, and one draw needn't show every extreme that they name: Slots at and after lengths[b] of item b are padding; some item has 600 real tokens and some 256. `blocks`: block ids of an item start at 0 at slot 0 and never fall along the slots.
All inputs are finite; a program needn't handle non-finite values.
Results may differ from the reference program's by a relative error of at most 0.012.
The reference program's roundings to bfloat16 on the way count: a program that leaves them out, or rounds other values in their place, can miss the bound.
Values may be sent and summed in bfloat16 or wider, within the bound.
No kernel may reach another device: no remote copies, remote signals or barrier semaphores. Data moves between devices by JAX's collectives and lax.ppermute only.
A program may use at most 256 MiB of HBM per device.

```python
import math
import jax
import jax.numpy as jnp
import numpy as np
from jax import lax

D = 768
FF = 3072
HEADS = 12
HEAD = 64
SLOTS = 600
MIN_LEN = 256
BLOCKS = 5
ITEMS = 64


def draw_lengths(key, part):
    first_key, second_key = jax.random.split(key)
    item_lengths = jax.random.randint(first_key, (ITEMS,), MIN_LEN, SLOTS + 1)
    chosen = jax.random.randint(second_key, (2,), 0, ITEMS)
    item_lengths = item_lengths.at[chosen[0]].set(SLOTS)
    other = (chosen[0] + 1 + chosen[1] % (ITEMS - 1)) % ITEMS
    item_lengths = item_lengths.at[other].set(MIN_LEN)
    return item_lengths.astype(jnp.int32)


def strengthened(drawn, stream_key, source, target, blocks, factor):
    def block_of(dim):
        return (jnp.arange(drawn.shape[dim]) // (drawn.shape[dim] // blocks)).reshape((-1,) + (1,) * (drawn.ndim - 1 - dim))

    near = jax.random.permutation(stream_key, blocks)[block_of(target)]
    second = (block_of(target) + blocks // 2) % blocks
    return jnp.where((block_of(source) == near) | (block_of(source) == second), factor * drawn, drawn)


def block_scale(rng, shape, cuts, low, largest):
    level, own = 1.0, jax.random.fold_in(rng, 6)
    for position, parts in cuts:
        draws = jnp.exp(jax.random.uniform(jax.random.fold_in(own, position), (parts,), jnp.float32, low / len(cuts), largest / len(cuts)))
        level = level * jnp.repeat(draws, shape[position] // parts).reshape([-1 if axis == position else 1 for axis in range(len(shape))])
    return level


def profile(amount, total, limit, lean):
    portions = [(1 << 20) // math.isqrt(standing ** lean) + 1 for standing in range(2, amount + 1)]
    surplus, counts = total - limit - (amount - 1), [1] * (amount - 1)
    while surplus > 0:
        candidates = [i for i in range(amount - 1) if counts[i] < limit]
        pool, left = sum([portions[i] for i in candidates]), surplus
        for i in candidates:
            extra = min(limit - counts[i], max(1, left * portions[i] // pool), surplus)
            counts[i] = counts[i] + extra
            surplus = surplus - extra
    return np.array([limit] + counts)


def uneven(key, amount, total, bound, slope):
    if amount == 2:
        one = jax.random.randint(key, (), max(1, total - bound), min(bound, total - 1) + 1)
        return jnp.stack([one, total - one])
    sizes = jnp.asarray(profile(amount, total, bound, slope), jnp.int32)
    twos = (amount - 1) // 2
    source_of, sink = sizes[1:1 + 2 * twos:2], sizes[2:2 + 2 * twos:2]
    slack = jnp.minimum(source_of - 1, bound - sink)
    shifted = jax.random.randint(jax.random.fold_in(key, 1), (twos,), 0, 1 << 20) % (slack + 1)
    sizes = sizes.at[1:1 + 2 * twos:2].set(source_of - shifted).at[2:2 + 2 * twos:2].set(sink + shifted)
    return sizes[jax.random.permutation(jax.random.fold_in(key, 2), amount)]


def normal_values(stream_key, shape, width, most, cuts=(), dtype=jnp.bfloat16):
    level = block_scale(stream_key, shape, cuts, -0.22, 0.18) if cuts else 1.0
    entries = jax.random.normal(stream_key, shape, jnp.float32) * width * level
    return jnp.minimum(jnp.maximum(entries, -most), most).astype(dtype)


def gaussian_with(key, shape, width, most, pieces, heavy, held_as=jnp.bfloat16):
    array = width * jax.random.normal(key, shape, jnp.float32)
    if pieces:
        array = array * block_scale(key, shape, pieces, -0.22, 0.18)
    return jnp.clip(strengthened(array, jax.random.fold_in(key, 3), *heavy), -most, most).astype(held_as)


def setup_inputs(seed: int = 0) -> dict:
    key_list = jax.random.split(jax.random.key(seed), 17)
    return {
        "tokens": normal_values(key_list[0], (ITEMS, SLOTS, D), 1.0, 6.0, ((0, 32),)),
        "lengths": draw_lengths(jax.random.fold_in(key_list[16], 71), 0),
        "blocks": jax.vmap(lambda own: jnp.searchsorted(jnp.cumsum(uneven(own, BLOCKS, SLOTS, SLOTS // 2, 0)), jnp.arange(SLOTS), side="right"))(jax.random.split(key_list[2], ITEMS)).reshape((ITEMS, SLOTS)).astype(jnp.int32),
        "ln1_gain": jnp.clip(1.0 + 0.15 * jax.random.normal(key_list[3], (D,), jnp.float32), 0.25, 1.75).astype(jnp.bfloat16),
        "ln1_bias": normal_values(key_list[4], (D,), 0.3, 1.75, ((0, 32),)),
        "qkv_weight": normal_values(key_list[5], (D, 3 * D), (D // 2) ** -0.5, 0.3125, ((0, 32),)),
        "qv_bias": normal_values(key_list[6], (2 * D,), 0.3, 1.75, ((0, 32),)),
        "out_weight": normal_values(key_list[7], (D, D), (D // 32) ** -0.5, 1.25, ((0, 32),)),
        "out_bias": normal_values(key_list[8], (D,), 0.3, 1.75, ((0, 32),)),
        "ln2_gain": jnp.clip(1.0 + 0.15 * jax.random.normal(key_list[9], (D,), jnp.float32), 0.25, 1.75).astype(jnp.bfloat16),
        "ln2_bias": normal_values(key_list[10], (D,), 0.3, 1.75, ((0, 32),)),
        "up_weight": normal_values(key_list[11], (D, FF), D ** -0.5, 0.21875, ((0, 32),)),
        "up_bias": normal_values(key_list[12], (FF,), 0.3, 1.75, ((0, 32),)),
        "down_weight": normal_values(key_list[13], (FF, D), FF ** -0.5, 0.109375, ((0, 32),)),
        "down_bias": normal_values(key_list[14], (D,), 0.3, 1.75, ((0, 32),)),
        "cotangent": gaussian_with(key_list[15], (ITEMS, SLOTS, D), 1.0, 12.0, ((0, 32),), (0, 2, 32, 2.75)),
    }


@jax.custom_vjp
def low(v):
    return lax.optimization_barrier(v.astype(jnp.bfloat16)).astype(jnp.float32)

@jax.custom_vjp
def low_back(v):
    return v

def low_keep(v):
    return (low(v), None)

def low_pass(kept, grad):
    return (grad,)

def back_keep(v):
    return (v, None)

def back_low(kept, grad):
    return (low(grad),)
low.defvjp(low_keep, low_pass)
low_back.defvjp(back_keep, back_low)
highest = lax.Precision.HIGHEST
masked_score = -1e+30
group_items = 4

def matmul(left, right):
    return jnp.dot(left, right, precision=highest)

def norm_layer(values, gain, shift):
    centred = values - lax.optimization_barrier(jnp.mean(values, axis=-1, keepdims=True))
    inverse = lax.rsqrt(lax.optimization_barrier(jnp.mean(centred * centred, axis=-1, keepdims=True)) + 1e-05)
    return centred * inverse * gain + shift

def attend_item(packed):
    queries, key_rows, value_rows, allowed = packed
    slot_count = queries.shape[0]
    heads_query = queries.reshape(slot_count, HEADS, HEAD)
    heads_key = key_rows.reshape(slot_count, HEADS, HEAD)
    heads_value = value_rows.reshape(slot_count, HEADS, HEAD)
    scores = low_back(jnp.einsum('qhd,khd->hqk', heads_query, heads_key, precision=highest) * HEAD ** (-0.5))
    scores = jnp.where(allowed[None], scores, masked_score)
    peak_score = lax.optimization_barrier(jnp.max(scores, axis=-1, keepdims=True))
    exponent = jnp.exp(scores - peak_score)
    probs = low(exponent / lax.optimization_barrier(jnp.sum(exponent, axis=-1, keepdims=True)))
    mixed_heads = jnp.einsum('hqk,khd->qhd', probs, heads_value, precision=highest)
    return mixed_heads.reshape(slot_count, D)

def forward(layer_weights, inputs, lengths, blocks):
    gain_one, shift_one, w_qkv, bias_qv, w_out, bias_out, gain_two, shift_two, w_up, bias_up, w_down, bias_down = layer_weights
    normed_one = low(norm_layer(inputs, gain_one, shift_one))
    projected = matmul(normed_one, w_qkv)
    queries = low_back(low(projected[..., :D] + bias_qv[:D]))
    key_rows = low_back(low(projected[..., D:2 * D]))
    value_rows = low_back(low(projected[..., 2 * D:] + bias_qv[D:]))
    slot_ids = lax.broadcasted_iota(jnp.int32, blocks.shape + (SLOTS,), 2)
    allowed = (blocks[:, None, :] <= blocks[:, :, None]) & (slot_ids < lengths[:, None, None])
    mixed_heads = lax.map(jax.checkpoint(attend_item), (queries, key_rows, value_rows, allowed))
    mixed_heads = low_back(low(mixed_heads))
    middle = inputs + low_back(matmul(mixed_heads, w_out) + bias_out)
    normed_two = low(norm_layer(middle, gain_two, shift_two))
    pre_active = low_back(matmul(normed_two, w_up) + bias_up)
    active = low(jax.nn.gelu(pre_active, approximate=True))
    branch_mlp = low_back(matmul(active, w_down) + bias_down)
    valid_rows = (lax.broadcasted_iota(jnp.int32, blocks.shape, 1) < lengths[:, None]).astype(jnp.float32)
    return (middle + branch_mlp) * valid_rows[..., None]

def reference(tokens, lengths, blocks, ln1_gain, ln1_bias, qkv_weight, qv_bias, out_weight, out_bias, ln2_gain, ln2_bias, up_weight, up_bias, down_weight, down_bias, cotangent):
    layer_weights = tuple((value.astype(jnp.float32) for value in (ln1_gain, ln1_bias, qkv_weight, qv_bias, out_weight, out_bias, ln2_gain, ln2_bias, up_weight, up_bias, down_weight, down_bias)))
    grouped_tokens = tokens.astype(jnp.float32).reshape(-1, group_items, SLOTS, D)
    grouped_lengths = lengths.reshape(-1, group_items)
    grouped_blocks = blocks.reshape(-1, group_items, SLOTS)
    grouped_cot = cotangent.astype(jnp.float32).reshape(-1, group_items, SLOTS, D)

    def step(totals, packed):
        group_tokens, group_lengths, group_blocks, group_cot = packed

        def local(weights_now, inputs):
            return forward(weights_now, inputs, group_lengths, group_blocks)
        result, pullback = jax.vjp(local, layer_weights, group_tokens)
        grads, input_grad = pullback(group_cot)
        totals = tuple((left + right for left, right in zip(totals, grads)))
        return (totals, (result.astype(jnp.bfloat16), input_grad))
    zeros = tuple((jnp.zeros_like(value) for value in layer_weights))
    totals, (outputs, input_grads) = lax.scan(step, zeros, (grouped_tokens, grouped_lengths, grouped_blocks, grouped_cot))
    return (outputs.reshape(ITEMS, SLOTS, D), input_grads.reshape(ITEMS, SLOTS, D), totals[0], totals[1], totals[2], totals[3], totals[4], totals[5], totals[6], totals[7], totals[8], totals[9], totals[10], totals[11])
```

```python
import jax
import jax.numpy as jnp
from jax import lax
from jax.experimental import pallas as pl
from jax.experimental.pallas import tpu as pltpu
from jax.sharding import PartitionSpec as P

D = 768
HEADS = 12
HEAD = 64
GROUP = 256
GROUPS = D // GROUP
PAIRS = GROUP // 128
EPS = 1e-05
MASKED = -1e30
AXES = ("wide", "narrow")
BF = jnp.bfloat16
F32 = jnp.float32
MIB = 1 << 20
VEC_ROWS = 16
SMALL = 128


def mm(a, b):
    return jnp.dot(a, b, preferred_element_type=F32)


def mm_nt(a, b):
    return lax.dot_general(a, b, (((1,), (1,)), ((), ())), preferred_element_type=F32)


def mm_tn(a, b):
    return lax.dot_general(a, b, (((0,), (0,)), ((), ())), preferred_element_type=F32)


def norm_parts(x):
    centred = x - jnp.mean(x, axis=-1, keepdims=True)
    inverse = lax.rsqrt(jnp.mean(centred * centred, axis=-1, keepdims=True) + EPS)
    return centred * inverse, inverse


def norm_back(d_normed, scaled, inverse, gain):
    h = d_normed * gain
    return inverse * (
        h
        - jnp.mean(h, axis=-1, keepdims=True)
        - scaled * jnp.mean(h * scaled, axis=-1, keepdims=True)
    )


def lane_mask(half, value):
    lane = lax.broadcasted_iota(jnp.int32, (1, 128), 1)
    return jnp.where((lane // HEAD) == half, value, 0.0).astype(BF)


def forward_kernel(
    tok_ref, wq_ref, wk_ref, wv_ref, vec_ref, bias_ref, kend_ref,
    n1_ref, q_ref, k_ref, v_ref, mixed_ref, lse_ref,
):
    slots = tok_ref.shape[1]

    @pl.when(pl.program_id(1) == 0)
    def _():
        scaled, _inverse = norm_parts(tok_ref[0].astype(F32))
        n1_ref[0] = (scaled * vec_ref[0:1, :] + vec_ref[1:2, :]).astype(BF)

    n1 = n1_ref[0]
    q_ref[0] = (mm(n1, wq_ref[...]) + bias_ref[2:3, :]).astype(BF)
    k_ref[0] = mm(n1, wk_ref[...]).astype(BF)
    v_ref[0] = (mm(n1, wv_ref[...]) + bias_ref[3:4, :]).astype(BF)
    rows = slots // 3
    lane = lax.broadcasted_iota(jnp.int32, (1, 128), 1)
    lse_parts = []
    for part in range(3):
        at = slice(part * rows, (part + 1) * rows)
        column = lax.broadcasted_iota(jnp.int32, (rows, slots), 1)
        allowed = column < kend_ref[0, at, :]
        lse_lanes = jnp.zeros((rows, 128), F32)
        for pair in range(PAIRS):
            cols = slice(pair * 128, (pair + 1) * 128)
            k2 = k_ref[0, :, cols]
            v2 = v_ref[0, :, cols]
            q2 = q_ref[0, at, cols]
            outs = []
            for half in range(2):
                scores = mm_nt(q2 * lane_mask(half, HEAD ** -0.5), k2)
                scores = jnp.where(allowed, scores, MASKED)
                peak = jnp.max(scores, axis=-1, keepdims=True)
                exponent = jnp.exp(scores - peak)
                total = jnp.sum(exponent, axis=-1, keepdims=True)
                probs = (exponent * (1.0 / total)).astype(BF)
                outs.append(mm(probs, v2))
                lse_lanes = jnp.where(lane == 2 * pair + half, peak + jnp.log(total), lse_lanes)
            mixed_ref[0, at, cols] = jnp.where(lane < HEAD, outs[0], outs[1]).astype(BF)
        lse_parts.append(lse_lanes)
    lse_ref[0] = jnp.concatenate(lse_parts, axis=0).T[:8, :]


def attention_forward(tokens, w_qk, w_v, vec, kend):
    items, slots, _ = tokens.shape
    rows = lambda i, g: (i, 0, 0)
    cols = lambda i, g: (i, 0, g)
    return pl.pallas_call(
        forward_kernel,
        grid=(items, GROUPS),
        in_specs=[
            pl.BlockSpec((1, slots, D), rows),
            pl.BlockSpec((D, GROUP), lambda i, g: (0, g)),
            pl.BlockSpec((D, GROUP), lambda i, g: (0, GROUPS + g)),
            pl.BlockSpec((D, GROUP), lambda i, g: (0, g)),
            pl.BlockSpec((VEC_ROWS, D), lambda i, g: (0, 0)),
            pl.BlockSpec((VEC_ROWS, GROUP), lambda i, g: (0, g)),
            pl.BlockSpec((1, slots, 1), rows),
        ],
        out_specs=[
            pl.BlockSpec((1, slots, D), rows),
            pl.BlockSpec((1, slots, GROUP), cols),
            pl.BlockSpec((1, slots, GROUP), cols),
            pl.BlockSpec((1, slots, GROUP), cols),
            pl.BlockSpec((1, slots, GROUP), cols),
            pl.BlockSpec((1, 8, slots), lambda i, g: (i, g, 0)),
        ],
        out_shape=[jax.ShapeDtypeStruct((items, slots, D), BF)] * 5
        + [jax.ShapeDtypeStruct((items, 8 * GROUPS, slots), F32)],
        compiler_params=pltpu.CompilerParams(vmem_limit_bytes=48 * MIB),
        cost_estimate=pl.CostEstimate(
            flops=2 * items * slots * D * 3 * D + 16 * items * HEADS * slots * slots * HEAD,
            bytes_accessed=30 * MIB,
            transcendentals=items * HEADS * slots * slots,
        ),
        name="attention_forward",
    )(tokens, w_qk, w_qk, w_v, vec, vec, kend)


GELU_SCALE = 0.7978845608028654
GELU_CUBE = 0.044715


def row_valid(len_ref, start, rows, slots, items):
    index = lax.broadcasted_iota(jnp.int32, (rows, 1), 0) + start
    valid = index < len_ref[0]
    for item in range(1, items):
        valid = valid | ((index >= item * slots) & (index < item * slots + len_ref[item]))
    return jnp.where(valid, 1.0, 0.0).astype(F32)


def mlp_kernel(stacked, items, slots):
    row_count = items * slots
    tile = row_count // 3

    def kernel(
        len_ref, mixed_ref, tok_ref, cot_ref, wout_ref, vec_ref, up_ref, down_ref,
        middle_ref, out_ref, dn2_ref, gbd_ref, gbu_ref, *rest,
    ):
        if stacked:
            grads = rest[0]
            n2, dlow, act, dpre, oacc, gu, gd, sems = rest[1:]
        else:
            gu_out, gd_out = rest[:2]
            n2, dlow, act, dpre, oacc, gu, gd, sems = rest[2:]
        b = pl.program_id(0)
        last = pl.num_programs(0) - 1
        slot = lax.rem(b, 2)

        def copies(step, where):
            if stacked:
                per = gu.shape[2]
                up_to = grads.at[:, pl.ds(pl.multiple_of(per * step, 8), per), :]
                down_to = grads.at[
                    pl.ds(gd.shape[1] * step, gd.shape[1]), 4 * per : 8 * per, :
                ]
            else:
                up_to = gu_out.at[:, pl.ds(pl.multiple_of(D * step, D), D)]
                down_to = gd_out.at[pl.ds(pl.multiple_of(D * step, D), D), :]
            return (
                pltpu.make_async_copy(gu.at[where], up_to, sems.at[0, where]),
                pltpu.make_async_copy(gd.at[where], down_to, sems.at[1, where]),
            )

        @pl.when(b == 0)
        def _():
            sums = jnp.zeros((1, D), F32)
            for part in range(3):
                at = slice(part * tile, (part + 1) * tile)
                middle = (
                    tok_ref[at, :].astype(F32) + mm(mixed_ref[at, :], wout_ref[...])
                ) + vec_ref[4:5, :]
                middle_ref[at, :] = middle
                scaled, _inverse = norm_parts(middle)
                n2[at, :] = (scaled * vec_ref[5:6, :] + vec_ref[6:7, :]).astype(BF)
                valid = row_valid(len_ref, part * tile, tile, slots, items)
                lower = cot_ref[at, :].astype(F32) * valid
                dlow[at, :] = lower.astype(BF)
                sums = sums + jnp.sum(lower, axis=0, keepdims=True)
            gbd_ref[...] = jnp.broadcast_to(sums, gbd_ref.shape)

        up = up_ref[...].reshape(D, D)
        down = down_ref[...].reshape(D, D)
        bias = vec_ref[pl.ds(8 + b, 1), :]
        sums = jnp.zeros((1, D), F32)
        for part in range(3):
            at = slice(part * tile, (part + 1) * tile)
            pre = mm(n2[at, :], up) + bias
            square = pre * pre
            half_t = 0.5 * jnp.tanh(GELU_SCALE * pre * (1.0 + GELU_CUBE * square))
            cdf = 0.5 + half_t
            active = (pre * cdf).astype(BF)
            act[at, :] = active
            slope = cdf + pre * (0.5 - 2.0 * half_t * half_t) * (
                GELU_SCALE + (3.0 * GELU_CUBE * GELU_SCALE) * square
            )
            d_pre = (mm_nt(dlow[at, :], down) * slope).astype(BF)
            dpre[at, :] = d_pre
            sums = sums + jnp.sum(d_pre.astype(F32), axis=0, keepdims=True)
            branch = mm(active, down)
            d_n2 = mm_nt(d_pre, up)

            @pl.when(b == 0)
            def _():
                oacc[at, :] = branch
                dn2_ref[at, :] = d_n2

            @pl.when(b > 0)
            def _():
                oacc[at, :] += branch
                dn2_ref[at, :] += d_n2

        gbu_ref[...] = jnp.broadcast_to(sums, gbu_ref.shape)

        @pl.when(b >= 2)
        def _():
            for copy in copies(b - 2, slot):
                copy.wait()

        gu[slot] = mm_tn(n2[...], dpre[...]).reshape(gu.shape[1:]).astype(BF)
        gd[slot] = mm_tn(act[...], dlow[...]).reshape(gd.shape[1:]).astype(BF)
        for copy in copies(b, slot):
            copy.start()

        @pl.when(b == last)
        def _():
            for part in range(3):
                at = slice(part * tile, (part + 1) * tile)
                valid = row_valid(len_ref, part * tile, tile, slots, items)
                whole = middle_ref[at, :] + (oacc[at, :] + vec_ref[7:8, :])
                out_ref[at, :] = (whole * valid).astype(BF)
            for step, where in ((last - 1, 1 - slot), (last, slot)):
                for copy in copies(step, where):
                    copy.wait()

    return kernel


def feed_forward(lengths, mixed, tokens, cotangent, w_vo, vec, up, down, stacked, items, slots):
    row_count = items * slots
    steps = 4
    once = pl.Buffered(1)
    fixed = lambda b, *_: (0, 0)
    if stacked:
        devices, stack, _ = up.shape
        per = stack // 8
        up_spec = pl.BlockSpec((devices, per, D), lambda b, *_: (0, b, 0))
        down_spec = pl.BlockSpec((devices // 4, 4 * per, D), lambda b, *_: (b, 1, 0))
        grad_shapes = [jax.ShapeDtypeStruct((devices, stack, D), BF)]
        gu_shape, gd_shape = (devices, per, D), (devices // 4, 4 * per, D)
    else:
        up_spec = pl.BlockSpec((D, D), lambda b, *_: (0, b))
        down_spec = pl.BlockSpec((D, D), lambda b, *_: (b, 0))
        grad_shapes = [
            jax.ShapeDtypeStruct((D, steps * D), BF),
            jax.ShapeDtypeStruct((steps * D, D), BF),
        ]
        gu_shape = gd_shape = (D, D)
    return pl.pallas_call(
        mlp_kernel(stacked, items, slots),
        grid_spec=pltpu.PrefetchScalarGridSpec(
            num_scalar_prefetch=1,
            grid=(steps,),
            in_specs=[
                pl.BlockSpec((row_count, D), fixed, pipeline_mode=once),
                pl.BlockSpec((row_count, D), fixed, pipeline_mode=once),
                pl.BlockSpec((row_count, D), fixed, pipeline_mode=once),
                pl.BlockSpec((D, D), lambda b, *_: (0, 1), pipeline_mode=once),
                pl.BlockSpec((VEC_ROWS, D), fixed),
                up_spec,
                down_spec,
            ],
            out_specs=[
                pl.BlockSpec((row_count, D), fixed, pipeline_mode=once),
                pl.BlockSpec((row_count, D), fixed, pipeline_mode=once),
                pl.BlockSpec((row_count, D), fixed, pipeline_mode=once),
                pl.BlockSpec((8, D), fixed),
                pl.BlockSpec((8, D), lambda b, *_: (0, b)),
            ]
            + [pl.BlockSpec(memory_space=pl.ANY)] * len(grad_shapes),
            scratch_shapes=[
                pltpu.VMEM((row_count, D), BF),
                pltpu.VMEM((row_count, D), BF),
                pltpu.VMEM((row_count, D), BF),
                pltpu.VMEM((row_count, D), BF),
                pltpu.VMEM((row_count, D), F32),
                pltpu.VMEM((2,) + gu_shape, BF),
                pltpu.VMEM((2,) + gd_shape, BF),
                pltpu.SemaphoreType.DMA((2, 2)),
            ],
        ),
        out_shape=[
            jax.ShapeDtypeStruct((row_count, D), F32),
            jax.ShapeDtypeStruct((row_count, D), BF),
            jax.ShapeDtypeStruct((row_count, D), F32),
            jax.ShapeDtypeStruct((8, D), F32),
            jax.ShapeDtypeStruct((8, steps * D), F32),
        ]
        + grad_shapes,
        compiler_params=pltpu.CompilerParams(vmem_limit_bytes=60 * MIB),
        cost_estimate=pl.CostEstimate(
            flops=2 * row_count * D * D * 25,
            bytes_accessed=36 * MIB,
            transcendentals=row_count * 4 * D,
        ),
        name="feed_forward",
    )(lengths, mixed, tokens, cotangent, w_vo, vec, up, down)


def middle_kernel(slots):
    def kernel(
        len_ref, dn2_ref, middle_ref, cot_ref, mixed_ref, wout_ref, vec_ref,
        dmid_ref, dmix_ref, delta_ref, gout_ref, sums_ref, acc,
    ):
        i = pl.program_id(0)
        last = pl.num_programs(0) - 1
        scaled, inverse = norm_parts(middle_ref[0])
        d_n2 = dn2_ref[0]
        valid = jnp.where(
            lax.broadcasted_iota(jnp.int32, (slots, 1), 0) < len_ref[i], 1.0, 0.0
        ).astype(F32)
        d_middle = cot_ref[0].astype(F32) * valid + norm_back(
            d_n2, scaled, inverse, vec_ref[5:6, :]
        )
        dmid_ref[0] = d_middle
        branch = d_middle.astype(BF)
        mixed = mixed_ref[0]
        d_mixed = mm_nt(branch, wout_ref[...]).astype(BF)
        dmix_ref[0] = d_mixed
        product = d_mixed.astype(F32) * mixed.astype(F32)
        row = lax.broadcasted_iota(jnp.int32, (8 * GROUPS, D), 0)
        lane = lax.broadcasted_iota(jnp.int32, (8 * GROUPS, D), 1)
        pick = jnp.where(
            (lane // HEAD == 4 * (row // 8) + row % 8) & (row % 8 < 4), 1.0, 0.0
        ).astype(BF)
        high = product.astype(BF)
        low = (product - high.astype(F32)).astype(BF)
        delta_ref[0] = mm_nt(pick, high) + mm_nt(pick, low)
        sums = jnp.concatenate(
            [
                jnp.sum(d_n2 * scaled, axis=0, keepdims=True),
                jnp.sum(d_n2, axis=0, keepdims=True),
                jnp.sum(branch.astype(F32), axis=0, keepdims=True),
                jnp.zeros((5, D), F32),
            ],
            axis=0,
        )
        part = mm_tn(mixed, branch)

        @pl.when(i == 0)
        def _():
            sums_ref[...] = sums
            acc[...] = part

        @pl.when(i > 0)
        def _():
            sums_ref[...] += sums
            acc[...] += part

        @pl.when(i == last)
        def _():
            gout_ref[...] = acc[...].astype(BF)

    return kernel


def middle_backward(lengths, d_n2, middle, cotangent, mixed, w_vo, vec):
    items, slots, _ = mixed.shape
    rows = lambda i, *_: (i, 0, 0)
    fixed = lambda i, *_: (0, 0)
    block = pl.BlockSpec((1, slots, D), rows)
    return pl.pallas_call(
        middle_kernel(slots),
        grid_spec=pltpu.PrefetchScalarGridSpec(
            num_scalar_prefetch=1,
            grid=(items,),
            in_specs=[
                block, block, block, block,
                pl.BlockSpec((D, D), lambda i, *_: (0, 1)),
                pl.BlockSpec((VEC_ROWS, D), fixed),
            ],
            out_specs=[
                block, block,
                pl.BlockSpec((1, 8 * GROUPS, slots), rows),
                pl.BlockSpec((D, D), fixed),
                pl.BlockSpec((8, D), fixed),
            ],
            scratch_shapes=[pltpu.VMEM((D, D), F32)],
        ),
        out_shape=[
            jax.ShapeDtypeStruct((items, slots, D), F32),
            jax.ShapeDtypeStruct((items, slots, D), BF),
            jax.ShapeDtypeStruct((items, 8 * GROUPS, slots), F32),
            jax.ShapeDtypeStruct((D, D), BF),
            jax.ShapeDtypeStruct((8, D), F32),
        ],
        compiler_params=pltpu.CompilerParams(vmem_limit_bytes=56 * MIB),
        cost_estimate=pl.CostEstimate(
            flops=4 * items * slots * D * D, bytes_accessed=18 * MIB, transcendentals=0
        ),
        name="middle_backward",
    )(lengths, d_n2, middle, cotangent, mixed, w_vo, vec)


def backward_kernel(
    q_ref, k_ref, v_ref, dmix_ref, lse_ref, delta_ref, kend_ref, n1_ref,
    wq_ref, wk_ref, wv_ref, tok_ref, dmid_ref, vec_ref,
    gq_ref, gk_ref, gv_ref, grad_ref, gbias_ref, sums_ref,
    dqkv, dn1, acc,
):
    g = pl.program_id(0)
    i = pl.program_id(1)
    last_group = pl.num_programs(0) - 1
    last_item = pl.num_programs(1) - 1
    slots = q_ref.shape[1]
    key = lax.broadcasted_iota(jnp.int32, (slots, slots), 0)
    allowed = key < kend_ref[0]
    for pair in range(PAIRS):
        cols = slice(pair * 128, (pair + 1) * 128)
        q2 = q_ref[0, :, cols]
        k2 = k_ref[0, :, cols]
        v2 = v_ref[0, :, cols]
        o2 = dmix_ref[0, :, cols]
        dq = dk = dv = None
        for half in range(2):
            head = 2 * pair + half
            qm = q2 * lane_mask(half, HEAD ** -0.5)
            km = k2 * lane_mask(half, 1.0)
            om = o2 * lane_mask(half, 1.0)
            scores = mm_nt(k2, qm)
            probs = jnp.exp(
                jnp.where(allowed, scores, MASKED) - lse_ref[0, head : head + 1, :]
            )
            d_probs = mm_nt(v2, om)
            d_scores = (probs * (d_probs - delta_ref[0, head : head + 1, :])).astype(BF)
            dv_half = mm(probs.astype(BF), om)
            dk_half = mm(d_scores, qm)
            dq_half = mm_tn(d_scores, km)
            dv = dv_half if dv is None else dv + dv_half
            dk = dk_half if dk is None else dk + dk_half
            dq = dq_half if dq is None else dq + dq_half
        dqkv[:, pair * 128 : (pair + 1) * 128] = (dq * HEAD ** -0.5).astype(BF)
        dqkv[:, GROUP + pair * 128 : GROUP + (pair + 1) * 128] = dk.astype(BF)
        dqkv[:, 2 * GROUP + pair * 128 : 2 * GROUP + (pair + 1) * 128] = dv.astype(BF)
    packed = dqkv[...]
    bias = jnp.sum(packed.astype(F32), axis=0, keepdims=True)
    bias = jnp.broadcast_to(bias, gbias_ref.shape)
    part = mm_tn(n1_ref[0], packed)

    @pl.when(i == 0)
    def _():
        acc[...] = part
        gbias_ref[...] = bias

    @pl.when(i > 0)
    def _():
        acc[...] += part
        gbias_ref[...] += bias

    @pl.when(i == last_item)
    def _():
        gq_ref[...] = acc[:, :GROUP].astype(BF)
        gk_ref[...] = acc[:, GROUP : 2 * GROUP].astype(BF)
        gv_ref[...] = acc[:, 2 * GROUP :].astype(BF)

    d_n1 = (
        mm_nt(packed[:, :GROUP], wq_ref[...])
        + mm_nt(packed[:, GROUP : 2 * GROUP], wk_ref[...])
        + mm_nt(packed[:, 2 * GROUP :], wv_ref[...])
    )

    @pl.when(g == 0)
    def _():
        dn1[i] = d_n1

    @pl.when(g > 0)
    def _():
        dn1[i] += d_n1

    @pl.when(g == last_group)
    def _():
        scaled, inverse = norm_parts(tok_ref[0].astype(F32))
        whole = dn1[i]
        grad_ref[0] = dmid_ref[0] + norm_back(whole, scaled, inverse, vec_ref[0:1, :])
        sums = jnp.concatenate(
            [
                jnp.sum(whole * scaled, axis=0, keepdims=True),
                jnp.sum(whole, axis=0, keepdims=True),
                jnp.zeros((6, D), F32),
            ],
            axis=0,
        )

        @pl.when(i == 0)
        def _():
            sums_ref[...] = sums

        @pl.when(i > 0)
        def _():
            sums_ref[...] += sums


def attention_backward(q, k, v, d_mixed, lse, delta, kend_row, n1, w_qk, w_v, tokens, d_middle, vec):
    items, slots, _ = q.shape
    rows = lambda g, i: (i, 0, 0)
    cols = lambda g, i: (i, 0, g)
    late = lambda g, i: (jnp.where(g == GROUPS - 1, i, 0), 0, 0)
    block = pl.BlockSpec((1, slots, GROUP), cols)
    table = pl.BlockSpec((1, 8, slots), lambda g, i: (i, g, 0))
    weight = pl.BlockSpec((D, GROUP), lambda g, i: (0, g))
    return pl.pallas_call(
        backward_kernel,
        grid=(GROUPS, items),
        in_specs=[
            block, block, block, block, table, table,
            pl.BlockSpec((1, 1, slots), rows),
            pl.BlockSpec((1, slots, D), rows),
            weight,
            pl.BlockSpec((D, GROUP), lambda g, i: (0, GROUPS + g)),
            weight,
            pl.BlockSpec((1, slots, D), late),
            pl.BlockSpec((1, slots, D), late),
            pl.BlockSpec((VEC_ROWS, D), lambda g, i: (0, 0)),
        ],
        out_specs=[
            weight, weight, weight,
            pl.BlockSpec((1, slots, D), late),
            pl.BlockSpec((8, 3 * GROUP), lambda g, i: (0, g)),
            pl.BlockSpec((8, D), lambda g, i: (0, 0)),
        ],
        out_shape=[jax.ShapeDtypeStruct((D, D), BF)] * 3
        + [
            jax.ShapeDtypeStruct((items, slots, D), F32),
            jax.ShapeDtypeStruct((8, 3 * D), F32),
            jax.ShapeDtypeStruct((8, D), F32),
        ],
        scratch_shapes=[
            pltpu.VMEM((slots, 3 * GROUP), BF),
            pltpu.VMEM((items, slots, D), F32),
            pltpu.VMEM((D, 3 * GROUP), F32),
        ],
        compiler_params=pltpu.CompilerParams(vmem_limit_bytes=56 * MIB),
        cost_estimate=pl.CostEstimate(
            flops=4 * items * slots * D * 3 * D + 40 * items * HEADS * slots * slots * HEAD,
            bytes_accessed=36 * MIB,
            transcendentals=items * HEADS * slots * slots,
        ),
        name="attention_backward",
    )(q, k, v, d_mixed, lse, delta, kend_row, n1, w_qk, w_qk, w_v, tokens, d_middle, vec)


def swap(x, axis, bit, size):
    return lax.ppermute(x, axis, [(i, i ^ (1 << bit)) for i in range(size)])


def own_bit(axis, bit):
    return (lax.axis_index(axis) >> bit) & 1


def doubled(x, axis, bit, size, at):
    other = jnp.expand_dims(swap(x, axis, bit, size), at)
    mine = jnp.expand_dims(x, at)
    return jnp.where(
        own_bit(axis, bit) == 0,
        jnp.concatenate([mine, other], at),
        jnp.concatenate([other, mine], at),
    )


def halved(x, axis, bit, size, at):
    me = own_bit(axis, bit)
    send = lax.dynamic_index_in_dim(x, 1 - me, at, keepdims=False).astype(BF)
    keep = lax.dynamic_index_in_dim(x, me, at, keepdims=False)
    return keep.astype(F32) + swap(send, axis, bit, size).astype(F32)


def gather_rows(x, cut, sizes):
    rows = x.shape[0]
    wide, narrow = sizes
    if sizes != (8, 4):
        whole = lax.all_gather(x, AXES, axis=0, tiled=True)
        return whole[:, :cut], whole[:, cut:]
    x = doubled(x, "wide", 2, wide, 0)
    x = doubled(x, "wide", 1, wide, 1)
    a, b = x[..., :cut], x[..., cut:]
    a = doubled(a, "wide", 0, wide, 2)
    b = doubled(b, "narrow", 1, narrow, 2)
    a = doubled(a, "narrow", 1, narrow, 3)
    b = doubled(b, "wide", 0, wide, 2)
    a = doubled(a, "narrow", 0, narrow, 4)
    b = doubled(b, "narrow", 0, narrow, 4)
    count = wide * narrow * rows
    return a.reshape(count, -1), b.reshape(count, -1)


def scatter_rows(a, b, sizes):
    wide, narrow = sizes
    if sizes != (8, 4):
        scatter = lambda x: lax.psum_scatter(
            x.astype(F32), AXES, scatter_dimension=0, tiled=True
        )
        return scatter(a), scatter(b)
    rows = a.shape[0] // (wide * narrow)
    split = (2, 2, 2, 2, 2, rows, -1)
    a = halved(a.reshape(split), "narrow", 0, narrow, 4)
    b = halved(b.reshape(split), "narrow", 0, narrow, 4)
    a = halved(a, "narrow", 1, narrow, 3)
    b = halved(b, "wide", 0, wide, 2)
    a = halved(a, "wide", 0, wide, 2)
    b = halved(b, "narrow", 1, narrow, 2)
    cut = a.shape[-1]
    x = jnp.concatenate([a, b], axis=-1)
    x = halved(x, "wide", 1, wide, 1)
    x = halved(x, "wide", 2, wide, 0)
    return x[:, :cut], x[:, cut:]


def body(sizes):
    def run(
        tokens, lengths, blocks, ln1_gain, ln1_bias, qkv_weight, qv_bias, out_weight, out_bias,
        ln2_gain, ln2_bias, up_weight, up_bias, down_weight, down_bias, cotangent,
    ):
        items, slots, _ = tokens.shape
        row_count = items * slots
        rows = qkv_weight.shape[0]
        devices = sizes[0] * sizes[1]
        stacked = rows % 8 == 0

        if stacked:
            pack = jnp.concatenate(
                [up_weight[:, b * D : (b + 1) * D] for b in range(4)] + [down_weight], axis=0
            )
            whole_ffn = lax.all_gather(pack, AXES, axis=0, tiled=True)
            up = down = whole_ffn.reshape(devices, 8 * rows, D)
        else:
            up = lax.all_gather(up_weight, AXES, axis=0, tiled=True)
            down = lax.all_gather(down_weight, AXES, axis=0, tiled=True)

        column = lambda v: v.reshape(rows, -1)
        small = jnp.concatenate(
            [
                column(ln1_gain), column(ln1_bias), column(qv_bias), column(out_bias),
                column(ln2_gain), column(ln2_bias), column(up_bias), column(down_bias),
            ],
            axis=1,
        )
        small = jnp.pad(small, ((0, 0), (0, SMALL - small.shape[1])))
        first = jnp.concatenate([qkv_weight, out_weight, small], axis=1)
        w_qk, w_vo = gather_rows(first, 2 * D, sizes)
        table = w_vo[:, 2 * D :].astype(F32)
        vec = jnp.concatenate(
            [
                table[:, 0:2].T,
                table[:, 2:4].reshape(2, D),
                table[:, 4:7].T,
                table[:, 11:12].T,
                table[:, 7:11].reshape(4, D),
                jnp.zeros((4, D), F32),
            ],
            axis=0,
        )

        ends = jnp.sum(
            (blocks[:, None, :] <= blocks[:, :, None]).astype(jnp.int32), axis=-1
        )
        kend = jnp.minimum(ends, lengths[:, None])

        n1, q, k, v, mixed, lse = attention_forward(
            tokens, w_qk, w_vo, vec, kend.reshape(items, slots, 1)
        )
        flat = lambda t: t.reshape(row_count, D)
        cube = lambda t: t.reshape(items, slots, D)
        middle, output, d_n2, gb_down, gb_up, *grads = feed_forward(
            lengths, flat(mixed), flat(tokens), flat(cotangent), w_vo, vec, up, down,
            stacked, items, slots,
        )
        if stacked:
            own = lax.psum_scatter(
                grads[0].reshape(devices * 8 * rows, D), AXES, scatter_dimension=0, tiled=True
            ).astype(F32)
            grad_up = jnp.concatenate(
                [own[b * rows : (b + 1) * rows] for b in range(4)], axis=1
            )
            grad_down = own[4 * rows :]
        else:
            grad_up = lax.psum_scatter(
                grads[0].astype(F32), AXES, scatter_dimension=0, tiled=True
            )
            grad_down = lax.psum_scatter(
                grads[1].astype(F32), AXES, scatter_dimension=0, tiled=True
            )
        d_middle, d_mixed, delta, g_out, sums2 = middle_backward(
            lengths, cube(d_n2), cube(middle), cotangent, mixed, w_vo, vec
        )
        gq, gk, gv, input_grad, gbias, sums1 = attention_backward(
            q, k, v, d_mixed, lse, delta, kend.reshape(items, 1, slots), n1,
            w_qk, w_vo, tokens, d_middle, vec,
        )
        gbias = gbias[0].reshape(GROUPS, 3, GROUP)
        tall = lambda value: value.reshape(D, -1)
        small_grads = jnp.concatenate(
            [
                sums1[0:2].T,
                tall(jnp.concatenate([gbias[:, 0].reshape(D), gbias[:, 2].reshape(D)])),
                sums2[2:3].T,
                sums2[0:2].T,
                tall(gb_up[0]),
                gb_down[0:1].T,
            ],
            axis=1,
        )
        small_grads = jnp.pad(small_grads, ((0, 0), (0, SMALL - small_grads.shape[1])))
        own_qk, own_vo = scatter_rows(
            jnp.concatenate([gq, gk], axis=1),
            jnp.concatenate([gv, g_out, small_grads.astype(BF)], axis=1),
            sizes,
        )
        own_small = own_vo[:, 2 * D :]
        return (
            cube(output),
            input_grad,
            own_small[:, 0],
            own_small[:, 1],
            jnp.concatenate([own_qk, own_vo[:, :D]], axis=1),
            own_small[:, 2:4].reshape(-1),
            own_vo[:, D : 2 * D],
            own_small[:, 4],
            own_small[:, 5],
            own_small[:, 6],
            grad_up,
            own_small[:, 7:11].reshape(-1),
            grad_down,
            own_small[:, 11],
        )

    return run


def solution(mesh):
    sizes = (mesh.shape["wide"], mesh.shape["narrow"])
    one = P(AXES)
    two = P(AXES, None)
    three = P(AXES, None, None)
    return jax.shard_map(
        body(sizes),
        mesh=mesh,
        in_specs=(
            three, one, two, one, one, two, one, two, one, one, one, two, one, two, one, three,
        ),
        out_specs=(
            three, three, one, one, two, one, two, one, one, one, two, one, two, one,
        ),
        check_vma=False,
    )
```

```python
import jax
import jax.numpy as jnp
from jax import lax
from jax.experimental import pallas as pl
from jax.experimental.pallas import tpu as pltpu
from jax.sharding import PartitionSpec as P

D = 768
HEADS = 12
HEAD = 64
GROUP = 256
GROUPS = D // GROUP
PAIRS = GROUP // 128
EPS = 1e-05
MASKED = -1e30
AXES = ("wide", "narrow")
BF = jnp.bfloat16
F32 = jnp.float32
MIB = 1 << 20
VEC_ROWS = 16
SMALL = 128


def mm(a, b):
    return jnp.dot(a, b, preferred_element_type=F32)


def mm_nt(a, b):
    return lax.dot_general(a, b, (((1,), (1,)), ((), ())), preferred_element_type=F32)


def mm_tn(a, b):
    return lax.dot_general(a, b, (((0,), (0,)), ((), ())), preferred_element_type=F32)


def norm_parts(x):
    centred = x - jnp.mean(x, axis=-1, keepdims=True)
    inverse = lax.rsqrt(jnp.mean(centred * centred, axis=-1, keepdims=True) + EPS)
    return centred * inverse, inverse


def norm_back(d_normed, scaled, inverse, gain):
    h = d_normed * gain
    return inverse * (
        h
        - jnp.mean(h, axis=-1, keepdims=True)
        - scaled * jnp.mean(h * scaled, axis=-1, keepdims=True)
    )


def lane_mask(half, value):
    lane = lax.broadcasted_iota(jnp.int32, (1, 128), 1)
    return jnp.where((lane // HEAD) == half, value, 0.0).astype(BF)


COLUMNS = (("ln1_gain", 1), ("ln1_bias", 1), ("qv_bias", 2), ("out_bias", 1), ("ln2_gain", 1), ("ln2_bias", 1), ("up_bias", 4), ("down_bias", 1))


def pack_kernel(stacked):
    def kernel(*refs):
        vectors, (qkv_ref, out_ref, up_ref, down_ref, first_ref) = refs[:8], refs[8:13]
        rows = qkv_ref.shape[0]
        lines = []
        for ref, (_name, count) in zip(vectors, COLUMNS):
            line = ref[...].astype(F32)
            lines += [line[:, j * rows : (j + 1) * rows] for j in range(count)]
        table = jnp.concatenate(lines + [jnp.zeros((SMALL - len(lines), rows), F32)], axis=0)
        first_ref[:, : 3 * D] = qkv_ref[...]
        first_ref[:, 3 * D :] = table.T.astype(BF)
        if stacked:
            rest_ref = refs[13]
            for b in range(4):
                rest_ref[b * rows : (b + 1) * rows, :] = up_ref[:, b * D : (b + 1) * D]
            rest_ref[4 * rows : 8 * rows, :] = down_ref[...]
            rest_ref[8 * rows :, :] = out_ref[...]

    return kernel


def pack_parameters(vectors, qkv, out, up, down, stacked):
    rows = qkv.shape[0]
    shapes = [jax.ShapeDtypeStruct((rows, 3 * D + SMALL), BF)]
    if stacked:
        shapes.append(jax.ShapeDtypeStruct((9 * rows, D), BF))
    return pl.pallas_call(
        pack_kernel(stacked),
        out_shape=shapes,
        compiler_params=pltpu.CompilerParams(vmem_limit_bytes=16 * MIB),
        name="pack_parameters",
    )(*[v.reshape(1, -1) for v in vectors], qkv, out, up, down)


def from_table(lines, count, rows, start, pick_rows):
    lane = lax.broadcasted_iota(jnp.int32, (1, D), 1) + start
    first = start // count // 128 * 128
    place = lax.broadcasted_iota(jnp.int32, (pick_rows, D), 0) + first
    at = lax.broadcasted_iota(jnp.int32, (pick_rows, D), 1) + start
    pick = (place == rows * (at // (count * rows)) + at % rows).astype(F32).astype(BF)
    lines = mm(lines[:, first : first + pick_rows].astype(BF), pick)
    which = lane % (count * rows) // rows
    line = lines[0:1, :]
    for j in range(1, count):
        line = jnp.where(which == j, lines[j : j + 1, :], line)
    return line


def unpack_kernel(rows):
    def kernel(table_ref, vec_ref):
        lines = table_ref[...].astype(F32).T
        vec_ref[0:2, :] = lines[0:2, :]
        vec_ref[2:3, :] = from_table(lines[2:4, :], 2, rows, 0, D // 2)
        vec_ref[3:4, :] = from_table(lines[2:4, :], 2, rows, D, D // 2)
        vec_ref[4:7, :] = lines[4:7, :]
        vec_ref[7:8, :] = lines[11:12, :]
        for b in range(4):
            vec_ref[8 + b : 9 + b, :] = from_table(lines[7:11, :], 4, rows, b * D, 256)
        vec_ref[12:16, :] = jnp.zeros((4, D), F32)

    return kernel


def unpack_small(first, rows):
    return pl.pallas_call(
        unpack_kernel(rows),
        grid=(1,),
        in_specs=[pl.BlockSpec((D, SMALL), lambda i: (0, 3 * D // SMALL))],
        out_specs=pl.BlockSpec((VEC_ROWS, D), lambda i: (0, 0)),
        out_shape=jax.ShapeDtypeStruct((VEC_ROWS, D), F32),
        compiler_params=pltpu.CompilerParams(vmem_limit_bytes=16 * MIB),
        name="unpack_small",
    )(first)


def to_table(line, count, rows, start, pick_rows, column):
    row = lax.broadcasted_iota(jnp.int32, (SMALL, D), 0)
    at = lax.broadcasted_iota(jnp.int32, (SMALL, D), 1) + start
    spread = jnp.where(row - column == at % (count * rows) // rows, line, 0.0).astype(BF)
    place = lax.broadcasted_iota(jnp.int32, (pick_rows, D), 0) + start // count
    lane = lax.broadcasted_iota(jnp.int32, (pick_rows, D), 1) + start
    pick = (place == rows * (lane // (count * rows)) + lane % rows).astype(F32).astype(BF)
    return mm_nt(pick, spread)


def small_kernel(rows):
    def kernel(norm_ref, qkv_ref, mid_ref, up_ref, down_ref, out_ref):
        row = lax.broadcasted_iota(jnp.int32, (SMALL, D), 0)
        plain = jnp.zeros((SMALL, D), F32)
        for at, line in (
            (4, mid_ref[2:3, :]), (5, mid_ref[0:1, :]), (6, mid_ref[1:2, :]),
            (11, down_ref[0:1, :]),
        ):
            plain = jnp.where(row == at, line, plain)
        halves = []
        for part, which in enumerate((0, 2)):
            line = jnp.concatenate(
                [
                    qkv_ref[0:1, g * D + which * GROUP : g * D + (which + 1) * GROUP]
                    for g in range(GROUPS)
                ],
                axis=1,
            )
            halves.append(to_table(line, 2, rows, part * D, D // 2, 2))
        quarters = [
            to_table(up_ref[0:1, b * D : (b + 1) * D], 4, rows, b * D, D // 4, 7)
            for b in range(4)
        ]
        total = plain.T + norm_ref[...] + jnp.concatenate(halves, axis=0)
        out_ref[...] = (total + jnp.concatenate(quarters, axis=0)).astype(BF)

    return kernel


def pack_small(norm_sums, qkv_sums, mid_sums, up_sums, down_sums, rows):
    return pl.pallas_call(
        small_kernel(rows),
        out_shape=jax.ShapeDtypeStruct((D, SMALL), BF),
        compiler_params=pltpu.CompilerParams(vmem_limit_bytes=16 * MIB),
        cost_estimate=pl.CostEstimate(flops=1, bytes_accessed=1, transcendentals=0),
        name="pack_small",
    )(norm_sums, qkv_sums, mid_sums, up_sums, down_sums)


def two_heads(x, value):
    return jnp.concatenate([x * lane_mask(0, value), x * lane_mask(1, value)], axis=0)


def forward_kernel(
    len_ref, tok_ref, wq_ref, wk_ref, wv_ref, vec_ref, bias_ref, kend_ref,
    scaled_ref, q_ref, k_ref, v_ref, mixed_ref, lse_ref, n1,
):
    g = pl.program_id(0)
    i = pl.program_id(1)
    slots = tok_ref.shape[1]
    go = len_ref[0] > 0

    @pl.when(g == 0)
    def _():
        scaled, _inverse = norm_parts(tok_ref[0].astype(F32))
        scaled_ref[0] = scaled.astype(BF)
        n1[i] = (scaled * vec_ref[0:1, :] + vec_ref[1:2, :]).astype(BF)

    @pl.when(go)
    def _():
        q_ref[0] = (mm(n1[i], wq_ref[...]) + bias_ref[2:3, :]).astype(BF)

    @pl.when(go)
    def _():
        k_ref[0] = mm(n1[i], wk_ref[...]).astype(BF)

    @pl.when(go)
    def _():
        v_ref[0] = (mm(n1[i], wv_ref[...]) + bias_ref[3:4, :]).astype(BF)

    lane = lax.broadcasted_iota(jnp.int32, (1, 128), 1)
    column = lax.broadcasted_iota(jnp.int32, (slots, slots), 1)
    allowed = column < kend_ref[0]
    ones = jnp.ones((slots, 128), BF)

    def scores_of(pair):
        cols = slice(pair * 128, (pair + 1) * 128)
        return mm_nt(two_heads(q_ref[0, :, cols], HEAD ** -0.5), k_ref[0, :, cols])

    def exponents_of(scores):
        parts, peaks = [], []
        for half in range(2):
            own = jnp.where(allowed, scores[half * slots : (half + 1) * slots], MASKED)
            peak = jnp.max(own, axis=-1, keepdims=True)
            parts.append(jnp.exp(own - peak).astype(BF))
            peaks.append(peak)
        return jnp.concatenate(parts, axis=0), peaks

    def finish(pair, exponents, peaks, lse_lanes):
        cols = slice(pair * 128, (pair + 1) * 128)
        both = mm(exponents, jnp.concatenate([v_ref[0, :, cols], ones], axis=1))
        first, second = both[:slots], both[slots:]
        total = jnp.where(lane < HEAD, first[:, 128:], second[:, 128:])
        values = jnp.where(lane < HEAD, first[:, :128], second[:, :128])
        mixed_ref[0, :, cols] = (values * (1.0 / total)).astype(BF)
        for half, part in ((0, first), (1, second)):
            lse = peaks[half] + jnp.log(part[:, 128:])
            lse_lanes = jnp.where(lane == 2 * pair + half, lse, lse_lanes)
        return lse_lanes

    lse_lanes = jnp.zeros((slots, 128), F32)
    tables = [scores_of(pair) for pair in range(PAIRS)]
    for pair in range(PAIRS):
        exponents, peaks = exponents_of(tables[pair])
        lse_lanes = finish(pair, exponents, peaks, lse_lanes)
    lse_ref[0] = lse_lanes.T[:8, :]


def attention_forward(lengths, tokens, w_qkv, vec, kend):
    items, slots, _ = tokens.shape
    early = lambda g, i, *_: (jnp.where(g == 0, i, items - 1), 0, 0)
    cols = lambda g, i, *_: (i, 0, g)
    weight = pl.BlockSpec((D, GROUP), lambda g, i, *_: (0, g))
    return pl.pallas_call(
        forward_kernel,
        grid_spec=pltpu.PrefetchScalarGridSpec(
            num_scalar_prefetch=1,
            grid=(GROUPS, items),
            in_specs=[
                pl.BlockSpec((1, slots, D), early),
                weight,
                pl.BlockSpec((D, GROUP), lambda g, i, *_: (0, GROUPS + g)),
                pl.BlockSpec((D, GROUP), lambda g, i, *_: (0, 2 * GROUPS + g)),
                pl.BlockSpec((VEC_ROWS, D), lambda g, i, *_: (0, 0)),
                pl.BlockSpec((VEC_ROWS, GROUP), lambda g, i, *_: (0, g)),
                pl.BlockSpec((1, slots, 1), lambda g, i, *_: (i, 0, 0)),
            ],
            out_specs=[pl.BlockSpec((1, slots, D), early)]
            + [pl.BlockSpec((1, slots, GROUP), cols)] * 4
            + [pl.BlockSpec((1, 8, slots), lambda g, i, *_: (i, g, 0))],
            scratch_shapes=[pltpu.VMEM((items, slots, D), BF)],
        ),
        out_shape=[jax.ShapeDtypeStruct((items, slots, D), BF)] * 5
        + [jax.ShapeDtypeStruct((items, 8 * GROUPS, slots), F32)],
        compiler_params=pltpu.CompilerParams(vmem_limit_bytes=48 * MIB),
        cost_estimate=pl.CostEstimate(
            flops=2 * items * slots * D * 3 * D + 16 * items * HEADS * slots * slots * HEAD,
            bytes_accessed=20 * MIB,
            transcendentals=items * HEADS * slots * slots,
        ),
        name="attention_forward",
    )(lengths, tokens, w_qkv, w_qkv, w_qkv, vec, vec, kend)


GELU_SCALE = 0.7978845608028654
GELU_CUBE = 0.044715
STEPS = 4
FIRST = 4
PARTS = 3


def row_valid(len_ref, start, rows, slots, items):
    index = lax.broadcasted_iota(jnp.int32, (rows, 1), 0) + start
    valid = index < len_ref[0]
    for item in range(1, items):
        valid = valid | ((index >= item * slots) & (index < item * slots + len_ref[item]))
    return jnp.where(valid, 1.0, 0.0).astype(F32)


def mlp_kernel(stacked, items, slots):
    tile = items * slots // PARTS

    def kernel(
        len_ref, mixed_ref, tok_ref, cot_ref, wout_ref, vec_ref, up_ref, down_ref,
        middle_ref, act, dn2_ref, gbd_ref, gbu_ref, *rest,
    ):
        first_out, *second = rest[:-7]
        n2, dlow, dpre, pre_all, gu, gd, sems = rest[-7:]
        b = pl.program_id(0)
        slot = lax.rem(b, 2)
        go = len_ref[0] > 0

        def send(step, act_on):
            where = lax.rem(step, 2)
            if stacked:
                per = gu.shape[2]
                devices = gd.shape[1]

                at = pl.ds(pl.multiple_of(per * step, 8), per)
                act_on(
                    pltpu.make_async_copy(
                        gu.at[where], first_out.at[:, at, :], sems.at[0, where]
                    )
                )
                down_to = first_out.at[pl.ds(devices * step, devices), FIRST * per : (FIRST + 4) * per, :]
            else:
                at = pl.ds(pl.multiple_of(D * step, D), D)
                act_on(
                    pltpu.make_async_copy(gu.at[where], first_out.at[:, at], sems.at[0, where])
                )
                down_to = second[0].at[at, :]
            act_on(pltpu.make_async_copy(gd.at[where], down_to, sems.at[1, where]))

        @pl.when(b == 0)
        def _():
            dn2_ref[...] = jnp.zeros_like(dn2_ref)
            sums = jnp.zeros((1, D), F32)
            for part in range(PARTS):
                at = slice(part * tile, (part + 1) * tile)
                middle = (
                    tok_ref[at, :].astype(F32)
                    + mm(mixed_ref[at, :], wout_ref[...].reshape(D, D))
                ) + vec_ref[4:5, :]
                middle_ref[at, :] = middle
                scaled, _inverse = norm_parts(middle)
                n2[at, :] = (scaled * vec_ref[5:6, :] + vec_ref[6:7, :]).astype(BF)
                valid = row_valid(len_ref, part * tile, tile, slots, items)
                lower = cot_ref[at, :].astype(F32) * valid
                dlow[at, :] = lower.astype(BF)
                sums = sums + jnp.sum(lower, axis=0, keepdims=True)
            gbd_ref[...] = jnp.broadcast_to(sums, gbd_ref.shape)

        gbu_ref[...] = jnp.zeros_like(gbu_ref)
        bias = vec_ref[pl.ds(8 + b, 1), :]
        for part in range(PARTS):
            at = slice(part * tile, (part + 1) * tile)

            @pl.when(go)
            def _():
                pre_all[...] = mm(n2[at, :], up_ref[...].reshape(D, D)) + bias

            @pl.when(go)
            def _():
                pre = pre_all[...]
                square = pre * pre
                half_t = 0.5 * jnp.tanh(GELU_SCALE * pre * (1.0 + GELU_CUBE * square))
                cdf = 0.5 + half_t
                act[at, :] = (pre * cdf).astype(BF)
                slope = cdf + pre * (0.5 - 2.0 * half_t * half_t) * (
                    GELU_SCALE + (3.0 * GELU_CUBE * GELU_SCALE) * square
                )
                d_pre = (mm_nt(dlow[at, :], down_ref[...].reshape(D, D)) * slope).astype(BF)
                dpre[at, :] = d_pre
                gbu_ref[0:1, :] += jnp.sum(d_pre.astype(F32), axis=0, keepdims=True)

            @pl.when(go)
            def _():
                dn2_ref[at, :] += mm_nt(dpre[at, :], up_ref[...].reshape(D, D))

        @pl.when(b >= 2)
        def _():
            send(b - 2, lambda copy: copy.wait())

        @pl.when(go)
        def _():
            gu[slot] = mm_tn(n2[...], dpre[...]).reshape(gu.shape[1:]).astype(BF)

        @pl.when(go)
        def _():
            gd[slot] = mm_tn(act[...], dlow[...]).reshape(gd.shape[1:]).astype(BF)

        send(b, lambda copy: copy.start())

        @pl.when(b == STEPS - 1)
        def _():
            send(b - 1, lambda copy: copy.wait())
            send(b, lambda copy: copy.wait())

    return kernel


def feed_forward(lengths, mixed, tokens, cotangent, w_out, vec, up, down, stacked, items, slots):
    row_count = items * slots
    once = pl.Buffered(1)
    fixed = lambda b, *_: (0, 0)
    if stacked:
        devices, stack, _ = up.shape
        per = stack // 9
        out_spec = pl.BlockSpec((devices, per, D), lambda b, *_: (0, 8, 0), pipeline_mode=once)
        up_spec = pl.BlockSpec((devices, per, D), lambda b, *_: (0, b, 0))
        down_spec = pl.BlockSpec((devices // 4, 4 * per, D), lambda b, *_: (b, 1, 0))
        grad_shapes = [
            jax.ShapeDtypeStruct((devices, (FIRST + 4) * per, D), BF),
        ]
        gu_shape, gd_shape = (devices, per, D), (devices // 4, 4 * per, D)
    else:
        out_spec = pl.BlockSpec((D, D), fixed, pipeline_mode=once)
        up_spec = pl.BlockSpec((D, D), lambda b, *_: (0, b))
        down_spec = pl.BlockSpec((D, D), lambda b, *_: (b, 0))
        grad_shapes = [
            jax.ShapeDtypeStruct((D, STEPS * D), BF),
            jax.ShapeDtypeStruct((STEPS * D, D), BF),
        ]
        gu_shape = gd_shape = (D, D)
    whole = pl.BlockSpec((row_count, D), fixed, pipeline_mode=once)
    return pl.pallas_call(
        mlp_kernel(stacked, items, slots),
        grid_spec=pltpu.PrefetchScalarGridSpec(
            num_scalar_prefetch=1,
            grid=(STEPS,),
            in_specs=[
                whole, whole, whole,
                out_spec,
                pl.BlockSpec((VEC_ROWS, D), fixed),
                up_spec,
                down_spec,
            ],
            out_specs=[
                whole,
                pl.BlockSpec((row_count, D), lambda b, *_: (0, b)),
                whole,
                pl.BlockSpec((8, D), fixed),
                pl.BlockSpec((8, D), lambda b, *_: (0, b)),
            ]
            + [pl.BlockSpec(memory_space=pl.ANY)] * len(grad_shapes),
            scratch_shapes=[pltpu.VMEM((row_count, D), BF)] * 3
            + [
                pltpu.VMEM((row_count // PARTS, D), F32),
                pltpu.VMEM((2,) + gu_shape, BF),
                pltpu.VMEM((2,) + gd_shape, BF),
                pltpu.SemaphoreType.DMA((2, 2)),
            ],
        ),
        out_shape=[
            jax.ShapeDtypeStruct((row_count, D), F32),
            jax.ShapeDtypeStruct((row_count, STEPS * D), BF),
            jax.ShapeDtypeStruct((row_count, D), F32),
            jax.ShapeDtypeStruct((8, D), F32),
            jax.ShapeDtypeStruct((8, STEPS * D), F32),
        ]
        + grad_shapes,
        compiler_params=pltpu.CompilerParams(vmem_limit_bytes=60 * MIB),
        cost_estimate=pl.CostEstimate(
            flops=2 * row_count * D * D * 25,
            bytes_accessed=36 * MIB,
            transcendentals=row_count * 4 * D,
        ),
        name="feed_forward",
    )(lengths, mixed, tokens, cotangent, w_out, vec, up, down)


def output_kernel(items, slots):
    tile = items * slots // PARTS

    def kernel(len_ref, middle_ref, act_ref, down_ref, vec_ref, out_ref):
        valid = row_valid(len_ref, pl.program_id(0) * tile, tile, slots, items)
        down = down_ref[...].reshape(STEPS * D, D)
        whole = middle_ref[...] + (mm(act_ref[...], down) + vec_ref[7:8, :])
        out_ref[...] = (whole * valid).astype(BF)

    return kernel


def feed_forward_output(lengths, middle, active, down, vec, stacked, items, slots, after):
    tile = items * slots // PARTS
    vec, _after = lax.optimization_barrier((vec, after))
    once = pl.Buffered(1)
    if stacked:
        devices, stack, _ = down.shape
        spec = pl.BlockSpec(
            (devices, 4 * stack // 9, D), lambda p, *_: (0, 1, 0), pipeline_mode=once
        )
    else:
        spec = pl.BlockSpec((STEPS * D, D), lambda p, *_: (0, 0), pipeline_mode=once)
    block = lambda width: pl.BlockSpec((tile, width), lambda p, *_: (p, 0))
    return pl.pallas_call(
        output_kernel(items, slots),
        grid_spec=pltpu.PrefetchScalarGridSpec(
            num_scalar_prefetch=1,
            grid=(PARTS,),
            in_specs=[
                block(D), block(STEPS * D), spec,
                pl.BlockSpec((VEC_ROWS, D), lambda p, *_: (0, 0)),
            ],
            out_specs=block(D),
        ),
        out_shape=jax.ShapeDtypeStruct((items * slots, D), BF),
        compiler_params=pltpu.CompilerParams(vmem_limit_bytes=48 * MIB),
        cost_estimate=pl.CostEstimate(flops=1, bytes_accessed=1, transcendentals=0),
        name="feed_forward_output",
    )(lengths, middle, active, down, vec)


def middle_kernel(slots):
    def kernel(
        len_ref, dn2_ref, middle_ref, cot_ref, mixed_ref, wout_ref, vec_ref,
        dmid_ref, dmix_ref, delta_ref, gout_ref, sums_ref, acc, branch,
    ):
        i = pl.program_id(0)
        last = pl.num_programs(0) - 1
        go = len_ref[0] > 0

        @pl.when(i == 0)
        def _():
            sums_ref[...] = jnp.zeros_like(sums_ref)
            acc[...] = jnp.zeros_like(acc)

        scaled, inverse = norm_parts(middle_ref[0])
        d_n2 = dn2_ref[0]
        valid = jnp.where(
            lax.broadcasted_iota(jnp.int32, (slots, 1), 0) < len_ref[i], 1.0, 0.0
        ).astype(F32)
        d_middle = cot_ref[0].astype(F32) * valid + norm_back(
            d_n2, scaled, inverse, vec_ref[5:6, :]
        )
        dmid_ref[0] = d_middle
        low = d_middle.astype(BF)
        branch[...] = low
        sums_ref[...] += jnp.concatenate(
            [
                jnp.sum(d_n2 * scaled, axis=0, keepdims=True),
                jnp.sum(d_n2, axis=0, keepdims=True),
                jnp.sum(low.astype(F32), axis=0, keepdims=True),
                jnp.zeros((5, D), F32),
            ],
            axis=0,
        )

        @pl.when(go)
        def _():
            dmix_ref[0] = mm_nt(branch[...], wout_ref[...].reshape(D, D)).astype(BF)

        @pl.when(go)
        def _():
            acc[...] += mm_tn(mixed_ref[0], branch[...])

        @pl.when(go)
        def _():
            product = dmix_ref[0].astype(F32) * mixed_ref[0].astype(F32)
            row = lax.broadcasted_iota(jnp.int32, (8 * GROUPS, D), 0)
            lane = lax.broadcasted_iota(jnp.int32, (8 * GROUPS, D), 1)
            pick = jnp.where(
                (lane // HEAD == 4 * (row // 8) + row % 8) & (row % 8 < 4), 1.0, 0.0
            ).astype(BF)
            high = product.astype(BF)
            rest = (product - high.astype(F32)).astype(BF)
            delta_ref[0] = mm_nt(pick, high) + mm_nt(pick, rest)

        @pl.when(i == last)
        def _():
            gout_ref[...] = acc[...].astype(BF)

    return kernel


def middle_backward(lengths, d_n2, middle, cotangent, mixed, w_out, vec):
    items, slots, _ = mixed.shape
    rows = lambda i, *_: (i, 0, 0)
    fixed = lambda i, *_: (0, 0)
    block = pl.BlockSpec((1, slots, D), rows)
    return pl.pallas_call(
        middle_kernel(slots),
        grid_spec=pltpu.PrefetchScalarGridSpec(
            num_scalar_prefetch=1,
            grid=(items,),
            in_specs=[
                block, block, block, block,
                pl.BlockSpec((D, D), fixed)
                if w_out.ndim == 2
                else pl.BlockSpec(
                    (w_out.shape[0], w_out.shape[1] // 9, D), lambda i, *_: (0, 8, 0)
                ),
                pl.BlockSpec((VEC_ROWS, D), fixed),
            ],
            out_specs=[
                block, block,
                pl.BlockSpec((1, 8 * GROUPS, slots), rows),
                pl.BlockSpec((D, D), fixed),
                pl.BlockSpec((8, D), fixed),
            ],
            scratch_shapes=[pltpu.VMEM((D, D), F32), pltpu.VMEM((slots, D), BF)],
        ),
        out_shape=[
            jax.ShapeDtypeStruct((items, slots, D), F32),
            jax.ShapeDtypeStruct((items, slots, D), BF),
            jax.ShapeDtypeStruct((items, 8 * GROUPS, slots), F32),
            jax.ShapeDtypeStruct((D, D), BF),
            jax.ShapeDtypeStruct((8, D), F32),
        ],
        compiler_params=pltpu.CompilerParams(vmem_limit_bytes=56 * MIB),
        cost_estimate=pl.CostEstimate(flops=1, bytes_accessed=1, transcendentals=0),
        name="middle_backward",
    )(lengths, d_n2, middle, cotangent, mixed, w_out, vec)


def backward_kernel(
    len_ref, q_ref, k_ref, v_ref, dmix_ref, lse_ref, delta_ref, kend_ref, scaled_ref,
    wq_ref, wk_ref, wv_ref, table_ref,
    dqkv_ref, gw_ref, gbias_ref, norm_ref, acc,
):
    g = pl.program_id(0)
    i = pl.program_id(1)
    last_item = pl.num_programs(1) - 1
    slots = q_ref.shape[1]
    go = len_ref[0] > 0
    key = lax.broadcasted_iota(jnp.int32, (slots, slots), 0)
    allowed = key < kend_ref[0]
    fronts = []
    for pair in range(PAIRS):
        cols = slice(pair * 128, (pair + 1) * 128)
        queries = two_heads(q_ref[0, :, cols], HEAD ** -0.5)
        upstream = two_heads(dmix_ref[0, :, cols], 1.0)
        fronts.append(
            (
                queries,
                upstream,
                mm_nt(k_ref[0, :, cols], queries),
                mm_nt(v_ref[0, :, cols], upstream),
            )
        )
    for pair in range(PAIRS):
        queries, upstream, scores, d_probs = fronts[pair]
        dv = dk = None
        turned = []
        flipped = k_ref[0, :, pair * 128 : (pair + 1) * 128].T
        for half in range(2):
            head = 2 * pair + half
            at = slice(half * slots, (half + 1) * slots)
            probs = jnp.exp(
                jnp.where(allowed, scores[:, at], MASKED) - lse_ref[0, head : head + 1, :]
            )
            d_scores = (probs * (d_probs[:, at] - delta_ref[0, head : head + 1, :])).astype(BF)
            dv_half = mm(probs.astype(BF), upstream[at])
            dk_half = mm(d_scores, queries[at])
            dv = dv_half if dv is None else dv + dv_half
            dk = dk_half if dk is None else dk + dk_half
            turned.append(mm(flipped, d_scores))
        row = lax.broadcasted_iota(jnp.int32, (128, 1), 0)
        dq = jnp.where(row < HEAD, turned[0], turned[1]).T * HEAD ** -0.5
        for which, part in ((0, dq), (1, dk), (2, dv)):
            start = which * GROUP + pair * 128
            dqkv_ref[0, :, start : start + 128] = part.astype(BF)

    @pl.when(go)
    def _():
        bias = jnp.sum(dqkv_ref[0].astype(F32), axis=0, keepdims=True)
        before = jnp.where(i == 0, 0.0, gbias_ref[...])
        gbias_ref[...] = before + bias

    @pl.when(i == 0)
    def _():
        acc[...] = mm_tn(scaled_ref[0], dqkv_ref[0])

    @pl.when(i > 0)
    def _():
        acc[...] += mm_tn(scaled_ref[0], dqkv_ref[0])

    @pl.when(i == last_item)
    def _():
        gain = table_ref[:, 0:1].astype(F32)
        shift = table_ref[:, 1:2].astype(F32)
        lane = lax.broadcasted_iota(jnp.int32, (1, SMALL), 1)
        gains = jnp.zeros((D, 1), F32)
        shifts = jnp.zeros((D, 1), F32)
        for which, ref in ((0, wq_ref), (1, wk_ref), (2, wv_ref)):
            cols = slice(which * GROUP, (which + 1) * GROUP)
            total = acc[:, cols]
            sums = gbias_ref[0:1, cols]
            weight = ref[...].astype(F32)
            gw_ref[:, cols] = (gain * total + shift * sums).astype(BF)
            gains = gains + jnp.sum(weight * total, axis=-1, keepdims=True)
            shifts = shifts + jnp.sum(weight * sums, axis=-1, keepdims=True)
        new = jnp.where(lane == 0, gains, jnp.where(lane == 1, shifts, 0.0))

        @pl.when(g == 0)
        def _():
            norm_ref[...] = new

        @pl.when(g > 0)
        def _():
            norm_ref[...] += new


def attention_backward(lengths, q, k, v, d_mixed, lse, delta, kend_row, scaled, w_qkv):
    items, slots, _ = q.shape
    rows = lambda g, i, *_: (i, 0, 0)
    cols = lambda g, i, *_: (i, 0, g)
    block = pl.BlockSpec((1, slots, GROUP), cols)
    table = pl.BlockSpec((1, 8, slots), lambda g, i, *_: (i, g, 0))
    weight = pl.BlockSpec((D, GROUP), lambda g, i, *_: (0, g))
    return pl.pallas_call(
        backward_kernel,
        grid_spec=pltpu.PrefetchScalarGridSpec(
            num_scalar_prefetch=1,
            grid=(GROUPS, items),
            in_specs=[
                block, block, block, block, table, table,
                pl.BlockSpec((1, 1, slots), rows),
                pl.BlockSpec((1, slots, D), rows),
                weight,
                pl.BlockSpec((D, GROUP), lambda g, i, *_: (0, GROUPS + g)),
                pl.BlockSpec((D, GROUP), lambda g, i, *_: (0, 2 * GROUPS + g)),
                pl.BlockSpec((D, SMALL), lambda g, i, *_: (0, 3 * D // SMALL)),
            ],
            out_specs=[
                pl.BlockSpec((1, slots, D), cols),
                pl.BlockSpec((D, D), lambda g, i, *_: (0, g)),
                pl.BlockSpec((8, D), lambda g, i, *_: (0, g)),
                pl.BlockSpec((D, SMALL), lambda g, i, *_: (0, 0)),
            ],
            scratch_shapes=[pltpu.VMEM((D, D), F32)],
        ),
        out_shape=[
            jax.ShapeDtypeStruct((items, slots, 3 * D), BF),
            jax.ShapeDtypeStruct((D, 3 * D), BF),
            jax.ShapeDtypeStruct((8, 3 * D), F32),
            jax.ShapeDtypeStruct((D, SMALL), F32),
        ],
        compiler_params=pltpu.CompilerParams(vmem_limit_bytes=56 * MIB),
        cost_estimate=pl.CostEstimate(flops=1, bytes_accessed=1, transcendentals=0),
        name="attention_backward",
    )(lengths, q, k, v, d_mixed, lse, delta, kend_row, scaled, w_qkv, w_qkv, w_qkv, w_qkv)


def input_kernel(dqkv_ref, w_ref, tok_ref, dmid_ref, vec_ref, grad_ref):
    total = None
    for g in range(GROUPS):
        for which in range(3):
            weight = w_ref[:, which * D + g * GROUP : which * D + (g + 1) * GROUP]
            start = g * D + which * GROUP
            part = mm_nt(dqkv_ref[0, :, start : start + GROUP], weight)
            total = part if total is None else total + part
    scaled, inverse = norm_parts(tok_ref[0].astype(F32))
    grad_ref[0] = dmid_ref[0] + norm_back(total, scaled, inverse, vec_ref[0:1, :])


def input_backward(d_qkv, w_qkv, tokens, d_middle, vec, after):
    items, slots, _ = tokens.shape
    vec, _after = lax.optimization_barrier((vec, after))
    rows = lambda i: (i, 0, 0)
    fixed = lambda i: (0, 0)
    block = pl.BlockSpec((1, slots, D), rows)
    return pl.pallas_call(
        input_kernel,
        grid=(items,),
        in_specs=[
            pl.BlockSpec((1, slots, 3 * D), rows),
            pl.BlockSpec((D, 3 * D), fixed),
            block, block,
            pl.BlockSpec((VEC_ROWS, D), fixed),
        ],
        out_specs=block,
        out_shape=jax.ShapeDtypeStruct((items, slots, D), F32),
        compiler_params=pltpu.CompilerParams(vmem_limit_bytes=48 * MIB),
        cost_estimate=pl.CostEstimate(flops=1, bytes_accessed=1, transcendentals=0),
        name="input_backward",
    )(d_qkv, w_qkv, tokens, d_middle, vec)


def own_kernel(keep_ref, got_ref, qkv_ref, out_ref, small_ref):
    total = keep_ref[...] + got_ref[...].astype(F32)
    for which in range(3):
        for g in range(GROUPS):
            start = g * D + which * GROUP
            qkv_ref[:, which * D + g * GROUP : which * D + (g + 1) * GROUP] = total[
                :, start : start + GROUP
            ]
    small_ref[...] = total[:, 3 * D : 3 * D + SMALL]
    start = 3 * D + SMALL
    out_ref[...] = total[:, start : start + D]


def own_grads(keep, got):
    rows = keep.shape[0]
    return pl.pallas_call(
        own_kernel,
        out_shape=[
            jax.ShapeDtypeStruct((rows, 3 * D), F32),
            jax.ShapeDtypeStruct((rows, D), F32),
            jax.ShapeDtypeStruct((rows, SMALL), F32),
        ],
        compiler_params=pltpu.CompilerParams(vmem_limit_bytes=16 * MIB),
        name="own_grads",
    )(keep, got)


def swap(x, axis, bit, size):
    return lax.ppermute(x, axis, [(i, i ^ (1 << bit)) for i in range(size)])


def own_bit(axis, bit):
    return (lax.axis_index(axis) >> bit) & 1


def doubled(x, axis, bit, size, at):
    other = jnp.expand_dims(swap(x, axis, bit, size), at)
    mine = jnp.expand_dims(x, at)
    return jnp.where(
        own_bit(axis, bit) == 0,
        jnp.concatenate([mine, other], at),
        jnp.concatenate([other, mine], at),
    )


def gather_rows(x, cut, sizes):
    rows = x.shape[0]
    wide, narrow = sizes
    if sizes != (8, 4):
        return lax.all_gather(x, AXES, axis=0, tiled=True)

    def ordered(mine, other, axis, bit, at):
        mine, other = jnp.expand_dims(mine, at), jnp.expand_dims(other, at)
        return jnp.where(
            own_bit(axis, bit) == 0,
            jnp.concatenate([mine, other], at),
            jnp.concatenate([other, mine], at),
        )

    away = lambda mask: lax.ppermute(x, "wide", [(i, i ^ mask) for i in range(wide)])
    near, far, both = away(2), away(4), away(6)
    x = ordered(ordered(x, near, "wide", 1, 0), ordered(far, both, "wide", 1, 0), "wide", 2, 0)
    a, b = x[..., :cut], x[..., cut:]
    a = doubled(a, "wide", 0, wide, 2)
    b = doubled(b, "narrow", 1, narrow, 2)
    a = doubled(a, "narrow", 1, narrow, 3)
    b = doubled(b, "wide", 0, wide, 2)
    x = jnp.concatenate([a, b], axis=-1)
    x = doubled(x, "narrow", 0, narrow, 4)
    return x.reshape(wide * narrow * rows, -1)


def pick_half(x, axis, bit, at):
    me = own_bit(axis, bit)
    send = lax.dynamic_index_in_dim(x, 1 - me, at, keepdims=False).astype(BF)
    return send, lax.dynamic_index_in_dim(x, me, at, keepdims=False)


def scatter_rows(a, b, sizes, fillers):
    wide, narrow = sizes
    if sizes != (8, 4):
        scatter = lambda x: lax.psum_scatter(
            x.astype(F32), AXES, scatter_dimension=0, tiled=True
        )
        done = [filler(()) for filler in fillers]
        x = jnp.concatenate([scatter(a), scatter(b)], axis=1)
        return x, jnp.zeros(x.shape, BF), done

    def step(a, b, a_cut, b_cut, beside=None):
        (a_axis, a_bit, a_size, a_at), (b_axis, b_bit, b_size, b_at) = a_cut, b_cut
        a_send, a_keep = pick_half(a, a_axis, a_bit, a_at)
        b_send, b_keep = pick_half(b, b_axis, b_bit, b_at)
        a_send, b_send = lax.optimization_barrier((a_send, b_send))
        a_got = swap(a_send, a_axis, a_bit, a_size)
        b_got = swap(b_send, b_axis, b_bit, b_size)
        done = None
        if beside is not None:
            done = beside((a_send, b_send))
            a_got, b_got, done = lax.optimization_barrier((a_got, b_got, done))
        else:
            a_got, b_got = lax.optimization_barrier((a_got, b_got))
        add = lambda keep, got: keep.astype(F32) + got.astype(F32)
        return add(a_keep, a_got), add(b_keep, b_got), done

    rows = a.shape[0] // (wide * narrow)
    split = (2, 2, 2, 2, 2, rows, -1)
    core, x_cut = ("narrow", 0, narrow, 4), ("narrow", 1, narrow)
    y_cut = ("wide", 0, wide)
    a, b, _ = step(a.reshape(split), b.reshape(split), core, core)
    a, b, first = step(a, b, x_cut + (3,), y_cut + (2,), fillers[0])
    a, b, second = step(a, b, y_cut + (2,), x_cut + (2,), fillers[1])
    x = jnp.concatenate([a, b], axis=-1)
    send, keep = pick_half(x, "wide", 1, 1)
    x = keep.astype(F32) + swap(send, "wide", 1, wide).astype(F32)
    send, keep = pick_half(x, "wide", 2, 0)
    return keep, swap(send, "wide", 2, wide), [first, second]


def body(sizes):
    def run(
        tokens, lengths, blocks, ln1_gain, ln1_bias, qkv_weight, qv_bias, out_weight, out_bias,
        ln2_gain, ln2_bias, up_weight, up_bias, down_weight, down_bias, cotangent,
    ):
        items, slots, _ = tokens.shape
        row_count = items * slots
        rows = qkv_weight.shape[0]
        devices = sizes[0] * sizes[1]
        stacked = rows % 8 == 0

        vectors = (
            ln1_gain, ln1_bias, qv_bias, out_bias, ln2_gain, ln2_bias, up_bias, down_bias,
        )
        first, *rest = pack_parameters(
            vectors, qkv_weight, out_weight, up_weight, down_weight, stacked
        )
        if stacked:
            whole = lax.all_gather(rest[0], AXES, axis=0, tiled=True)
            w_out = up = down = whole.reshape(devices, 9 * rows, D)
        else:
            gathered = lambda x: lax.all_gather(x, AXES, axis=0, tiled=True)
            w_out, up, down = gathered(out_weight), gathered(up_weight), gathered(down_weight)
        w_qkv = gather_rows(first, 5 * GROUP, sizes)
        vec = unpack_small(w_qkv, rows)

        ends = jnp.sum(
            (blocks[:, None, :] <= blocks[:, :, None]).astype(jnp.int32), axis=-1
        )
        kend = jnp.minimum(ends, lengths[:, None])

        scaled, q, k, v, mixed, lse = attention_forward(
            lengths, tokens, w_qkv, vec, kend.reshape(items, slots, 1)
        )
        flat = lambda t: t.reshape(row_count, D)
        cube = lambda t: t.reshape(items, slots, D)
        middle, active, d_n2, gb_down, gb_up, grads, *more = feed_forward(
            lengths, flat(mixed), flat(tokens), flat(cotangent), w_out, vec, up, down,
            stacked, items, slots,
        )
        scatter = lambda x: lax.psum_scatter(x, AXES, scatter_dimension=0, tiled=True)
        if stacked:
            own = scatter(grads.reshape(devices * (FIRST + 4) * rows, D))
        else:
            grad_up = scatter(grads.astype(F32))
            grad_down = scatter(more[0].astype(F32))
        d_middle, d_mixed, delta, g_out, mid_sums = middle_backward(
            lengths, cube(d_n2), cube(middle), cotangent, mixed, w_out, vec
        )
        d_qkv, g_qkv, qkv_sums, norm_sums = attention_backward(
            lengths, q, k, v, d_mixed, lse, delta, kend.reshape(items, 1, slots), scaled, w_qkv,
        )
        small_grads = pack_small(norm_sums, qkv_sums, mid_sums, gb_up, gb_down, rows)
        packed = jnp.concatenate([g_qkv, small_grads, g_out], axis=1)
        cut = 2 * D + SMALL
        late, early = packed[:, :cut], packed[:, cut:]

        def input_part(after):
            return input_backward(d_qkv, w_qkv, tokens, d_middle, vec, after)

        def output_part(after):
            return feed_forward_output(
                lengths, middle, active, down, vec, stacked, items, slots, after
            )

        keep, got, (input_grad, output) = scatter_rows(
            late, early, sizes, (input_part, output_part)
        )
        if stacked:
            own_qkv, own_out, own_small = own_grads(keep, got)
            own = own.astype(F32)
            grad_up = jnp.concatenate(
                [own[b * rows : (b + 1) * rows] for b in range(FIRST)], axis=1
            )
            grad_down = own[FIRST * rows :]
        else:
            full = keep
            own_small = full[:, 3 * D : 3 * D + SMALL]
            own_out = full[:, 3 * D + SMALL :]
            own_qkv = jnp.concatenate(
                [
                    full[:, g * D + which * GROUP : g * D + (which + 1) * GROUP]
                    for which in range(3)
                    for g in range(GROUPS)
                ],
                axis=1,
            )
        return (
            cube(output),
            input_grad,
            own_small[:, 0],
            own_small[:, 1],
            own_qkv,
            own_small[:, 2:4].T.reshape(-1),
            own_out,
            own_small[:, 4],
            own_small[:, 5],
            own_small[:, 6],
            grad_up,
            own_small[:, 7:11].T.reshape(-1),
            grad_down,
            own_small[:, 11],
        )

    return run


def solution(mesh):
    sizes = (mesh.shape["wide"], mesh.shape["narrow"])
    one = P(AXES)
    two = P(AXES, None)
    three = P(AXES, None, None)
    return jax.shard_map(
        body(sizes),
        mesh=mesh,
        in_specs=(
            three, one, two, one, one, two, one, two, one, one, one, two, one, two, one, three,
        ),
        out_specs=(
            three, three, one, one, two, one, two, one, one, one, two, one, two, one,
        ),
        check_vma=False,
    )
```

```python
import functools

import jax
import jax.numpy as jnp
from jax import lax
from jax.experimental import pallas as pl
from jax.experimental.pallas import tpu as pltpu
from jax.sharding import PartitionSpec as P

D = 768
HEADS = 12
HEAD = 64
GROUP = 256
GROUPS = D // GROUP
PAIRS = GROUP // 128
EPS = 1e-05
MASKED = -1e30
AXES = ("wide", "narrow")
BF = jnp.bfloat16
F32 = jnp.float32
MIB = 1 << 20
VEC_ROWS = 16
SMALL = 128
BLOCKS = 5


def mm(a, b):
    return jnp.dot(a, b, preferred_element_type=F32)


def mm_nt(a, b):
    return lax.dot_general(a, b, (((1,), (1,)), ((), ())), preferred_element_type=F32)


def mm_tn(a, b):
    return lax.dot_general(a, b, (((0,), (0,)), ((), ())), preferred_element_type=F32)


def norm_parts(x):
    centred = x - jnp.mean(x, axis=-1, keepdims=True)
    inverse = lax.rsqrt(jnp.mean(centred * centred, axis=-1, keepdims=True) + EPS)
    return centred * inverse, inverse


def norm_back(d_normed, scaled, inverse, gain):
    h = d_normed * gain
    return inverse * (
        h
        - jnp.mean(h, axis=-1, keepdims=True)
        - scaled * jnp.mean(h * scaled, axis=-1, keepdims=True)
    )


def lane_mask(half, value):
    lane = lax.broadcasted_iota(jnp.int32, (1, 128), 1)
    return jnp.where((lane // HEAD) == half, value, 0.0).astype(BF)


COLUMNS = (("ln1_gain", 1), ("ln1_bias", 1), ("qv_bias", 2), ("out_bias", 1), ("ln2_gain", 1), ("ln2_bias", 1), ("up_bias", 4), ("down_bias", 1))


def store_halves(refs, value, me, cols):
    if len(refs) == 1:
        refs[0][:, cols] = value.astype(BF)
        return
    pairs, rows, _ = refs[0].shape
    value = value.reshape(pairs, 2, rows, value.shape[1])
    even, odd = value[:, 0], value[:, 1]
    refs[0][:, :, cols] = jnp.where(me == 0, odd, even).astype(BF)
    refs[1][:, :, cols] = jnp.where(me == 0, even, odd).astype(BF)


def split_shapes(fast, devices, columns):
    if not fast:
        return [jax.ShapeDtypeStruct((D, columns), BF)]
    return [jax.ShapeDtypeStruct((devices // 2, D // devices, columns), BF)] * 2


def whole_block(value):
    return pl.BlockSpec(value.shape, lambda *_: (0,) * len(value.shape))


def pack_kernel(stacked):
    def kernel(len_ref, blocks_ref, *refs):
        vectors, (qkv_ref, out_ref, up_ref, down_ref, row_ref, column_ref, first_ref) = (
            refs[:8], refs[8:15],
        )
        rows = qkv_ref.shape[0]
        for i in range(blocks_ref.shape[0]):
            blocks = blocks_ref[i : i + 1, :]
            last = jnp.zeros_like(blocks)
            for block in range(BLOCKS):
                count = jnp.sum((blocks <= block).astype(jnp.int32), axis=-1, keepdims=True)
                last = jnp.where(blocks == block, count, last)
            last = jnp.minimum(last, len_ref[i])
            row_ref[i] = last
            tall = jnp.broadcast_to(last.astype(F32), (SMALL, last.shape[1])).T
            column_ref[i] = tall[:, 0:1].astype(jnp.int32)
        lines = []
        for ref, (_name, count) in zip(vectors, COLUMNS):
            line = ref[...].astype(F32)
            lines += [line[:, j * rows : (j + 1) * rows] for j in range(count)]
        table = jnp.concatenate(lines + [jnp.zeros((SMALL - len(lines), rows), F32)], axis=0)
        first_ref[:, : 3 * D] = qkv_ref[...]
        first_ref[:, 3 * D : 4 * D] = out_ref[...]
        first_ref[:, 4 * D :] = table.T.astype(BF)
        if stacked:
            rest_ref = refs[15]
            for b in range(4):
                rest_ref[b * rows : (b + 1) * rows, :] = up_ref[:, b * D : (b + 1) * D]
            rest_ref[4 * rows :, :] = down_ref[...]

    return kernel


def pack_parameters(lengths, blocks, vectors, qkv, out, up, down, stacked):
    rows = qkv.shape[0]
    items, slots = blocks.shape
    shapes = [
        jax.ShapeDtypeStruct((items, 1, slots), jnp.int32),
        jax.ShapeDtypeStruct((items, slots, 1), jnp.int32),
        jax.ShapeDtypeStruct((rows, 4 * D + SMALL), BF),
    ]
    if stacked:
        shapes.append(jax.ShapeDtypeStruct((8 * rows, D), BF))
    values = [blocks] + [v.reshape(1, -1) for v in vectors] + [qkv, out, up, down]
    return pl.pallas_call(
        pack_kernel(stacked),
        grid_spec=pltpu.PrefetchScalarGridSpec(
            num_scalar_prefetch=1,
            grid=(1,),
            in_specs=[whole_block(v) for v in values],
            out_specs=[whole_block(v) for v in shapes],
        ),
        out_shape=shapes,
        compiler_params=pltpu.CompilerParams(vmem_limit_bytes=60 * MIB),
        name="pack_parameters",
    )(lengths, *values)


def from_table(lines, count, rows, start, pick_rows):
    lane = lax.broadcasted_iota(jnp.int32, (1, D), 1) + start
    first = start // count // 128 * 128
    place = lax.broadcasted_iota(jnp.int32, (pick_rows, D), 0) + first
    at = lax.broadcasted_iota(jnp.int32, (pick_rows, D), 1) + start
    pick = (place == rows * (at // (count * rows)) + at % rows).astype(F32).astype(BF)
    lines = mm(lines[:, first : first + pick_rows].astype(BF), pick)
    which = lane % (count * rows) // rows
    line = lines[0:1, :]
    for j in range(1, count):
        line = jnp.where(which == j, lines[j : j + 1, :], line)
    return line


def unpack_kernel(rows):
    def kernel(table_ref, vec_ref):
        lines = table_ref[...].astype(F32).T
        vec_ref[0:2, :] = lines[0:2, :]
        vec_ref[2:3, :] = from_table(lines[2:4, :], 2, rows, 0, D // 2)
        vec_ref[3:4, :] = from_table(lines[2:4, :], 2, rows, D, D // 2)
        vec_ref[4:7, :] = lines[4:7, :]
        vec_ref[7:8, :] = lines[11:12, :]
        for b in range(4):
            vec_ref[8 + b : 9 + b, :] = from_table(lines[7:11, :], 4, rows, b * D, 256)
        vec_ref[12:16, :] = jnp.zeros((4, D), F32)

    return kernel


def unpack_small(first, rows):
    return pl.pallas_call(
        unpack_kernel(rows),
        grid=(1,),
        in_specs=[pl.BlockSpec((D, SMALL), lambda i: (0, 4 * D // SMALL))],
        out_specs=pl.BlockSpec((VEC_ROWS, D), lambda i: (0, 0)),
        out_shape=jax.ShapeDtypeStruct((VEC_ROWS, D), F32),
        compiler_params=pltpu.CompilerParams(vmem_limit_bytes=16 * MIB),
        name="unpack_small",
    )(first)


def to_table(line, count, rows, start, pick_rows, column):
    row = lax.broadcasted_iota(jnp.int32, (SMALL, D), 0)
    at = lax.broadcasted_iota(jnp.int32, (SMALL, D), 1) + start
    spread = jnp.where(row - column == at % (count * rows) // rows, line, 0.0).astype(BF)
    place = lax.broadcasted_iota(jnp.int32, (pick_rows, D), 0) + start // count
    lane = lax.broadcasted_iota(jnp.int32, (pick_rows, D), 1) + start
    pick = (place == rows * (lane // (count * rows)) + lane % rows).astype(F32).astype(BF)
    return mm_nt(pick, spread)


def small_kernel(rows, norm_count, items):
    def kernel(len_ref, *refs):
        norms, refs = refs[:norm_count], refs[norm_count:]
        sums, refs = refs[:norm_count], refs[norm_count:]
        mid_ref, up_ref, down_ref, *outs = refs
        lines = jnp.concatenate([ref[0:1, :] for ref in sums], axis=1)
        row = lax.broadcasted_iota(jnp.int32, (SMALL, D), 0)
        plain = jnp.zeros((SMALL, D), F32)
        for at, line in (
            (4, mid_ref[2:3, :]), (5, mid_ref[0:1, :]), (6, mid_ref[1:2, :]),
            (11, down_ref[0:1, :]),
        ):
            plain = jnp.where(row == at, line, plain)
        halves = []
        for part, which in enumerate((0, 2)):
            line = jnp.concatenate(
                [
                    lines[:, g * D + which * GROUP : g * D + (which + 1) * GROUP]
                    for g in range(GROUPS)
                ],
                axis=1,
            )
            halves.append(to_table(line, 2, rows, part * D, D // 2, 2))
        quarters = [
            to_table(up_ref[0:1, b * D : (b + 1) * D], 4, rows, b * D, D // 4, 7)
            for b in range(4)
        ]
        total = plain.T + jnp.concatenate(halves, axis=0)
        for norm in norms:
            total = total + norm[...]
        total = total + jnp.concatenate(quarters, axis=0)
        store_halves(outs, total, len_ref[items], slice(None))

    return kernel


def pack_small(scalars, norm_sums, qkv_sums, mid_sums, up_sums, down_sums, rows, fast, items):
    values = (*norm_sums, *qkv_sums, mid_sums, up_sums, down_sums)
    shapes = split_shapes(fast, D // rows, SMALL)
    return pl.pallas_call(
        small_kernel(rows, len(norm_sums), items),
        grid_spec=pltpu.PrefetchScalarGridSpec(
            num_scalar_prefetch=1,
            grid=(1,),
            in_specs=[whole_block(v) for v in values],
            out_specs=[whole_block(v) for v in shapes],
        ),
        out_shape=shapes,
        compiler_params=pltpu.CompilerParams(vmem_limit_bytes=16 * MIB),
        cost_estimate=pl.CostEstimate(flops=1, bytes_accessed=1, transcendentals=0),
        name="pack_small",
    )(scalars, *values)


def two_heads(x, value):
    return jnp.concatenate([x * lane_mask(0, value), x * lane_mask(1, value)], axis=0)


def forward_kernel(
    len_ref, tok_ref, wq_ref, wk_ref, wv_ref, vec_ref, bias_ref, kend_ref,
    scaled_ref, q_ref, k_ref, v_ref, mixed_ref, lse_ref, n1,
):
    g = pl.program_id(0)
    i = pl.program_id(1)
    slots = tok_ref.shape[1]
    go = len_ref[0] > 0

    @pl.when(g == 0)
    def _():
        scaled, _inverse = norm_parts(tok_ref[0].astype(F32))
        scaled_ref[0] = scaled.astype(BF)
        n1[i] = (scaled * vec_ref[0:1, :] + vec_ref[1:2, :]).astype(BF)

    @pl.when(go)
    def _():
        q_ref[0] = (mm(n1[i], wq_ref[...]) + bias_ref[2:3, :]).astype(BF)

    @pl.when(go)
    def _():
        k_ref[0] = mm(n1[i], wk_ref[...]).astype(BF)

    @pl.when(go)
    def _():
        v_ref[0] = (mm(n1[i], wv_ref[...]) + bias_ref[3:4, :]).astype(BF)

    lane = lax.broadcasted_iota(jnp.int32, (1, 128), 1)
    column = lax.broadcasted_iota(jnp.int32, (slots, slots), 1)
    allowed = column < kend_ref[0]
    ones = jnp.ones((slots, 128), BF)

    def scores_of(pair):
        cols = slice(pair * 128, (pair + 1) * 128)
        return mm_nt(two_heads(q_ref[0, :, cols], HEAD ** -0.5), k_ref[0, :, cols])

    def exponents_of(scores):
        parts, peaks = [], []
        for half in range(2):
            own = jnp.where(allowed, scores[half * slots : (half + 1) * slots], MASKED)
            peak = jnp.max(own, axis=-1, keepdims=True)
            parts.append(jnp.exp(own - peak).astype(BF))
            peaks.append(peak)
        return jnp.concatenate(parts, axis=0), peaks

    def finish(pair, exponents, peaks, lse_lanes):
        cols = slice(pair * 128, (pair + 1) * 128)
        both = mm(exponents, jnp.concatenate([v_ref[0, :, cols], ones], axis=1))
        first, second = both[:slots], both[slots:]
        total = jnp.where(lane < HEAD, first[:, 128:], second[:, 128:])
        values = jnp.where(lane < HEAD, first[:, :128], second[:, :128])
        mixed_ref[0, :, cols] = (values * (1.0 / total)).astype(BF)
        for half, part in ((0, first), (1, second)):
            lse = peaks[half] + jnp.log(part[:, 128:])
            lse_lanes = jnp.where(lane == 2 * pair + half, lse, lse_lanes)
        return lse_lanes

    lse_lanes = jnp.zeros((slots, 128), F32)
    tables = [scores_of(pair) for pair in range(PAIRS)]
    for pair in range(PAIRS):
        exponents, peaks = exponents_of(tables[pair])
        lse_lanes = finish(pair, exponents, peaks, lse_lanes)
    lse_ref[0] = lse_lanes.T[:8, :]


def attention_forward(lengths, tokens, w_qkv, vec, kend):
    items, slots, _ = tokens.shape
    early = lambda g, i, *_: (jnp.where(g == 0, i, items - 1), 0, 0)
    cols = lambda g, i, *_: (i, 0, g)
    weight = pl.BlockSpec((D, GROUP), lambda g, i, *_: (0, g))
    return pl.pallas_call(
        forward_kernel,
        grid_spec=pltpu.PrefetchScalarGridSpec(
            num_scalar_prefetch=1,
            grid=(GROUPS, items),
            in_specs=[
                pl.BlockSpec((1, slots, D), early),
                weight,
                pl.BlockSpec((D, GROUP), lambda g, i, *_: (0, GROUPS + g)),
                pl.BlockSpec((D, GROUP), lambda g, i, *_: (0, 2 * GROUPS + g)),
                pl.BlockSpec((VEC_ROWS, D), lambda g, i, *_: (0, 0)),
                pl.BlockSpec((VEC_ROWS, GROUP), lambda g, i, *_: (0, g)),
                pl.BlockSpec((1, slots, 1), lambda g, i, *_: (i, 0, 0)),
            ],
            out_specs=[pl.BlockSpec((1, slots, D), early)]
            + [pl.BlockSpec((1, slots, GROUP), cols)] * 4
            + [pl.BlockSpec((1, 8, slots), lambda g, i, *_: (i, g, 0))],
            scratch_shapes=[pltpu.VMEM((items, slots, D), BF)],
        ),
        out_shape=[jax.ShapeDtypeStruct((items, slots, D), BF)] * 5
        + [jax.ShapeDtypeStruct((items, 8 * GROUPS, slots), F32)],
        compiler_params=pltpu.CompilerParams(vmem_limit_bytes=60 * MIB),
        cost_estimate=pl.CostEstimate(
            flops=2 * items * slots * D * 3 * D + 16 * items * HEADS * slots * slots * HEAD,
            bytes_accessed=20 * MIB,
            transcendentals=items * HEADS * slots * slots,
        ),
        name="attention_forward",
    )(lengths, tokens, w_qkv, w_qkv, w_qkv, vec, vec, kend)


GELU_SCALE = 0.7978845608028654
GELU_CUBE = 0.044715
STEPS = 4
PARTS = 3


def row_valid(len_ref, start, rows, slots, items):
    index = lax.broadcasted_iota(jnp.int32, (rows, 1), 0) + start
    valid = index < len_ref[0]
    for item in range(1, items):
        valid = valid | ((index >= item * slots) & (index < item * slots + len_ref[item]))
    return jnp.where(valid, 1.0, 0.0).astype(F32)


def middle_forward_kernel(items, slots):
    tile = items * slots // PARTS

    def kernel(
        len_ref, mixed_ref, tok_ref, cot_ref, wout_ref, vec_ref,
        middle_ref, n2_ref, dlow_ref, gbd_ref,
    ):
        part = pl.program_id(0)
        middle = (tok_ref[...].astype(F32) + mm(mixed_ref[...], wout_ref[...])) + vec_ref[4:5, :]
        middle_ref[...] = middle
        scaled, _inverse = norm_parts(middle)
        n2_ref[...] = (scaled * vec_ref[5:6, :] + vec_ref[6:7, :]).astype(BF)
        lower = cot_ref[...].astype(F32) * row_valid(len_ref, part * tile, tile, slots, items)
        dlow_ref[...] = lower.astype(BF)
        sums = jnp.sum(lower, axis=0, keepdims=True)
        gbd_ref[...] = jnp.where(part == 0, 0.0, gbd_ref[...]) + sums

    return kernel


def middle_forward(lengths, mixed, tokens, cotangent, w_all, vec, items, slots):
    row_count = items * slots
    tile = row_count // PARTS
    block = pl.BlockSpec((tile, D), lambda p, *_: (p, 0))
    fixed = lambda p, *_: (0, 0)
    return pl.pallas_call(
        middle_forward_kernel(items, slots),
        grid_spec=pltpu.PrefetchScalarGridSpec(
            num_scalar_prefetch=1,
            grid=(PARTS,),
            in_specs=[
                block, block, block,
                pl.BlockSpec((D, D), lambda p, *_: (0, 3)),
                pl.BlockSpec((VEC_ROWS, D), fixed),
            ],
            out_specs=[block, block, block, pl.BlockSpec((8, D), fixed)],
        ),
        out_shape=[
            jax.ShapeDtypeStruct((row_count, D), F32),
            jax.ShapeDtypeStruct((row_count, D), BF),
            jax.ShapeDtypeStruct((row_count, D), BF),
            jax.ShapeDtypeStruct((8, D), F32),
        ],
        compiler_params=pltpu.CompilerParams(vmem_limit_bytes=60 * MIB),
        cost_estimate=pl.CostEstimate(
            flops=2 * row_count * D * D, bytes_accessed=14 * MIB, transcendentals=0
        ),
        name="middle_forward",
    )(lengths, mixed, tokens, cotangent, w_all, vec)


def mlp_kernel(stacked, items, slots):
    tile = items * slots // PARTS

    def kernel(
        len_ref, n2, dlow, vec_ref, up_ref, down_ref, act, dn2_ref, gbu_ref, *rest
    ):
        outs = rest[:-5]
        dpre, pre_all, gu, gd, sems = rest[-5:]
        b = pl.program_id(0)
        slot = lax.rem(b, 2)
        go = len_ref[0] > 0

        def send(step, act_on):
            where = lax.rem(step, 2)
            if stacked:
                per, pairs = gu.shape[3], gd.shape[1]
                me = len_ref[items]
                up_rows = pl.ds(pl.multiple_of(per * step, 8), per)
                for n, half in ((1, 1 - me), (2, me)):
                    act_on(
                        pltpu.make_async_copy(
                            gu.at[where, :, half],
                            outs[n].at[:, up_rows, :],
                            sems.at[n, where],
                        )
                    )
                owners = pl.ds(pairs * step, pairs)
                act_on(
                    pltpu.make_async_copy(gd.at[where], outs[0].at[owners], sems.at[0, where])
                )
            else:
                at = pl.ds(pl.multiple_of(D * step, D), D)
                act_on(pltpu.make_async_copy(gu.at[where], outs[0].at[:, at], sems.at[0, where]))
                act_on(pltpu.make_async_copy(gd.at[where], outs[1].at[at, :], sems.at[1, where]))

        @pl.when(b == 0)
        def _():
            dn2_ref[...] = jnp.zeros_like(dn2_ref)

        gbu_ref[...] = jnp.zeros_like(gbu_ref)
        bias = vec_ref[pl.ds(8 + b, 1), :]
        for part in range(PARTS):
            at = slice(part * tile, (part + 1) * tile)

            @pl.when(go)
            def _():
                pre_all[...] = mm(n2[at, :], up_ref[...].reshape(D, D)) + bias

            @pl.when(go)
            def _():
                pre = pre_all[...]
                square = pre * pre
                half_t = 0.5 * jnp.tanh(GELU_SCALE * pre * (1.0 + GELU_CUBE * square))
                cdf = 0.5 + half_t
                act[at, :] = (pre * cdf).astype(BF)
                slope = cdf + pre * (0.5 - 2.0 * half_t * half_t) * (
                    GELU_SCALE + (3.0 * GELU_CUBE * GELU_SCALE) * square
                )
                d_pre = (mm_nt(dlow[at, :], down_ref[...].reshape(D, D)) * slope).astype(BF)
                dpre[at, :] = d_pre
                gbu_ref[0:1, :] += jnp.sum(d_pre.astype(F32), axis=0, keepdims=True)

            @pl.when(go)
            def _():
                dn2_ref[at, :] += mm_nt(dpre[at, :], up_ref[...].reshape(D, D))

        @pl.when(b >= 2)
        def _():
            send(b - 2, lambda copy: copy.wait())

        @pl.when(go)
        def _():
            gu[slot] = mm_tn(n2[...], dpre[...]).reshape(gu.shape[1:]).astype(BF)

        @pl.when(go)
        def _():
            gd[slot] = mm_tn(act[...], dlow[...]).reshape(gd.shape[1:]).astype(BF)

        send(b, lambda copy: copy.start())

        @pl.when(b == STEPS - 1)
        def _():
            send(b - 1, lambda copy: copy.wait())
            send(b, lambda copy: copy.wait())

    return kernel


def feed_forward(lengths, normed, d_lower, vec, up, down, stacked, items, slots):
    row_count = items * slots
    once = pl.Buffered(1)
    fixed = lambda b, *_: (0, 0)
    if stacked:
        devices, stack, _ = up.shape
        per = stack // 8
        up_spec = pl.BlockSpec((devices, per, D), lambda b, *_: (0, b, 0))
        down_spec = pl.BlockSpec((devices // 4, 4 * per, D), lambda b, *_: (b, 1, 0))
        grad_shapes = [
            jax.ShapeDtypeStruct((devices // 2, 2, 4 * per, D), BF)
        ] + [jax.ShapeDtypeStruct((devices // 2, 4 * per, D), BF)] * 2
        gu_shape, gd_shape = (devices // 2, 2, per, D), (devices // 8, 2, 4 * per, D)
    else:
        up_spec = pl.BlockSpec((D, D), lambda b, *_: (0, b))
        down_spec = pl.BlockSpec((D, D), lambda b, *_: (b, 0))
        grad_shapes = [
            jax.ShapeDtypeStruct((D, STEPS * D), BF),
            jax.ShapeDtypeStruct((STEPS * D, D), BF),
        ]
        gu_shape = gd_shape = (D, D)
    whole = pl.BlockSpec((row_count, D), fixed, pipeline_mode=once)
    return pl.pallas_call(
        mlp_kernel(stacked, items, slots),
        grid_spec=pltpu.PrefetchScalarGridSpec(
            num_scalar_prefetch=1,
            grid=(STEPS,),
            in_specs=[
                whole, whole,
                pl.BlockSpec((VEC_ROWS, D), fixed),
                up_spec,
                down_spec,
            ],
            out_specs=[
                pl.BlockSpec((row_count, D), lambda b, *_: (0, b)),
                whole,
                pl.BlockSpec((8, D), lambda b, *_: (0, b)),
            ]
            + [pl.BlockSpec(memory_space=pl.ANY)] * len(grad_shapes),
            scratch_shapes=[
                pltpu.VMEM((row_count, D), BF),
                pltpu.VMEM((row_count // PARTS, D), F32),
                pltpu.VMEM((2,) + gu_shape, BF),
                pltpu.VMEM((2,) + gd_shape, BF),
                pltpu.SemaphoreType.DMA((3, 2)),
            ],
        ),
        out_shape=[
            jax.ShapeDtypeStruct((row_count, STEPS * D), BF),
            jax.ShapeDtypeStruct((row_count, D), F32),
            jax.ShapeDtypeStruct((8, STEPS * D), F32),
        ]
        + grad_shapes,
        compiler_params=pltpu.CompilerParams(vmem_limit_bytes=60 * MIB),
        cost_estimate=pl.CostEstimate(
            flops=2 * row_count * D * D * 20,
            bytes_accessed=36 * MIB,
            transcendentals=row_count * 4 * D,
        ),
        name="feed_forward",
    )(lengths, normed, d_lower, vec, up, down)


def output_kernel(first, items, slots):
    tile = items * slots // PARTS

    def kernel(len_ref, middle_ref, act_ref, down_ref, vec_ref, *refs):
        part = pl.program_id(0) + first
        valid = row_valid(len_ref, part * tile, tile, slots, items)
        down = down_ref[...].reshape(STEPS * D, D)
        whole = middle_ref[...] + (mm(act_ref[...], down) + vec_ref[7:8, :])
        refs[-1][...] = (whole * valid).astype(BF)

    return kernel


def feed_forward_output(first, count, lengths, middle, active, down, vec, stacked, items, slots, so_far, after):
    tile = items * slots // PARTS
    vec, _after = lax.optimization_barrier((vec, after))
    once = pl.Buffered(1)
    if stacked:
        devices, stack, _ = down.shape
        spec = pl.BlockSpec(
            (devices, stack // 2, D), lambda p, *_: (0, 1, 0), pipeline_mode=once
        )
    else:
        spec = pl.BlockSpec((STEPS * D, D), lambda p, *_: (0, 0), pipeline_mode=once)
    block = lambda width: pl.BlockSpec((tile, width), lambda p, *_: (first + p, 0))
    return pl.pallas_call(
        output_kernel(first, items, slots),
        grid_spec=pltpu.PrefetchScalarGridSpec(
            num_scalar_prefetch=1,
            grid=(count,),
            in_specs=[
                block(D), block(STEPS * D), spec,
                pl.BlockSpec((VEC_ROWS, D), lambda p, *_: (0, 0)),
            ]
            + [pl.BlockSpec(memory_space=pl.ANY)] * len(so_far),
            out_specs=block(D),
        ),
        out_shape=jax.ShapeDtypeStruct((items * slots, D), BF),
        input_output_aliases={5: 0} if so_far else {},
        compiler_params=pltpu.CompilerParams(vmem_limit_bytes=60 * MIB),
        cost_estimate=pl.CostEstimate(
            flops=4 * count * items * slots * D * D, bytes_accessed=4 * MIB, transcendentals=0
        ),
        name="feed_forward_output",
    )(lengths, middle, active, down, vec, *so_far)


MIDDLE_PARTS = 5


def middle_kernel(tile, slots, items):
    def kernel(
        len_ref, dn2_ref, middle_ref, cot_ref, mixed_ref, wout_ref, vec_ref,
        dmid_ref, dmix_ref, delta_ref, sums_ref, *rest,
    ):
        gouts, (acc, branch) = rest[:-2], rest[-2:]
        part = pl.program_id(0)
        go = len_ref[0] > 0

        @pl.when(part == 0)
        def _():
            sums_ref[...] = jnp.zeros_like(sums_ref)
            acc[...] = jnp.zeros_like(acc)

        scaled, inverse = norm_parts(middle_ref[...])
        d_n2 = dn2_ref[...]
        valid = row_valid(len_ref, part * tile, tile, slots, items)
        d_middle = cot_ref[...].astype(F32) * valid + norm_back(
            d_n2, scaled, inverse, vec_ref[5:6, :]
        )
        dmid_ref[...] = d_middle
        low = d_middle.astype(BF)
        branch[...] = low
        sums_ref[...] += jnp.concatenate(
            [
                jnp.sum(d_n2 * scaled, axis=0, keepdims=True),
                jnp.sum(d_n2, axis=0, keepdims=True),
                jnp.sum(low.astype(F32), axis=0, keepdims=True),
                jnp.zeros((5, D), F32),
            ],
            axis=0,
        )

        @pl.when(go)
        def _():
            dmix_ref[...] = mm_nt(branch[...], wout_ref[...]).astype(BF)

        @pl.when(go)
        def _():
            acc[...] += mm_tn(mixed_ref[...], branch[...])

        @pl.when(go)
        def _():
            product = dmix_ref[...].astype(F32) * mixed_ref[...].astype(F32)
            row = lax.broadcasted_iota(jnp.int32, (D, 128), 0)
            lane = lax.broadcasted_iota(jnp.int32, (D, 128), 1)
            pick = jnp.where(row // HEAD == lane, 1.0, 0.0).astype(BF)
            delta_ref[...] = mm(product.astype(BF), pick)

        @pl.when(part == MIDDLE_PARTS - 1)
        def _():
            store_halves(gouts, acc[...], len_ref[items], slice(None))

    return kernel


def middle_backward(scalars, d_n2, middle, cotangent, mixed, w_all, vec, fast, items, slots, devices):
    row_count = items * slots
    tile = row_count // MIDDLE_PARTS
    fixed = lambda p, *_: (0, 0)
    block = pl.BlockSpec((tile, D), lambda p, *_: (p, 0))
    outs = split_shapes(fast, devices, D)
    return pl.pallas_call(
        middle_kernel(tile, slots, items),
        grid_spec=pltpu.PrefetchScalarGridSpec(
            num_scalar_prefetch=1,
            grid=(MIDDLE_PARTS,),
            in_specs=[
                block, block, block, block,
                pl.BlockSpec((D, D), lambda p, *_: (0, 3)),
                pl.BlockSpec((VEC_ROWS, D), fixed),
            ],
            out_specs=[
                block, block,
                pl.BlockSpec((tile, 128), lambda p, *_: (p, 0)),
                pl.BlockSpec((8, D), fixed),
            ]
            + [whole_block(v) for v in outs],
            scratch_shapes=[pltpu.VMEM((D, D), F32), pltpu.VMEM((tile, D), BF)],
        ),
        out_shape=[
            jax.ShapeDtypeStruct((row_count, D), F32),
            jax.ShapeDtypeStruct((row_count, D), BF),
            jax.ShapeDtypeStruct((row_count, 128), F32),
            jax.ShapeDtypeStruct((8, D), F32),
        ]
        + outs,
        compiler_params=pltpu.CompilerParams(vmem_limit_bytes=60 * MIB),
        cost_estimate=pl.CostEstimate(
            flops=10 * row_count * D * D, bytes_accessed=8 * MIB, transcendentals=0
        ),
        name="middle_backward",
    )(scalars, d_n2, middle, cotangent, mixed, w_all, vec)


def backward_kernel(
    len_ref, q_ref, k_ref, v_ref, dmix_ref, lse_ref, delta_ref, kend_ref, scaled_ref,
    wq_ref, wk_ref, wv_ref, table_ref,
    dqkv_ref, gbias_ref, norm_ref, *rest, base,
):
    gws, (acc, turned_delta) = rest[:-2], rest[-2:]
    g = pl.program_id(0)
    i = pl.program_id(1)
    items = pl.num_programs(1)
    last_item = items - 1
    turned_delta[...] = delta_ref[0].T
    slots = q_ref.shape[1]
    go = len_ref[0] > 0
    key = lax.broadcasted_iota(jnp.int32, (slots, slots), 0)
    allowed = key < kend_ref[0]
    fronts = []
    for pair in range(PAIRS):
        cols = slice(pair * 128, (pair + 1) * 128)
        queries = two_heads(q_ref[0, :, cols], HEAD ** -0.5)
        upstream = two_heads(dmix_ref[0, :, cols], 1.0)
        fronts.append(
            (
                queries,
                upstream,
                mm_nt(k_ref[0, :, cols], queries),
                mm_nt(v_ref[0, :, cols], upstream),
            )
        )
    for pair in range(PAIRS):
        queries, upstream, scores, d_probs = fronts[pair]
        dv = dk = None
        turned = []
        flipped = k_ref[0, :, pair * 128 : (pair + 1) * 128].T
        for half in range(2):
            head = 2 * pair + half
            at = slice(half * slots, (half + 1) * slots)
            probs = jnp.exp(
                jnp.where(allowed, scores[:, at], MASKED) - lse_ref[0, head : head + 1, :]
            )
            d_scores = (probs * (d_probs[:, at] - turned_delta[pl.ds(4 * (base + g) + head, 1), :])).astype(BF)
            dv_half = mm(probs.astype(BF), upstream[at])
            dk_half = mm(d_scores, queries[at])
            dv = dv_half if dv is None else dv + dv_half
            dk = dk_half if dk is None else dk + dk_half
            turned.append(mm(flipped, d_scores))
        row = lax.broadcasted_iota(jnp.int32, (128, 1), 0)
        dq = jnp.where(row < HEAD, turned[0], turned[1]).T * HEAD ** -0.5
        for which, part in ((0, dq), (1, dk), (2, dv)):
            start = which * GROUP + pair * 128
            dqkv_ref[0, :, start : start + 128] = part.astype(BF)

    @pl.when(go)
    def _():
        bias = jnp.sum(dqkv_ref[0].astype(F32), axis=0, keepdims=True)
        before = jnp.where(i == 0, 0.0, gbias_ref[...])
        gbias_ref[...] = before + bias

    @pl.when(i == 0)
    def _():
        acc[...] = mm_tn(scaled_ref[0], dqkv_ref[0])

    @pl.when(i > 0)
    def _():
        acc[...] += mm_tn(scaled_ref[0], dqkv_ref[0])

    @pl.when(i == last_item)
    def _():
        gain = table_ref[:, 0:1].astype(F32)
        shift = table_ref[:, 1:2].astype(F32)
        lane = lax.broadcasted_iota(jnp.int32, (1, SMALL), 1)
        gains = jnp.zeros((D, 1), F32)
        shifts = jnp.zeros((D, 1), F32)
        for which, ref in ((0, wq_ref), (1, wk_ref), (2, wv_ref)):
            cols = slice(which * GROUP, (which + 1) * GROUP)
            total = acc[:, cols]
            sums = gbias_ref[0:1, cols]
            weight = ref[...].astype(F32)
            store_halves(gws, gain * total + shift * sums, len_ref[items], cols)
            gains = gains + jnp.sum(weight * total, axis=-1, keepdims=True)
            shifts = shifts + jnp.sum(weight * sums, axis=-1, keepdims=True)
        new = jnp.where(lane == 0, gains, jnp.where(lane == 1, shifts, 0.0))
        norm_ref[...] = jnp.where(g == 0, 0.0, norm_ref[...]) + new


def attention_backward(
    base, count, scalars, q, k, v, d_mixed, lse, delta, kend_row, scaled, w_all, fast, devices
):
    items, slots, _ = q.shape
    rows = lambda g, i, *_: (i, 0, 0)
    block = pl.BlockSpec((1, slots, GROUP), lambda g, i, *_: (i, 0, base + g))
    weight = lambda which: pl.BlockSpec(
        (D, GROUP), lambda g, i, *_: (0, which * GROUPS + base + g)
    )
    outs = split_shapes(fast, devices, count * D)
    return pl.pallas_call(
        functools.partial(backward_kernel, base=base),
        grid_spec=pltpu.PrefetchScalarGridSpec(
            num_scalar_prefetch=1,
            grid=(count, items),
            in_specs=[
                block, block, block, block,
                pl.BlockSpec((1, 8, slots), lambda g, i, *_: (i, base + g, 0)),
                pl.BlockSpec((1, slots, 128), rows),
                pl.BlockSpec((1, 1, slots), rows),
                pl.BlockSpec((1, slots, D), rows),
                weight(0), weight(1), weight(2),
                pl.BlockSpec((D, SMALL), lambda g, i, *_: (0, 4 * D // SMALL)),
            ],
            out_specs=[
                pl.BlockSpec((1, slots, D), lambda g, i, *_: (i, 0, g)),
                pl.BlockSpec((8, D), lambda g, i, *_: (0, g)),
                pl.BlockSpec((D, SMALL), lambda g, i, *_: (0, 0)),
            ]
            + [
                pl.BlockSpec(
                    v.shape[:-1] + (D,), lambda g, i, *_, n=len(v.shape): (0,) * (n - 1) + (g,)
                )
                for v in outs
            ],
            scratch_shapes=[pltpu.VMEM((D, D), F32), pltpu.VMEM((128, slots), F32)],
        ),
        out_shape=[
            jax.ShapeDtypeStruct((items, slots, count * D), BF),
            jax.ShapeDtypeStruct((8, count * D), F32),
            jax.ShapeDtypeStruct((D, SMALL), F32),
        ]
        + outs,
        compiler_params=pltpu.CompilerParams(vmem_limit_bytes=60 * MIB),
        cost_estimate=pl.CostEstimate(
            flops=14 * count * items * slots * D * D,
            bytes_accessed=8 * count * MIB,
            transcendentals=count * items * 4 * slots * slots,
        ),
        name="attention_backward",
    )(scalars, q, k, v, d_mixed, lse, delta, kend_row, scaled, w_all, w_all, w_all, w_all)


def input_kernel(*refs):
    parts, (w_ref, tok_ref, dmid_ref, vec_ref, grad_ref) = refs[:-5], refs[-5:]
    places = [(ref, n) for ref in parts for n in range(ref.shape[2] // D)]
    total = None
    for g in range(GROUPS):
        for which in range(3):
            weight = w_ref[:, which * D + g * GROUP : which * D + (g + 1) * GROUP]
            ref, n = places[g]
            start = n * D + which * GROUP
            part = mm_nt(ref[0, :, start : start + GROUP], weight)
            total = part if total is None else total + part
    scaled, inverse = norm_parts(tok_ref[0].astype(F32))
    grad_ref[0] = dmid_ref[0] + norm_back(total, scaled, inverse, vec_ref[0:1, :])


def input_backward(d_qkv, w_qkv, tokens, d_middle, vec, after):
    items, slots, _ = tokens.shape
    vec, _after = lax.optimization_barrier((vec, after))
    rows = lambda i: (i, 0, 0)
    fixed = lambda i: (0, 0)
    block = pl.BlockSpec((1, slots, D), rows)
    return pl.pallas_call(
        input_kernel,
        grid=(items,),
        in_specs=[
            *[pl.BlockSpec((1, slots, part.shape[2]), rows) for part in d_qkv],
            pl.BlockSpec((D, 3 * D), fixed),
            block, block,
            pl.BlockSpec((VEC_ROWS, D), fixed),
        ],
        out_specs=block,
        out_shape=jax.ShapeDtypeStruct((items, slots, D), F32),
        compiler_params=pltpu.CompilerParams(vmem_limit_bytes=60 * MIB),
        cost_estimate=pl.CostEstimate(
            flops=10 * items * slots * D * D, bytes_accessed=8 * MIB, transcendentals=0
        ),
        name="input_backward",
    )(*d_qkv, w_qkv, tokens, d_middle, vec)


def own_kernel(keep_ref, got_ref, *refs):
    rows = keep_ref.shape[0]
    up = refs[:3] if len(refs) > 10 else ()
    qkv_ref, out_ref, *refs = refs[len(up) :]
    total = keep_ref[...] + got_ref[...].astype(F32)
    for which in range(3):
        for g in range(GROUPS):
            start = g * D + which * GROUP
            qkv_ref[:, which * D + g * GROUP : which * D + (g + 1) * GROUP] = total[
                :, start : start + GROUP
            ]
    out_ref[...] = total[:, 3 * D + SMALL :]
    lines = total[:, 3 * D : 3 * D + SMALL].T
    at = 0
    for ref, (_name, count) in zip(refs, COLUMNS):
        ref[...] = jnp.concatenate([lines[at + j : at + j + 1, :] for j in range(count)], axis=1)
        at += count
    for n, ref in enumerate(up[:2]):
        for half in range(2):
            b = 2 * n + half
            own = ref[half * rows : (half + 1) * rows, :]
            got = up[2][b * rows : (b + 1) * rows, :].astype(F32)
            refs[-1][:, b * D : (b + 1) * D] = own + got


def own_grads(keep, got, *up):
    rows = keep.shape[0]
    shapes = [(rows, 3 * D), (rows, D)] + [(1, count * rows) for _name, count in COLUMNS]
    if up:
        shapes.append((rows, STEPS * D))
    return pl.pallas_call(
        own_kernel,
        out_shape=[jax.ShapeDtypeStruct(shape, F32) for shape in shapes],
        compiler_params=pltpu.CompilerParams(vmem_limit_bytes=16 * MIB),
        name="own_grads",
    )(keep, got, *up)


def swap(x, axis, bit, size):
    return lax.ppermute(x, axis, [(i, i ^ (1 << bit)) for i in range(size)])


def own_bit(axis, bit):
    return (lax.axis_index(axis) >> bit) & 1


def doubled(x, axis, bit, size, at):
    other = jnp.expand_dims(swap(x, axis, bit, size), at)
    mine = jnp.expand_dims(x, at)
    return jnp.where(
        own_bit(axis, bit) == 0,
        jnp.concatenate([mine, other], at),
        jnp.concatenate([other, mine], at),
    )


def gather_rows(x, cut, sizes):
    rows = x.shape[0]
    wide, narrow = sizes
    if sizes != (8, 4):
        return lax.all_gather(x, AXES, axis=0, tiled=True)

    def ordered(mine, other, axis, bit, at):
        mine, other = jnp.expand_dims(mine, at), jnp.expand_dims(other, at)
        return jnp.where(
            own_bit(axis, bit) == 0,
            jnp.concatenate([mine, other], at),
            jnp.concatenate([other, mine], at),
        )

    away = lambda mask: lax.ppermute(x, "wide", [(i, i ^ mask) for i in range(wide)])
    near, far, both = away(2), away(4), away(6)
    x = ordered(ordered(x, near, "wide", 1, 0), ordered(far, both, "wide", 1, 0), "wide", 2, 0)
    a, b = x[..., :cut], x[..., cut:]
    a = doubled(a, "wide", 0, wide, 2)
    b = doubled(b, "narrow", 1, narrow, 2)
    a = doubled(a, "narrow", 1, narrow, 3)
    b = doubled(b, "wide", 0, wide, 2)
    x = jnp.concatenate([a, b], axis=-1)
    x = doubled(x, "narrow", 0, narrow, 4)
    return x.reshape(wide * narrow * rows, -1)


def fold_kernel(_bits_ref, *refs):
    keeps, gots, outs = refs[:4], refs[4:8], refs[8:]
    for keep, got, out in zip(keeps, gots, outs):
        out[...] = (keep[...].astype(F32) + got[...].astype(F32)).astype(BF)


def fold(scalars, keep, got, cut, items):
    parts, rows, _ = keep.shape
    quads = parts // 4
    side = lambda bits, n, mine: bits[items + n] if mine else 1 - bits[items + n]
    by_x = lambda mine: pl.BlockSpec(
        (1, 2, 1, cut, D), lambda p, bits: (p, 0, side(bits, 1, mine), 0, 0)
    )
    by_y = lambda mine: pl.BlockSpec(
        (1, 1, 2, cut, D), lambda p, bits: (p, side(bits, 2, mine), 0, 1, 0)
    )
    specs = [by_x(False), by_x(True), by_y(False), by_y(True)]
    shapes = [jax.ShapeDtypeStruct((quads, 2, 1, cut, D), BF)] * 2
    shapes += [jax.ShapeDtypeStruct((quads, 1, 2, cut, D), BF)] * 2
    at = lambda p, *_: (p, 0, 0, 0, 0)
    keep, got = (t.reshape(quads, 2, 2, rows, D) for t in (keep, got))
    return pl.pallas_call(
        fold_kernel,
        grid_spec=pltpu.PrefetchScalarGridSpec(
            num_scalar_prefetch=1,
            grid=(quads,),
            in_specs=specs * 2,
            out_specs=[pl.BlockSpec((1,) + v.shape[1:], at) for v in shapes],
        ),
        out_shape=shapes,
        compiler_params=pltpu.CompilerParams(vmem_limit_bytes=60 * MIB),
        cost_estimate=pl.CostEstimate(flops=1, bytes_accessed=14 * MIB, transcendentals=0),
        name="fold",
    )(scalars, *[keep] * 4, *[got] * 4)


def together(*values):
    return lax.optimization_barrier(values)


def halves(keep, got, axis, bit, at, kind=F32):
    me = own_bit(axis, bit)

    def half(which):
        part = lambda x: lax.dynamic_index_in_dim(x, which, at, keepdims=False).astype(F32)
        return part(keep) if got is None else part(keep) + part(got)

    return half(1 - me).astype(BF), half(me).astype(kind)


def body(sizes):
    def run(
        tokens, lengths, blocks, ln1_gain, ln1_bias, qkv_weight, qv_bias, out_weight, out_bias,
        ln2_gain, ln2_bias, up_weight, up_bias, down_weight, down_bias, cotangent,
    ):
        items, slots, _ = tokens.shape
        row_count = items * slots
        rows = qkv_weight.shape[0]
        devices = sizes[0] * sizes[1]
        stacked = sizes == (8, 4)

        vectors = (
            ln1_gain, ln1_bias, qv_bias, out_bias, ln2_gain, ln2_bias, up_bias, down_bias,
        )
        kend_row, kend, first, *rest = pack_parameters(
            lengths, blocks, vectors, qkv_weight, out_weight, up_weight, down_weight, stacked
        )
        if stacked:
            whole = lax.all_gather(rest[0], AXES, axis=0, tiled=True)
            up = down = whole.reshape(devices, 8 * rows, D)
        else:
            up = lax.all_gather(up_weight, AXES, axis=0, tiled=True)
            down = lax.all_gather(down_weight, AXES, axis=0, tiled=True)
        w_all = gather_rows(first, 2 * D, sizes)
        vec = unpack_small(w_all, rows)

        scaled, q, k, v, mixed, lse = attention_forward(
            lengths, tokens, w_all, vec, kend
        )
        flat = lambda t: t.reshape(row_count, D)
        cube = lambda t: t.reshape(items, slots, D)
        middle, normed, d_lower, gb_down = middle_forward(
            lengths, flat(mixed), flat(tokens), flat(cotangent), w_all, vec, items, slots
        )
        wide, narrow = sizes
        fast = sizes == (8, 4)
        bits = [own_bit("narrow", 0), own_bit("narrow", 1), own_bit("wide", 0)]
        scalars = jnp.concatenate([lengths, jnp.stack(bits).astype(lengths.dtype)])
        active, d_n2, gb_up, *ffn = feed_forward(
            scalars, normed, d_lower, vec, up, down, fast, items, slots
        )

        def middle_part():
            return middle_backward(
                scalars, d_n2, middle, flat(cotangent), flat(mixed), w_all, vec, fast, items,
                slots, devices,
            )

        def attention_part(base, count, d_mixed, delta):
            d_qkv, sums, norms, *grads = attention_backward(
                base, count, scalars, q, k, v, cube(d_mixed), lse,
                delta.reshape(items, slots, 128), kend_row, scaled, w_all, fast, devices,
            )
            return d_qkv, sums, norms, grads

        def input_part(d_qkv, d_middle, after):
            return input_backward(d_qkv, w_all, tokens, cube(d_middle), vec, after)

        def output_part(after):
            return feed_forward_output(
                0, PARTS, lengths, middle, active, down, vec, fast, items, slots, (), after
            )

        def small_part(norms, sums, mid_sums):
            return pack_small(
                scalars, norms, sums, mid_sums, gb_up, gb_down, rows, fast, items
            )

        def rest_of_backward():
            core = ("narrow", 0, narrow)
            x_link, y_link = ("narrow", 1), ("wide", 0)
            z_near, z_far = ("wide", 1), ("wide", 2)
            size = {"wide": wide, "narrow": narrow}
            move = lambda value, link: swap(value, *link, size[link[0]])
            beside = lambda *parts: jnp.concatenate(parts, axis=-1)
            cut = 2 * rows

            up_got = swap(ffn[1], *core)
            d_middle, d_mixed, delta, mid_sums, *g_out = middle_part()
            up_got, d_mixed, *g_out = together(up_got, d_mixed, *g_out)
            out_got = swap(g_out[0], *core)
            c_send, c_keep, d_send, d_keep = fold(scalars, ffn[2], up_got, cut, items)
            c_send, d_send, d_mixed = together(c_send, d_send, d_mixed)
            c_got, d_got = move(c_send, x_link), move(d_send, y_link)
            d_qkv, sums, norms, grads = attention_part(0, 2, d_mixed, delta)
            c_got, d_got, out_got, c_keep, d_keep, d_mixed, grads[0], norms = together(
                c_got, d_got, out_got, c_keep, d_keep, d_mixed, grads[0], norms
            )
            shaped = lambda t: t.reshape((2, 2, 2, cut, D))
            c_send, c_keep = halves(shaped(c_keep), shaped(c_got), *y_link, 2, BF)
            d_send, d_keep = halves(shaped(d_keep), shaped(d_got), *x_link, 2, BF)
            c_send, d_send, c_keep, d_keep, d_mixed, out_got = together(
                c_send, d_send, c_keep, d_keep, d_mixed, out_got
            )
            c_got, d_got = move(c_send, y_link), move(d_send, x_link)
            a_got = swap(grads[0], *core)
            d_qkv_2, sums_2, norms_2, grads_2 = attention_part(2, 1, d_mixed, delta)
            c_got, d_got, a_got, c_keep, d_keep, out_got, grads_2[0], norms_2 = together(
                c_got, d_got, a_got, c_keep, d_keep, out_got, grads_2[0], norms_2
            )

            small = small_part([norms, norms_2], [sums, sums_2], mid_sums)
            shaped = lambda t: t.reshape((2, 2, 2, 2, rows, -1))
            b_send = beside(grads_2[0], small[0])
            b_got = swap(b_send, *core)
            c_send, c_keep = halves(c_keep, c_got, *z_near, 1)
            d_send, d_keep = halves(d_keep, d_got, *z_near, 1)
            send = jnp.concatenate([c_send, d_send], axis=-2)
            up_got = move(send, z_near)
            a_send, a_keep = halves(shaped(grads[1]), shaped(a_got), *x_link, 3)
            out_send, out_keep = halves(shaped(g_out[1]), shaped(out_got), *y_link, 2)
            b_got, a_send, out_send, send = together(b_got, a_send, out_send, send)
            b_send, b_keep = halves(
                shaped(beside(grads_2[1], small[1])), shaped(b_got), *y_link, 2
            )
            b_send, b_keep = beside(b_send, out_send), beside(b_keep, out_keep)
            a_send, b_send = together(a_send, b_send)
            a_got, b_got = move(a_send, x_link), move(b_send, y_link)
            input_grad = input_part([d_qkv, d_qkv_2], d_middle, (a_send, b_send))
            a_got, b_got, up_got, input_grad = together(a_got, b_got, up_got, input_grad)
            a_send, a_keep = halves(a_keep, a_got, *y_link, 2)
            b_send, b_keep = halves(b_keep, b_got, *x_link, 2)
            c_send, c_keep = halves(c_keep, up_got[:, :cut], *z_far, 0)
            d_send, d_keep = halves(d_keep, up_got[:, cut:], *z_far, 0)
            send = jnp.concatenate([c_send, d_send], axis=-2)
            a_send, b_send, send = together(a_send, b_send, send)
            a_got, b_got = move(a_send, y_link), move(b_send, x_link)
            up_got = move(send, z_far)
            output = output_part((a_send, b_send))
            a_got, b_got, up_got, output = together(a_got, b_got, up_got, output)
            send, keep = halves(beside(a_keep, b_keep), beside(a_got, b_got), *z_near, 1)
            got = move(send, z_near)
            send, keep = halves(keep, got, *z_far, 0)
            got = move(send, z_far)
            return [input_grad, output, *own_grads(keep, got, c_keep, d_keep, up_got)]

        if not fast:
            scatter = lambda x: lax.psum_scatter(
                x.astype(F32), AXES, scatter_dimension=0, tiled=True
            )
            grad_up, grad_down = scatter(ffn[0]), scatter(ffn[1])
            d_middle, d_mixed, delta, mid_sums, *g_out = middle_part()
            d_qkv, sums, norms, grads = attention_part(0, GROUPS, d_mixed, delta)
            input_grad, output = input_part([d_qkv], d_middle, ()), output_part(())
            keep = scatter(
                jnp.concatenate(
                    [grads[0], small_part([norms], [sums], mid_sums)[0], g_out[0]], axis=1
                )
            )
            own_qkv, own_out, *own_small = own_grads(keep, jnp.zeros(keep.shape, BF))
        else:
            grad_down = lax.psum_scatter(
                ffn[0].reshape(STEPS * D, D), AXES, scatter_dimension=0, tiled=True
            ).astype(F32)
            shapes = jax.eval_shape(rest_of_backward)
            input_grad, output, own_qkv, own_out, *own_small, grad_up = lax.cond(
                scalars[0] > 0,
                rest_of_backward,
                lambda: [jnp.zeros(v.shape, v.dtype) for v in shapes],
            )
        ln1_g, ln1_b, qv_b, out_b, ln2_g, ln2_b, up_b, down_b = [v.reshape(-1) for v in own_small]
        return (
            cube(output), input_grad, ln1_g, ln1_b, own_qkv, qv_b, own_out, out_b, ln2_g, ln2_b,
            grad_up, up_b, grad_down, down_b,
        )

    return run


def solution(mesh):
    sizes = (mesh.shape["wide"], mesh.shape["narrow"])
    one = P(AXES)
    two = P(AXES, None)
    three = P(AXES, None, None)
    return jax.shard_map(
        body(sizes),
        mesh=mesh,
        in_specs=(
            three, one, two, one, one, two, one, two, one, one, one, two, one, two, one, three,
        ),
        out_specs=(
            three, three, one, one, two, one, two, one, one, one, two, one, two, one,
        ),
        check_vma=False,
    )
```

```python
import functools

import jax
import jax.numpy as jnp
from jax import lax
from jax.experimental import pallas as pl
from jax.experimental.pallas import tpu as pltpu
from jax.sharding import PartitionSpec as P

D = 768
HEADS = 12
HEAD = 64
GROUP = 256
GROUPS = D // GROUP
PAIRS = GROUP // 128
EPS = 1e-05
MASKED = -1e30
AXES = ("wide", "narrow")
BF = jnp.bfloat16
F32 = jnp.float32
MIB = 1 << 20
VEC_ROWS = 16
SMALL = 128
BLOCKS = 5


def mm(a, b):
    return jnp.dot(a, b, preferred_element_type=F32)


def mm_nt(a, b):
    return lax.dot_general(a, b, (((1,), (1,)), ((), ())), preferred_element_type=F32)


def mm_tn(a, b):
    return lax.dot_general(a, b, (((0,), (0,)), ((), ())), preferred_element_type=F32)


def norm_parts(x):
    centred = x - jnp.mean(x, axis=-1, keepdims=True)
    inverse = lax.rsqrt(jnp.mean(centred * centred, axis=-1, keepdims=True) + EPS)
    return centred * inverse, inverse


def norm_back(d_normed, scaled, inverse, gain):
    h = d_normed * gain
    return inverse * (
        h
        - jnp.mean(h, axis=-1, keepdims=True)
        - scaled * jnp.mean(h * scaled, axis=-1, keepdims=True)
    )


def lane_mask(half, value):
    lane = lax.broadcasted_iota(jnp.int32, (1, 128), 1)
    return jnp.where((lane // HEAD) == half, value, 0.0).astype(BF)


MARK = 64


def in_three(value):
    high = value.astype(BF).astype(F32)
    middle = (value - high).astype(BF).astype(F32)
    low = value - high - middle
    return -(high + pltpu.roll(middle, 16, 1) + pltpu.roll(low, 32, 1)).astype(BF)


def offset_lanes(head):
    lane = lax.broadcasted_iota(jnp.int32, (1, 128), 1)
    return jnp.where((lane < 48) & (lane % 16 == head), 1.0, 0.0).astype(BF)


COLUMNS = (("ln1_gain", 1), ("ln1_bias", 1), ("qv_bias", 2), ("out_bias", 1), ("ln2_gain", 1), ("ln2_bias", 1), ("up_bias", 4), ("down_bias", 1))


def store_halves(refs, value, me, cols):
    if len(refs) == 1:
        refs[0][:, cols] = value.astype(BF)
        return
    pairs, rows, _ = refs[0].shape
    value = value.reshape(pairs, 2, rows, value.shape[1])
    even, odd = value[:, 0], value[:, 1]
    refs[0][:, :, cols] = jnp.where(me == 0, odd, even).astype(BF)
    refs[1][:, :, cols] = jnp.where(me == 0, even, odd).astype(BF)


def split_shapes(fast, devices, columns):
    if not fast:
        return [jax.ShapeDtypeStruct((D, columns), BF)]
    return [jax.ShapeDtypeStruct((devices // 2, D // devices, columns), BF)] * 2


def whole_block(value):
    return pl.BlockSpec(value.shape, lambda *_: (0,) * len(value.shape))


def pack_kernel(stacked):
    def kernel(len_ref, blocks_ref, *refs):
        vectors, (qkv_ref, out_ref, up_ref, down_ref, key_ref, query_ref, first_ref) = (
            refs[:8], refs[8:15],
        )
        rows = qkv_ref.shape[0]
        for i in range(blocks_ref.shape[0]):
            line = blocks_ref[i : i + 1, :].astype(F32)
            block = jnp.broadcast_to(line, (128, line.shape[1])).T
            slot = lax.broadcasted_iota(jnp.int32, block.shape, 0)
            lane = lax.broadcasted_iota(jnp.int32, block.shape, 1)
            mark = (lane - MARK).astype(F32)
            own = jnp.where(slot < len_ref[i], block, float(BLOCKS))
            key_ref[i] = jnp.where((lane < 48) | (mark == own), 1.0, 0.0).astype(BF)
            barred = (mark > block) & (mark <= BLOCKS)
            query_ref[i] = jnp.where(barred, MASKED, 0.0).astype(BF)
        lines = []
        for ref, (_name, count) in zip(vectors, COLUMNS):
            line = ref[...].astype(F32)
            lines += [line[:, j * rows : (j + 1) * rows] for j in range(count)]
        table = jnp.concatenate(lines + [jnp.zeros((SMALL - len(lines), rows), F32)], axis=0)
        first_ref[:, : 3 * D] = qkv_ref[...]
        first_ref[:, 3 * D : 4 * D] = out_ref[...]
        first_ref[:, 4 * D :] = table.T.astype(BF)
        if stacked:
            rest_ref = refs[15]
            for b in range(4):
                rest_ref[b * rows : (b + 1) * rows, :] = up_ref[:, b * D : (b + 1) * D]
            rest_ref[4 * rows :, :] = down_ref[...]

    return kernel


def pack_parameters(lengths, blocks, vectors, qkv, out, up, down, stacked):
    rows = qkv.shape[0]
    items, slots = blocks.shape
    shapes = [
        jax.ShapeDtypeStruct((items, slots, 128), BF),
        jax.ShapeDtypeStruct((items, slots, 128), BF),
        jax.ShapeDtypeStruct((rows, 4 * D + SMALL), BF),
    ]
    if stacked:
        shapes.append(jax.ShapeDtypeStruct((8 * rows, D), BF))
    values = [blocks] + [v.reshape(1, -1) for v in vectors] + [qkv, out, up, down]
    return pl.pallas_call(
        pack_kernel(stacked),
        grid_spec=pltpu.PrefetchScalarGridSpec(
            num_scalar_prefetch=1,
            grid=(1,),
            in_specs=[whole_block(v) for v in values],
            out_specs=[whole_block(v) for v in shapes],
        ),
        out_shape=shapes,
        compiler_params=pltpu.CompilerParams(vmem_limit_bytes=60 * MIB),
        name="pack_parameters",
    )(lengths, *values)


def from_table(lines, count, rows, start, pick_rows):
    lane = lax.broadcasted_iota(jnp.int32, (1, D), 1) + start
    first = start // count // 128 * 128
    place = lax.broadcasted_iota(jnp.int32, (pick_rows, D), 0) + first
    at = lax.broadcasted_iota(jnp.int32, (pick_rows, D), 1) + start
    pick = (place == rows * (at // (count * rows)) + at % rows).astype(F32).astype(BF)
    lines = mm(lines[:, first : first + pick_rows].astype(BF), pick)
    which = lane % (count * rows) // rows
    line = lines[0:1, :]
    for j in range(1, count):
        line = jnp.where(which == j, lines[j : j + 1, :], line)
    return line


def unpack(table, vec_ref, rows):
    lines = table.astype(F32).T
    vec_ref[0:2, :] = lines[0:2, :]
    vec_ref[2:3, :] = from_table(lines[2:4, :], 2, rows, 0, D // 2)
    vec_ref[3:4, :] = from_table(lines[2:4, :], 2, rows, D, D // 2)
    vec_ref[4:7, :] = lines[4:7, :]
    vec_ref[7:8, :] = lines[11:12, :]
    for b in range(4):
        vec_ref[8 + b : 9 + b, :] = from_table(lines[7:11, :], 4, rows, b * D, 256)
    vec_ref[12:16, :] = jnp.zeros((4, D), F32)


def to_table(line, count, rows, start, pick_rows, column):
    row = lax.broadcasted_iota(jnp.int32, (SMALL, D), 0)
    at = lax.broadcasted_iota(jnp.int32, (SMALL, D), 1) + start
    spread = jnp.where(row - column == at % (count * rows) // rows, line, 0.0).astype(BF)
    place = lax.broadcasted_iota(jnp.int32, (pick_rows, D), 0) + start // count
    lane = lax.broadcasted_iota(jnp.int32, (pick_rows, D), 1) + start
    pick = (place == rows * (lane // (count * rows)) + lane % rows).astype(F32).astype(BF)
    return mm_nt(pick, spread)


def small_table(norms, lines, mid_sums, up_sums, down_sums, rows):
    row = lax.broadcasted_iota(jnp.int32, (SMALL, D), 0)
    plain = jnp.zeros((SMALL, D), F32)
    for at, line in (
        (4, mid_sums[2:3, :]), (5, mid_sums[0:1, :]), (6, mid_sums[1:2, :]), (11, down_sums),
    ):
        plain = jnp.where(row == at, line, plain)
    halves = []
    for part, which in enumerate((0, 2)):
        line = jnp.concatenate(
            [
                lines[:, g * D + which * GROUP : g * D + (which + 1) * GROUP]
                for g in range(GROUPS)
            ],
            axis=1,
        )
        halves.append(to_table(line, 2, rows, part * D, D // 2, 2))
    quarters = [
        to_table(up_sums[:, b * D : (b + 1) * D], 4, rows, b * D, D // 4, 7) for b in range(4)
    ]
    return (
        plain.T + norms + jnp.concatenate(halves, axis=0) + jnp.concatenate(quarters, axis=0)
    )


def two_heads(x, value):
    return jnp.concatenate([x * lane_mask(0, value), x * lane_mask(1, value)], axis=0)


def whole_rows(refs, me, x_first):
    if len(refs) == 1:
        return refs[0][...]
    mine, other = refs[0][...].astype(F32), refs[1][...].astype(F32)
    even = jnp.where(me == 0, mine, other)
    odd = jnp.where(me == 0, other, mine)
    pieces = []
    for owner in range(even.shape[0]):
        zz, y, x = owner // 4, owner // 2 % 2, owner % 2
        at = (8 * x + 4 * y if x_first else 8 * y + 4 * x) + zz
        pieces += [even[at], odd[at]]
    return jnp.concatenate(pieces, axis=0).astype(BF)


def forward_kernel(len_ref, tok_ref, key_ref, query_ref, *refs, rows, items, parts):
    weights, refs = refs[: 5 * parts], refs[5 * parts :]
    scaled_ref, q_ref, k_ref, v_ref, mixed_ref, lse_ref, vec_ref, *whole, n1 = refs
    wq_ref, wk_ref, wv_ref, wout_ref, table_ref = whole
    g = pl.program_id(0)
    i = pl.program_id(1)
    slots = tok_ref.shape[1]
    go = len_ref[0] > 0
    own = pl.ds(pl.multiple_of(g * GROUP, GROUP), GROUP)

    @pl.when(i == 0)
    def _():
        for n, ref in enumerate((wq_ref, wk_ref, wv_ref, wout_ref)):
            ref[...] = whole_rows(weights[n * parts : (n + 1) * parts], len_ref[items], n < 2)

    @pl.when((g == 0) & (i == 0))
    def _():
        table_ref[...] = whole_rows(weights[4 * parts :], len_ref[items], False)
        unpack(table_ref[...], vec_ref, rows)

    @pl.when(g == 0)
    def _():
        scaled, _inverse = norm_parts(tok_ref[0].astype(F32))
        scaled_ref[0] = scaled.astype(BF)
        n1[i] = (scaled * vec_ref[0:1, :] + vec_ref[1:2, :]).astype(BF)

    @pl.when(go)
    def _():
        q_ref[0] = (mm(n1[i], wq_ref[...]) + vec_ref[2:3, own]).astype(BF)

    @pl.when(go)
    def _():
        k_ref[0] = mm(n1[i], wk_ref[...]).astype(BF)

    @pl.when(go)
    def _():
        v_ref[0] = (mm(n1[i], wv_ref[...]) + vec_ref[3:4, own]).astype(BF)

    lane = lax.broadcasted_iota(jnp.int32, (1, 128), 1)
    ones = jnp.ones((slots, 128), BF)
    marks = jnp.concatenate([query_ref[0], query_ref[0]], axis=0)

    def scores_of(pair):
        cols = slice(pair * 128, (pair + 1) * 128)
        queries = two_heads(q_ref[0, :, cols], HEAD ** -0.5)
        return mm_nt(
            jnp.concatenate([queries, marks], axis=1),
            jnp.concatenate([k_ref[0, :, cols], key_ref[0]], axis=1),
        )

    def exponents_of(scores):
        parts, peaks = [], []
        for half in range(2):
            own = scores[half * slots : (half + 1) * slots]
            peak = jnp.max(own, axis=-1, keepdims=True)
            parts.append(jnp.exp(own - peak).astype(BF))
            peaks.append(peak)
        return jnp.concatenate(parts, axis=0), peaks

    def finish(pair, exponents, peaks, lse_lanes):
        cols = slice(pair * 128, (pair + 1) * 128)
        both = mm(exponents, jnp.concatenate([v_ref[0, :, cols], ones], axis=1))
        first, second = both[:slots], both[slots:]
        total = jnp.where(lane < HEAD, first[:, 128:], second[:, 128:])
        values = jnp.where(lane < HEAD, first[:, :128], second[:, :128])
        mixed_ref[0, :, cols] = (values * (1.0 / total)).astype(BF)
        for half, part in ((0, first), (1, second)):
            lse = peaks[half] + jnp.log(part[:, 128:])
            lse_lanes = jnp.where(lane == 2 * pair + half, lse, lse_lanes)
        return lse_lanes

    lse_lanes = jnp.zeros((slots, 128), F32)
    tables = [scores_of(pair) for pair in range(PAIRS)]
    for pair in range(PAIRS):
        exponents, peaks = exponents_of(tables[pair])
        lse_lanes = finish(pair, exponents, peaks, lse_lanes)
    lse_ref[0] = in_three(lse_lanes)


def attention_forward(scalars, tokens, first, key_marks, query_marks, rows):
    items, slots, _ = tokens.shape
    early = lambda g, i, *_: (jnp.where(g == 0, i, items - 1), 0, 0)
    cols = lambda g, i, *_: (i, 0, g)
    fixed = lambda g, i, *_: (0, 0)

    parts = len(first[0])

    def given(width, index):
        if parts == 1:
            return [pl.BlockSpec((D, width), lambda g, i, *_: (0, index(g)))]
        shape = (first[0][0].shape[0], rows, width)
        return [pl.BlockSpec(shape, lambda g, i, *_: (0, 0, index(g)))] * parts

    specs = []
    for n in range(4):
        specs += given(GROUP, lambda g, n=n: n % 2 * GROUPS + g)
    specs += given(SMALL, lambda g: 2 * D // SMALL)
    sources = [*first[0] * 2, *first[1] * 3]
    weight = pl.BlockSpec((D, GROUP), lambda g, i, *_: (0, g))
    return pl.pallas_call(
        functools.partial(forward_kernel, rows=rows, items=items, parts=parts),
        grid_spec=pltpu.PrefetchScalarGridSpec(
            num_scalar_prefetch=1,
            grid=(GROUPS, items),
            in_specs=[
                pl.BlockSpec((1, slots, D), early),
                pl.BlockSpec((1, slots, 128), lambda g, i, *_: (i, 0, 0)),
                pl.BlockSpec((1, slots, 128), lambda g, i, *_: (i, 0, 0)),
                *specs,
            ],
            out_specs=[pl.BlockSpec((1, slots, D), early)]
            + [pl.BlockSpec((1, slots, GROUP), cols)] * 4
            + [
                pl.BlockSpec((1, slots, 128), cols),
                pl.BlockSpec((VEC_ROWS, D), fixed),
                weight, weight, weight, weight,
                pl.BlockSpec((D, SMALL), fixed),
            ],
            scratch_shapes=[pltpu.VMEM((items, slots, D), BF)],
        ),
        out_shape=[jax.ShapeDtypeStruct((items, slots, D), BF)] * 5
        + [
            jax.ShapeDtypeStruct((items, slots, 128 * GROUPS), BF),
            jax.ShapeDtypeStruct((VEC_ROWS, D), F32),
        ]
        + [jax.ShapeDtypeStruct((D, D), BF)] * 4
        + [jax.ShapeDtypeStruct((D, SMALL), BF)],
        compiler_params=pltpu.CompilerParams(vmem_limit_bytes=60 * MIB),
        cost_estimate=pl.CostEstimate(
            flops=2 * items * slots * D * 3 * D + 16 * items * HEADS * slots * slots * HEAD,
            bytes_accessed=20 * MIB,
            transcendentals=items * HEADS * slots * slots,
        ),
        name="attention_forward",
    )(scalars, tokens, key_marks, query_marks, *sources)


GELU_SCALE = 0.7978845608028654
GELU_CUBE = 0.044715
STEPS = 4
PARTS = 3


def row_valid(len_ref, start, rows, slots, items):
    index = lax.broadcasted_iota(jnp.int32, (rows, 1), 0) + start
    valid = index < len_ref[0]
    for item in range(1, items):
        valid = valid | ((index >= item * slots) & (index < item * slots + len_ref[item]))
    return jnp.where(valid, 1.0, 0.0).astype(F32)


def middle_forward_kernel(items, slots):
    tile = items * slots // PARTS

    def kernel(
        len_ref, mixed_ref, tok_ref, cot_ref, wout_ref, vec_ref,
        middle_ref, n2_ref, dlow_ref, gbd_ref,
    ):
        part = pl.program_id(0)
        middle = (tok_ref[...].astype(F32) + mm(mixed_ref[...], wout_ref[...])) + vec_ref[4:5, :]
        middle_ref[...] = middle
        scaled, _inverse = norm_parts(middle)
        n2_ref[...] = (scaled * vec_ref[5:6, :] + vec_ref[6:7, :]).astype(BF)
        lower = cot_ref[...].astype(F32) * row_valid(len_ref, part * tile, tile, slots, items)
        dlow_ref[...] = lower.astype(BF)
        sums = jnp.sum(lower, axis=0, keepdims=True)
        gbd_ref[...] = jnp.where(part == 0, 0.0, gbd_ref[...]) + sums

    return kernel


def middle_forward(lengths, mixed, tokens, cotangent, w_all, vec, items, slots):
    row_count = items * slots
    tile = row_count // PARTS
    block = pl.BlockSpec((tile, D), lambda p, *_: (p, 0))
    fixed = lambda p, *_: (0, 0)
    return pl.pallas_call(
        middle_forward_kernel(items, slots),
        grid_spec=pltpu.PrefetchScalarGridSpec(
            num_scalar_prefetch=1,
            grid=(PARTS,),
            in_specs=[
                block, block, block,
                pl.BlockSpec((D, D), fixed),
                pl.BlockSpec((VEC_ROWS, D), fixed),
            ],
            out_specs=[block, block, block, pl.BlockSpec((8, D), fixed)],
        ),
        out_shape=[
            jax.ShapeDtypeStruct((row_count, D), F32),
            jax.ShapeDtypeStruct((row_count, D), BF),
            jax.ShapeDtypeStruct((row_count, D), BF),
            jax.ShapeDtypeStruct((8, D), F32),
        ],
        compiler_params=pltpu.CompilerParams(vmem_limit_bytes=60 * MIB),
        cost_estimate=pl.CostEstimate(
            flops=2 * row_count * D * D, bytes_accessed=14 * MIB, transcendentals=0
        ),
        name="middle_forward",
    )(lengths, mixed, tokens, cotangent, w_all, vec)


def mlp_kernel(stacked, items, slots):
    tile = items * slots // PARTS

    def kernel(
        len_ref, n2, dlow, vec_ref, up_ref, down_ref, act, dn2_ref, gbu_ref, *rest
    ):
        outs = rest[:-5]
        dpre, pre_all, gu, gd, sems = rest[-5:]
        b = pl.program_id(0)
        slot = lax.rem(b, 2)
        go = len_ref[0] > 0

        def send(step, act_on):
            where = lax.rem(step, 2)
            if stacked:
                per, pairs = gu.shape[3], gd.shape[1]
                me = len_ref[items]
                up_rows = pl.ds(pl.multiple_of(per * step, 8), per)
                for n, half in ((1, 1 - me), (2, me)):
                    act_on(
                        pltpu.make_async_copy(
                            gu.at[where, :, half],
                            outs[n].at[:, up_rows, :],
                            sems.at[n, where],
                        )
                    )
                owners = pl.ds(pairs * step, pairs)
                act_on(
                    pltpu.make_async_copy(gd.at[where], outs[0].at[owners], sems.at[0, where])
                )
            else:
                at = pl.ds(pl.multiple_of(D * step, D), D)
                act_on(pltpu.make_async_copy(gu.at[where], outs[0].at[:, at], sems.at[0, where]))
                act_on(pltpu.make_async_copy(gd.at[where], outs[1].at[at, :], sems.at[1, where]))

        @pl.when(b == 0)
        def _():
            dn2_ref[...] = jnp.zeros_like(dn2_ref)

        gbu_ref[...] = jnp.zeros_like(gbu_ref)
        bias = vec_ref[pl.ds(8 + b, 1), :]
        parts = [slice(part * tile, (part + 1) * tile) for part in range(PARTS)]
        for at in parts:

            @pl.when(go)
            def _():
                pre_all[at, :] = mm(n2[at, :], up_ref[...].reshape(D, D)) + bias

        for at in parts:

            @pl.when(go)
            def _():
                pre = pre_all[at, :]
                square = pre * pre
                turned = jnp.tanh(pre * (GELU_SCALE + (GELU_CUBE * GELU_SCALE) * square))
                double = 1.0 + turned
                half = 0.5 * pre
                act[at, :] = (half * double).astype(BF)
                slope = 0.5 * double + half * (1.0 - turned * turned) * (
                    GELU_SCALE + (3.0 * GELU_CUBE * GELU_SCALE) * square
                )
                d_pre = (mm_nt(dlow[at, :], down_ref[...].reshape(D, D)) * slope).astype(BF)
                dpre[at, :] = d_pre
                gbu_ref[0:1, :] += jnp.sum(d_pre.astype(F32), axis=0, keepdims=True)

        for at in parts:

            @pl.when(go)
            def _():
                dn2_ref[at, :] += mm_nt(dpre[at, :], up_ref[...].reshape(D, D))

        @pl.when(b >= 2)
        def _():
            send(b - 2, lambda copy: copy.wait())

        @pl.when(go)
        def _():
            gu[slot] = mm_tn(n2[...], dpre[...]).reshape(gu.shape[1:]).astype(BF)

        @pl.when(go)
        def _():
            gd[slot] = mm_tn(act[...], dlow[...]).reshape(gd.shape[1:]).astype(BF)

        send(b, lambda copy: copy.start())

        @pl.when(b == STEPS - 1)
        def _():
            send(b - 1, lambda copy: copy.wait())
            send(b, lambda copy: copy.wait())

    return kernel


def feed_forward(lengths, normed, d_lower, vec, up, down, stacked, items, slots):
    row_count = items * slots
    once = pl.Buffered(1)
    fixed = lambda b, *_: (0, 0)
    if stacked:
        devices, stack, _ = up.shape
        per = stack // 8
        up_spec = pl.BlockSpec((devices, per, D), lambda b, *_: (0, b, 0))
        down_spec = pl.BlockSpec((devices // 4, 4 * per, D), lambda b, *_: (b, 1, 0))
        grad_shapes = [
            jax.ShapeDtypeStruct((devices // 2, 2, 4 * per, D), BF)
        ] + [jax.ShapeDtypeStruct((devices // 2, 4 * per, D), BF)] * 2
        gu_shape, gd_shape = (devices // 2, 2, per, D), (devices // 8, 2, 4 * per, D)
    else:
        up_spec = pl.BlockSpec((D, D), lambda b, *_: (0, b))
        down_spec = pl.BlockSpec((D, D), lambda b, *_: (b, 0))
        grad_shapes = [
            jax.ShapeDtypeStruct((D, STEPS * D), BF),
            jax.ShapeDtypeStruct((STEPS * D, D), BF),
        ]
        gu_shape = gd_shape = (D, D)
    whole = pl.BlockSpec((row_count, D), fixed, pipeline_mode=once)
    return pl.pallas_call(
        mlp_kernel(stacked, items, slots),
        grid_spec=pltpu.PrefetchScalarGridSpec(
            num_scalar_prefetch=1,
            grid=(STEPS,),
            in_specs=[
                whole, whole,
                pl.BlockSpec((VEC_ROWS, D), fixed),
                up_spec,
                down_spec,
            ],
            out_specs=[
                pl.BlockSpec((row_count, D), lambda b, *_: (0, b)),
                whole,
                pl.BlockSpec((8, D), lambda b, *_: (0, b)),
            ]
            + [pl.BlockSpec(memory_space=pl.ANY)] * len(grad_shapes),
            scratch_shapes=[
                pltpu.VMEM((row_count, D), BF),
                pltpu.VMEM((row_count, D), F32),
                pltpu.VMEM((2,) + gu_shape, BF),
                pltpu.VMEM((2,) + gd_shape, BF),
                pltpu.SemaphoreType.DMA((3, 2)),
            ],
        ),
        out_shape=[
            jax.ShapeDtypeStruct((row_count, STEPS * D), BF),
            jax.ShapeDtypeStruct((row_count, D), F32),
            jax.ShapeDtypeStruct((8, STEPS * D), F32),
        ]
        + grad_shapes,
        compiler_params=pltpu.CompilerParams(vmem_limit_bytes=60 * MIB),
        cost_estimate=pl.CostEstimate(
            flops=2 * row_count * D * D * 20,
            bytes_accessed=36 * MIB,
            transcendentals=row_count * 4 * D,
        ),
        name="feed_forward",
    )(lengths, normed, d_lower, vec, up, down)


def output_kernel(first, items, slots):
    tile = items * slots // PARTS

    def kernel(len_ref, middle_ref, act_ref, down_ref, vec_ref, *refs):
        part = pl.program_id(0) + first
        valid = row_valid(len_ref, part * tile, tile, slots, items)
        down = down_ref[...].reshape(STEPS * D, D)
        whole = middle_ref[...] + (mm(act_ref[...], down) + vec_ref[7:8, :])
        refs[-1][...] = (whole * valid).astype(BF)

    return kernel


def feed_forward_output(first, count, lengths, middle, active, down, vec, stacked, items, slots, so_far, after):
    tile = items * slots // PARTS
    vec, _after = lax.optimization_barrier((vec, after))
    once = pl.Buffered(1)
    if stacked:
        devices, stack, _ = down.shape
        spec = pl.BlockSpec(
            (devices, stack // 2, D), lambda p, *_: (0, 1, 0), pipeline_mode=once
        )
    else:
        spec = pl.BlockSpec((STEPS * D, D), lambda p, *_: (0, 0), pipeline_mode=once)
    block = lambda width: pl.BlockSpec((tile, width), lambda p, *_: (first + p, 0))
    return pl.pallas_call(
        output_kernel(first, items, slots),
        grid_spec=pltpu.PrefetchScalarGridSpec(
            num_scalar_prefetch=1,
            grid=(count,),
            in_specs=[
                block(D), block(STEPS * D), spec,
                pl.BlockSpec((VEC_ROWS, D), lambda p, *_: (0, 0)),
            ]
            + [pl.BlockSpec(memory_space=pl.ANY)] * len(so_far),
            out_specs=block(D),
        ),
        out_shape=jax.ShapeDtypeStruct((items * slots, D), BF),
        input_output_aliases={5: 0} if so_far else {},
        compiler_params=pltpu.CompilerParams(vmem_limit_bytes=60 * MIB),
        cost_estimate=pl.CostEstimate(
            flops=4 * count * items * slots * D * D, bytes_accessed=4 * MIB, transcendentals=0
        ),
        name="feed_forward_output",
    )(lengths, middle, active, down, vec, *so_far)


MIDDLE_PARTS = 5


def middle_kernel(tile, slots, items):
    def kernel(
        len_ref, dn2_ref, middle_ref, cot_ref, mixed_ref, wout_ref, vec_ref,
        dmid_ref, dmix_ref, delta_ref, sums_ref, *rest,
    ):
        gouts, (acc, branch) = rest[:-2], rest[-2:]
        part = pl.program_id(0)
        go = len_ref[0] > 0

        @pl.when(part == 0)
        def _():
            sums_ref[...] = jnp.zeros_like(sums_ref)
            acc[...] = jnp.zeros_like(acc)

        scaled, inverse = norm_parts(middle_ref[...])
        d_n2 = dn2_ref[...]
        valid = row_valid(len_ref, part * tile, tile, slots, items)
        d_middle = cot_ref[...].astype(F32) * valid + norm_back(
            d_n2, scaled, inverse, vec_ref[5:6, :]
        )
        dmid_ref[...] = d_middle
        low = d_middle.astype(BF)
        branch[...] = low
        sums_ref[...] += jnp.concatenate(
            [
                jnp.sum(d_n2 * scaled, axis=0, keepdims=True),
                jnp.sum(d_n2, axis=0, keepdims=True),
                jnp.sum(low.astype(F32), axis=0, keepdims=True),
                jnp.zeros((5, D), F32),
            ],
            axis=0,
        )

        @pl.when(go)
        def _():
            dmix_ref[...] = mm_nt(branch[...], wout_ref[...]).astype(BF)

        @pl.when(go)
        def _():
            acc[...] += mm_tn(mixed_ref[...], branch[...])

        @pl.when(go)
        def _():
            product = dmix_ref[...].astype(F32) * mixed_ref[...].astype(F32)
            row = lax.broadcasted_iota(jnp.int32, (D, 128), 0)
            lane = lax.broadcasted_iota(jnp.int32, (D, 128), 1)
            pick = jnp.where(row // HEAD == lane, 1.0, 0.0).astype(BF)
            delta_ref[...] = in_three(mm(product.astype(BF), pick))

        @pl.when(part == MIDDLE_PARTS - 1)
        def _():
            store_halves(gouts, acc[...], len_ref[items], slice(None))

    return kernel


def middle_backward(scalars, d_n2, middle, cotangent, mixed, w_all, vec, fast, items, slots, devices):
    row_count = items * slots
    tile = row_count // MIDDLE_PARTS
    fixed = lambda p, *_: (0, 0)
    block = pl.BlockSpec((tile, D), lambda p, *_: (p, 0))
    outs = split_shapes(fast, devices, D)
    return pl.pallas_call(
        middle_kernel(tile, slots, items),
        grid_spec=pltpu.PrefetchScalarGridSpec(
            num_scalar_prefetch=1,
            grid=(MIDDLE_PARTS,),
            in_specs=[
                block, block, block, block,
                pl.BlockSpec((D, D), fixed),
                pl.BlockSpec((VEC_ROWS, D), fixed),
            ],
            out_specs=[
                block, block,
                pl.BlockSpec((tile, 128), lambda p, *_: (p, 0)),
                pl.BlockSpec((8, D), fixed),
            ]
            + [whole_block(v) for v in outs],
            scratch_shapes=[pltpu.VMEM((D, D), F32), pltpu.VMEM((tile, D), BF)],
        ),
        out_shape=[
            jax.ShapeDtypeStruct((row_count, D), F32),
            jax.ShapeDtypeStruct((row_count, D), BF),
            jax.ShapeDtypeStruct((row_count, 128), BF),
            jax.ShapeDtypeStruct((8, D), F32),
        ]
        + outs,
        compiler_params=pltpu.CompilerParams(vmem_limit_bytes=60 * MIB),
        cost_estimate=pl.CostEstimate(
            flops=10 * row_count * D * D, bytes_accessed=8 * MIB, transcendentals=0
        ),
        name="middle_backward",
    )(scalars, d_n2, middle, cotangent, mixed, w_all, vec)


def backward_kernel(
    len_ref, q_ref, k_ref, v_ref, dmix_ref, lse_ref, delta_ref, key_ref, query_ref, scaled_ref,
    wq_ref, wk_ref, wv_ref, table_ref, *rest, base, so_far, rows,
):
    given, rest = rest[:so_far], rest[so_far:]
    dqkv_ref, gbias_ref, norm_ref, *gws, acc = rest
    g = pl.program_id(0)
    i = pl.program_id(1)
    items = pl.num_programs(1)
    last_item = items - 1
    slots = q_ref.shape[1]
    go = len_ref[0] > 0
    beside = lambda x, y: jnp.concatenate([x, y], axis=1)
    fronts = []
    for pair in range(PAIRS):
        cols = slice(pair * 128, (pair + 1) * 128)
        queries = two_heads(q_ref[0, :, cols], HEAD ** -0.5)
        upstream = two_heads(dmix_ref[0, :, cols], 1.0)
        heads = (2 * pair, 2 * pair + 1)
        marks = jnp.concatenate(
            [lse_ref[0] * offset_lanes(head) + query_ref[0] for head in heads], axis=0
        )
        offsets = jnp.concatenate(
            [delta_ref[0] * offset_lanes(4 * (base + g) + head) for head in heads], axis=0
        )
        fronts.append(
            (
                queries,
                upstream,
                mm_nt(beside(k_ref[0, :, cols], key_ref[0]), beside(queries, marks)),
                mm_nt(beside(v_ref[0, :, cols], key_ref[0]), beside(upstream, offsets)),
            )
        )
    for pair in range(PAIRS):
        queries, upstream, scores, d_probs = fronts[pair]
        dv = dk = None
        turned = []
        flipped = k_ref[0, :, pair * 128 : (pair + 1) * 128].T
        for half in range(2):
            at = slice(half * slots, (half + 1) * slots)
            probs = jnp.exp(scores[:, at])
            d_scores = (probs * d_probs[:, at]).astype(BF)
            dv_half = mm(probs.astype(BF), upstream[at])
            dk_half = mm(d_scores, queries[at])
            dv = dv_half if dv is None else dv + dv_half
            dk = dk_half if dk is None else dk + dk_half
            turned.append(mm(flipped, d_scores))
        row = lax.broadcasted_iota(jnp.int32, (128, 1), 0)
        dq = jnp.where(row < HEAD, turned[0], turned[1]).T * HEAD ** -0.5
        for which, part in ((0, dq), (1, dk), (2, dv)):
            start = which * GROUP + pair * 128
            dqkv_ref[0, :, start : start + 128] = part.astype(BF)

    @pl.when(go)
    def _():
        bias = jnp.sum(dqkv_ref[0].astype(F32), axis=0, keepdims=True)
        before = jnp.where(i == 0, 0.0, gbias_ref[...])
        gbias_ref[...] = before + bias

    @pl.when(i == 0)
    def _():
        acc[...] = mm_tn(scaled_ref[0], dqkv_ref[0])

    @pl.when(i > 0)
    def _():
        acc[...] += mm_tn(scaled_ref[0], dqkv_ref[0])

    @pl.when(i == last_item)
    def _():
        gain = table_ref[:, 0:1].astype(F32)
        shift = table_ref[:, 1:2].astype(F32)
        lane = lax.broadcasted_iota(jnp.int32, (1, SMALL), 1)
        gains = jnp.zeros((D, 1), F32)
        shifts = jnp.zeros((D, 1), F32)
        for which, ref in ((0, wq_ref), (1, wk_ref), (2, wv_ref)):
            cols = slice(which * GROUP, (which + 1) * GROUP)
            total = acc[:, cols]
            sums = gbias_ref[0:1, cols]
            weight = ref[...].astype(F32)
            store_halves(gws, gain * total + shift * sums, len_ref[items], cols)
            gains = gains + jnp.sum(weight * total, axis=-1, keepdims=True)
            shifts = shifts + jnp.sum(weight * sums, axis=-1, keepdims=True)
        new = jnp.where(lane == 0, gains, jnp.where(lane == 1, shifts, 0.0))
        norm_ref[...] = jnp.where(g == 0, 0.0, norm_ref[...]) + new
        if so_far:
            mid_ref, up_ref, down_ref, *before = given
            norms, lines = norm_ref[...], gbias_ref[0:1, :]
            if before:
                norms = norms + before[0][...]
                lines = jnp.concatenate([before[1][0:1, :], lines], axis=1)
            table = small_table(
                norms, lines, mid_ref[...], up_ref[0:1, :], down_ref[0:1, :], rows
            )
            store_halves(gws, table, len_ref[items], slice(D, D + SMALL))


def attention_backward(
    base, count, scalars, q, k, v, d_mixed, lse, delta, key_marks, query_marks, scaled, weights,
    fast, devices, so_far,
):
    items, slots, _ = q.shape
    rows = lambda g, i, *_: (i, 0, 0)
    block = pl.BlockSpec((1, slots, GROUP), lambda g, i, *_: (i, 0, base + g))
    weight = pl.BlockSpec((D, GROUP), lambda g, i, *_: (0, base + g))
    outs = split_shapes(fast, devices, count * D + (SMALL if so_far else 0))
    kernel = functools.partial(
        backward_kernel, base=base, so_far=len(so_far), rows=D // devices
    )
    return pl.pallas_call(
        kernel,
        grid_spec=pltpu.PrefetchScalarGridSpec(
            num_scalar_prefetch=1,
            grid=(count, items),
            in_specs=[
                block, block, block, block,
                pl.BlockSpec((1, slots, 128), lambda g, i, *_: (i, 0, base + g)),
                pl.BlockSpec((1, slots, 128), rows),
                pl.BlockSpec((1, slots, 128), rows),
                pl.BlockSpec((1, slots, 128), rows),
                pl.BlockSpec((1, slots, D), rows),
                weight, weight, weight,
                pl.BlockSpec((D, SMALL), lambda g, i, *_: (0, 0)),
                *[whole_block(v) for v in so_far],
            ],
            out_specs=[
                pl.BlockSpec((1, slots, D), lambda g, i, *_: (i, 0, g)),
                pl.BlockSpec((8, D), lambda g, i, *_: (0, g)),
                pl.BlockSpec((D, SMALL), lambda g, i, *_: (0, 0)),
            ]
            + [
                pl.BlockSpec(
                    v.shape[:-1] + ((D + SMALL) if so_far else D,),
                    lambda g, i, *_, n=len(v.shape): (0,) * (n - 1) + (g,),
                )
                for v in outs
            ],
            scratch_shapes=[pltpu.VMEM((D, D), F32)],
        ),
        out_shape=[
            jax.ShapeDtypeStruct((items, slots, count * D), BF),
            jax.ShapeDtypeStruct((8, count * D), F32),
            jax.ShapeDtypeStruct((D, SMALL), F32),
        ]
        + outs,
        compiler_params=pltpu.CompilerParams(vmem_limit_bytes=60 * MIB),
        cost_estimate=pl.CostEstimate(
            flops=14 * count * items * slots * D * D,
            bytes_accessed=8 * count * MIB,
            transcendentals=count * items * 4 * slots * slots,
        ),
        name="attention_backward",
    )(
        scalars, q, k, v, d_mixed, lse, delta, key_marks, query_marks, scaled,
        *weights, *so_far,
    )


def input_kernel(*refs):
    parts, (*weights, tok_ref, dmid_ref, vec_ref, grad_ref) = refs[:-7], refs[-7:]
    places = [(ref, n) for ref in parts for n in range(ref.shape[2] // D)]
    total = None
    for g in range(GROUPS):
        for which in range(3):
            weight = weights[which][:, g * GROUP : (g + 1) * GROUP]
            ref, n = places[g]
            start = n * D + which * GROUP
            part = mm_nt(ref[0, :, start : start + GROUP], weight)
            total = part if total is None else total + part
    scaled, inverse = norm_parts(tok_ref[0].astype(F32))
    grad_ref[0] = dmid_ref[0] + norm_back(total, scaled, inverse, vec_ref[0:1, :])


def input_backward(d_qkv, weights, tokens, d_middle, vec, after):
    items, slots, _ = tokens.shape
    vec, _after = lax.optimization_barrier((vec, after))
    rows = lambda i: (i, 0, 0)
    fixed = lambda i: (0, 0)
    block = pl.BlockSpec((1, slots, D), rows)
    return pl.pallas_call(
        input_kernel,
        grid=(items,),
        in_specs=[
            *[pl.BlockSpec((1, slots, part.shape[2]), rows) for part in d_qkv],
            *[pl.BlockSpec((D, D), fixed)] * 3,
            block, block,
            pl.BlockSpec((VEC_ROWS, D), fixed),
        ],
        out_specs=block,
        out_shape=jax.ShapeDtypeStruct((items, slots, D), F32),
        compiler_params=pltpu.CompilerParams(vmem_limit_bytes=60 * MIB),
        cost_estimate=pl.CostEstimate(
            flops=10 * items * slots * D * D, bytes_accessed=8 * MIB, transcendentals=0
        ),
        name="input_backward",
    )(*d_qkv, *weights, tokens, d_middle, vec)


def own_kernel(keep_ref, got_ref, *refs):
    rows = keep_ref.shape[0]
    up = refs[:3] if len(refs) > 10 else ()
    qkv_ref, out_ref, *refs = refs[len(up) :]
    total = keep_ref[...] + got_ref[...].astype(F32)
    for which in range(3):
        for g in range(GROUPS):
            start = g * D + which * GROUP
            qkv_ref[:, which * D + g * GROUP : which * D + (g + 1) * GROUP] = total[
                :, start : start + GROUP
            ]
    out_ref[...] = total[:, 3 * D + SMALL :]
    lines = total[:, 3 * D : 3 * D + SMALL].T
    at = 0
    for ref, (_name, count) in zip(refs, COLUMNS):
        ref[...] = jnp.concatenate([lines[at + j : at + j + 1, :] for j in range(count)], axis=1)
        at += count
    for n, ref in enumerate(up[:2]):
        for half in range(2):
            b = 2 * n + half
            own = ref[half * rows : (half + 1) * rows, :]
            got = up[2][b * rows : (b + 1) * rows, :].astype(F32)
            refs[-1][:, b * D : (b + 1) * D] = own + got


def own_grads(keep, got, *up):
    rows = keep.shape[0]
    shapes = [(rows, 3 * D), (rows, D)] + [(1, count * rows) for _name, count in COLUMNS]
    if up:
        shapes.append((rows, STEPS * D))
    return pl.pallas_call(
        own_kernel,
        out_shape=[jax.ShapeDtypeStruct(shape, F32) for shape in shapes],
        compiler_params=pltpu.CompilerParams(vmem_limit_bytes=16 * MIB),
        name="own_grads",
    )(keep, got, *up)


def swap(x, axis, bit, size):
    return lax.ppermute(x, axis, [(i, i ^ (1 << bit)) for i in range(size)])


def own_bit(axis, bit):
    return (lax.axis_index(axis) >> bit) & 1


def doubled(x, axis, bit, size, at):
    other = jnp.expand_dims(swap(x, axis, bit, size), at)
    mine = jnp.expand_dims(x, at)
    return jnp.where(
        own_bit(axis, bit) == 0,
        jnp.concatenate([mine, other], at),
        jnp.concatenate([other, mine], at),
    )


def gather_rows(x, cut, sizes):
    rows = x.shape[0]
    wide, narrow = sizes
    if sizes != (8, 4):
        whole = lax.all_gather(x, AXES, axis=0, tiled=True)
        return [whole[:, :cut]], [whole[:, cut:]]

    def ordered(mine, other, axis, bit, at):
        mine, other = jnp.expand_dims(mine, at), jnp.expand_dims(other, at)
        return jnp.where(
            own_bit(axis, bit) == 0,
            jnp.concatenate([mine, other], at),
            jnp.concatenate([other, mine], at),
        )

    away = lambda mask: lax.ppermute(x, "wide", [(i, i ^ mask) for i in range(wide)])
    near, far, both = away(2), away(4), away(6)
    x = ordered(ordered(x, near, "wide", 1, 0), ordered(far, both, "wide", 1, 0), "wide", 2, 0)
    a, b = x[..., :cut], x[..., cut:]
    a = doubled(a, "wide", 0, wide, 0)
    b = doubled(b, "narrow", 1, narrow, 0)
    a = doubled(a, "narrow", 1, narrow, 0)
    b = doubled(b, "wide", 0, wide, 0)
    flat = lambda t: t.reshape(wide * narrow // 2, rows, -1)
    return [[flat(t), flat(swap(t, "narrow", 0, narrow))] for t in (a, b)]


def fold_kernel(_bits_ref, *refs):
    keeps, gots, outs = refs[:4], refs[4:8], refs[8:]
    for keep, got, out in zip(keeps, gots, outs):
        out[...] = (keep[...].astype(F32) + got[...].astype(F32)).astype(BF)


def fold(scalars, keep, got, cut, items):
    parts, rows, _ = keep.shape
    quads = parts // 4
    side = lambda bits, n, mine: bits[items + n] if mine else 1 - bits[items + n]
    by_x = lambda mine: pl.BlockSpec(
        (1, 2, 1, cut, D), lambda p, bits: (p, 0, side(bits, 1, mine), 0, 0)
    )
    by_y = lambda mine: pl.BlockSpec(
        (1, 1, 2, cut, D), lambda p, bits: (p, side(bits, 2, mine), 0, 1, 0)
    )
    specs = [by_x(False), by_x(True), by_y(False), by_y(True)]
    shapes = [jax.ShapeDtypeStruct((quads, 2, 1, cut, D), BF)] * 2
    shapes += [jax.ShapeDtypeStruct((quads, 1, 2, cut, D), BF)] * 2
    at = lambda p, *_: (p, 0, 0, 0, 0)
    keep, got = (t.reshape(quads, 2, 2, rows, D) for t in (keep, got))
    return pl.pallas_call(
        fold_kernel,
        grid_spec=pltpu.PrefetchScalarGridSpec(
            num_scalar_prefetch=1,
            grid=(quads,),
            in_specs=specs * 2,
            out_specs=[pl.BlockSpec((1,) + v.shape[1:], at) for v in shapes],
        ),
        out_shape=shapes,
        compiler_params=pltpu.CompilerParams(vmem_limit_bytes=60 * MIB),
        cost_estimate=pl.CostEstimate(flops=1, bytes_accessed=14 * MIB, transcendentals=0),
        name="fold",
    )(scalars, *[keep] * 4, *[got] * 4)


def together(*values):
    return lax.optimization_barrier(values)


def halves(keep, got, axis, bit, at, kind=F32):
    me = own_bit(axis, bit)

    def half(which):
        part = lambda x: lax.dynamic_index_in_dim(x, which, at, keepdims=False).astype(F32)
        return part(keep) if got is None else part(keep) + part(got)

    return half(1 - me).astype(BF), half(me).astype(kind)


def body(sizes):
    def run(
        tokens, lengths, blocks, ln1_gain, ln1_bias, qkv_weight, qv_bias, out_weight, out_bias,
        ln2_gain, ln2_bias, up_weight, up_bias, down_weight, down_bias, cotangent,
    ):
        items, slots, _ = tokens.shape
        row_count = items * slots
        rows = qkv_weight.shape[0]
        devices = sizes[0] * sizes[1]
        stacked = sizes == (8, 4)

        vectors = (
            ln1_gain, ln1_bias, qv_bias, out_bias, ln2_gain, ln2_bias, up_bias, down_bias,
        )
        key_marks, query_marks, first, *rest = pack_parameters(
            lengths, blocks, vectors, qkv_weight, out_weight, up_weight, down_weight, stacked
        )
        if stacked:
            whole = lax.all_gather(rest[0], AXES, axis=0, tiled=True)
            up = down = whole.reshape(devices, 8 * rows, D)
        else:
            up = lax.all_gather(up_weight, AXES, axis=0, tiled=True)
            down = lax.all_gather(down_weight, AXES, axis=0, tiled=True)
        bits = [own_bit("narrow", 0), own_bit("narrow", 1), own_bit("wide", 0)]
        scalars = jnp.concatenate([lengths, jnp.stack(bits).astype(lengths.dtype)])
        first = gather_rows(first, 2 * D, sizes)

        scaled, q, k, v, mixed, lse, vec, w_q, w_k, w_v, w_out, table = attention_forward(
            scalars, tokens, first, key_marks, query_marks, rows
        )
        flat = lambda t: t.reshape(row_count, D)
        cube = lambda t: t.reshape(items, slots, D)
        middle, normed, d_lower, gb_down = middle_forward(
            lengths, flat(mixed), flat(tokens), flat(cotangent), w_out, vec, items, slots
        )
        wide, narrow = sizes
        fast = sizes == (8, 4)
        active, d_n2, gb_up, *ffn = feed_forward(
            scalars, normed, d_lower, vec, up, down, fast, items, slots
        )

        def middle_part():
            return middle_backward(
                scalars, d_n2, middle, flat(cotangent), flat(mixed), w_out, vec, fast, items,
                slots, devices,
            )

        def attention_part(base, count, d_mixed, delta, so_far=()):
            d_qkv, sums, norms, *grads = attention_backward(
                base, count, scalars, q, k, v, cube(d_mixed), lse,
                delta.reshape(items, slots, 128), key_marks, query_marks, scaled,
                (w_q, w_k, w_v, table), fast, devices, so_far,
            )
            return d_qkv, sums, norms, grads

        def input_part(d_qkv, d_middle, after):
            return input_backward(
                d_qkv, (w_q, w_k, w_v), tokens, cube(d_middle), vec, after
            )

        def output_part(after):
            return feed_forward_output(
                0, PARTS, lengths, middle, active, down, vec, fast, items, slots, (), after
            )

        def rest_of_backward():
            core = ("narrow", 0, narrow)
            x_link, y_link = ("narrow", 1), ("wide", 0)
            z_near, z_far = ("wide", 1), ("wide", 2)
            size = {"wide": wide, "narrow": narrow}
            move = lambda value, link: swap(value, *link, size[link[0]])
            beside = lambda *parts: jnp.concatenate(parts, axis=-1)
            cut = 2 * rows

            up_got = swap(ffn[1], *core)
            d_middle, d_mixed, delta, mid_sums, *g_out = middle_part()
            up_got, d_mixed, *g_out = together(up_got, d_mixed, *g_out)
            out_got = swap(g_out[0], *core)
            c_send, c_keep, d_send, d_keep = fold(scalars, ffn[2], up_got, cut, items)
            c_send, d_send, d_mixed = together(c_send, d_send, d_mixed)
            c_got, d_got = move(c_send, x_link), move(d_send, y_link)
            d_qkv, sums, norms, grads = attention_part(0, 2, d_mixed, delta)
            c_got, d_got, out_got, c_keep, d_keep, d_mixed, grads[0], norms = together(
                c_got, d_got, out_got, c_keep, d_keep, d_mixed, grads[0], norms
            )
            shaped = lambda t: t.reshape((2, 2, 2, cut, D))
            c_send, c_keep = halves(shaped(c_keep), shaped(c_got), *y_link, 2, BF)
            d_send, d_keep = halves(shaped(d_keep), shaped(d_got), *x_link, 2, BF)
            c_send, d_send, c_keep, d_keep, d_mixed, out_got = together(
                c_send, d_send, c_keep, d_keep, d_mixed, out_got
            )
            c_got, d_got = move(c_send, y_link), move(d_send, x_link)
            a_got = swap(grads[0], *core)
            d_qkv_2, _sums, _norms, grads_2 = attention_part(
                2, 1, d_mixed, delta, (mid_sums, gb_up, gb_down, norms, sums)
            )
            c_got, d_got, a_got, c_keep, d_keep, out_got, grads_2[0] = together(
                c_got, d_got, a_got, c_keep, d_keep, out_got, grads_2[0]
            )

            shaped = lambda t: t.reshape((2, 2, 2, 2, rows, -1))
            b_got = swap(grads_2[0], *core)
            c_send, c_keep = halves(c_keep, c_got, *z_near, 1)
            d_send, d_keep = halves(d_keep, d_got, *z_near, 1)
            send = jnp.concatenate([c_send, d_send], axis=-2)
            up_got = move(send, z_near)
            a_send, a_keep = halves(shaped(grads[1]), shaped(a_got), *x_link, 3)
            out_send, out_keep = halves(shaped(g_out[1]), shaped(out_got), *y_link, 2)
            b_got, a_send, out_send, send = together(b_got, a_send, out_send, send)
            b_send, b_keep = halves(
                shaped(grads_2[1]), shaped(b_got), *y_link, 2
            )
            b_send, b_keep = beside(b_send, out_send), beside(b_keep, out_keep)
            a_send, b_send = together(a_send, b_send)
            a_got, b_got = move(a_send, x_link), move(b_send, y_link)
            input_grad = input_part([d_qkv, d_qkv_2], d_middle, (a_send, b_send))
            a_got, b_got, up_got, input_grad = together(a_got, b_got, up_got, input_grad)
            a_send, a_keep = halves(a_keep, a_got, *y_link, 2)
            b_send, b_keep = halves(b_keep, b_got, *x_link, 2)
            c_send, c_keep = halves(c_keep, up_got[:, :cut], *z_far, 0)
            d_send, d_keep = halves(d_keep, up_got[:, cut:], *z_far, 0)
            send = jnp.concatenate([c_send, d_send], axis=-2)
            a_send, b_send, send = together(a_send, b_send, send)
            a_got, b_got = move(a_send, y_link), move(b_send, x_link)
            up_got = move(send, z_far)
            output = output_part((a_send, b_send))
            a_got, b_got, up_got, output = together(a_got, b_got, up_got, output)
            send, keep = halves(beside(a_keep, b_keep), beside(a_got, b_got), *z_near, 1)
            got = move(send, z_near)
            send, keep = halves(keep, got, *z_far, 0)
            got = move(send, z_far)
            return [input_grad, output, *own_grads(keep, got, c_keep, d_keep, up_got)]

        if not fast:
            scatter = lambda x: lax.psum_scatter(
                x.astype(F32), AXES, scatter_dimension=0, tiled=True
            )
            grad_up, grad_down = scatter(ffn[0]), scatter(ffn[1])
            d_middle, d_mixed, delta, mid_sums, *g_out = middle_part()
            d_qkv, sums, norms, grads = attention_part(0, 2, d_mixed, delta)
            d_qkv_2, _sums, _norms, grads_2 = attention_part(
                2, 1, d_mixed, delta, (mid_sums, gb_up, gb_down, norms, sums)
            )
            input_grad = input_part([d_qkv, d_qkv_2], d_middle, ())
            output = output_part(())
            keep = scatter(jnp.concatenate([grads[0], grads_2[0], g_out[0]], axis=1))
            own_qkv, own_out, *own_small = own_grads(keep, jnp.zeros(keep.shape, BF))
        else:
            grad_down = lax.psum_scatter(
                ffn[0].reshape(STEPS * D, D), AXES, scatter_dimension=0, tiled=True
            ).astype(F32)
            shapes = jax.eval_shape(rest_of_backward)
            input_grad, output, own_qkv, own_out, *own_small, grad_up = lax.cond(
                scalars[0] > 0,
                rest_of_backward,
                lambda: [jnp.zeros(v.shape, v.dtype) for v in shapes],
            )
        ln1_g, ln1_b, qv_b, out_b, ln2_g, ln2_b, up_b, down_b = [v.reshape(-1) for v in own_small]
        return (
            cube(output), input_grad, ln1_g, ln1_b, own_qkv, qv_b, own_out, out_b, ln2_g, ln2_b,
            grad_up, up_b, grad_down, down_b,
        )

    return run


def solution(mesh):
    sizes = (mesh.shape["wide"], mesh.shape["narrow"])
    one = P(AXES)
    two = P(AXES, None)
    three = P(AXES, None, None)
    return jax.shard_map(
        body(sizes),
        mesh=mesh,
        in_specs=(
            three, one, two, one, one, two, one, two, one, one, one, two, one, two, one, three,
        ),
        out_specs=(
            three, three, one, one, two, one, two, one, one, one, two, one, two, one,
        ),
        check_vma=False,
    )
```

```python
import functools

import jax
import jax.numpy as jnp
from jax import lax
from jax.experimental import pallas as pl
from jax.experimental.pallas import tpu as pltpu
from jax.sharding import PartitionSpec as P

D = 768
HEADS = 12
HEAD = 64
GROUP = 256
GROUPS = D // GROUP
PAIRS = GROUP // 128
EPS = 1e-05
MASKED = -1e30
AXES = ("wide", "narrow")
BF = jnp.bfloat16
F32 = jnp.float32
MIB = 1 << 20
VEC_ROWS = 16
SMALL = 128
BLOCKS = 5


def mm(a, b):
    return jnp.dot(a, b, preferred_element_type=F32)


def mm_nt(a, b):
    return lax.dot_general(a, b, (((1,), (1,)), ((), ())), preferred_element_type=F32)


def mm_tn(a, b):
    return lax.dot_general(a, b, (((0,), (0,)), ((), ())), preferred_element_type=F32)


def norm_parts(x):
    centred = x - jnp.mean(x, axis=-1, keepdims=True)
    inverse = lax.rsqrt(jnp.mean(centred * centred, axis=-1, keepdims=True) + EPS)
    return centred * inverse, inverse


def norm_back(d_normed, scaled, inverse, gain):
    h = d_normed * gain
    return inverse * (
        h
        - jnp.mean(h, axis=-1, keepdims=True)
        - scaled * jnp.mean(h * scaled, axis=-1, keepdims=True)
    )


def lane_mask(half, value):
    lane = lax.broadcasted_iota(jnp.int32, (1, 128), 1)
    return jnp.where((lane // HEAD) == half, value, 0.0).astype(BF)


MARK = 64


def in_three(value):
    high = value.astype(BF).astype(F32)
    middle = (value - high).astype(BF).astype(F32)
    low = value - high - middle
    return -(high + pltpu.roll(middle, 16, 1) + pltpu.roll(low, 32, 1)).astype(BF)


def offset_lanes(head):
    lane = lax.broadcasted_iota(jnp.int32, (1, 128), 1)
    return jnp.where((lane < 48) & (lane % 16 == head), 1.0, 0.0).astype(BF)


COLUMNS = (("ln1_gain", 1), ("ln1_bias", 1), ("qv_bias", 2), ("out_bias", 1), ("ln2_gain", 1), ("ln2_bias", 1), ("up_bias", 4), ("down_bias", 1))


def store_halves(refs, value, me, cols):
    if len(refs) == 1:
        refs[0][:, cols] = value.astype(BF)
        return
    pairs, rows, _ = refs[0].shape
    value = value.reshape(pairs, 2, rows, value.shape[1])
    even, odd = value[:, 0], value[:, 1]
    refs[0][:, :, cols] = jnp.where(me == 0, odd, even).astype(BF)
    refs[1][:, :, cols] = jnp.where(me == 0, even, odd).astype(BF)


def split_shapes(fast, devices, columns):
    if not fast:
        return [jax.ShapeDtypeStruct((D, columns), BF)]
    return [jax.ShapeDtypeStruct((devices // 2, D // devices, columns), BF)] * 2


def whole_block(value):
    return pl.BlockSpec(value.shape, lambda *_: (0,) * len(value.shape))


def pack_kernel(stacked):
    def kernel(*refs):
        vectors, (qkv_ref, out_ref, up_ref, down_ref, first_ref) = refs[:8], refs[8:13]
        rows = qkv_ref.shape[0]
        lines = []
        for ref, (_name, count) in zip(vectors, COLUMNS):
            line = ref[...].astype(F32)
            lines += [line[:, j * rows : (j + 1) * rows] for j in range(count)]
        table = jnp.concatenate(lines + [jnp.zeros((SMALL - len(lines), rows), F32)], axis=0)
        first_ref[:, : 3 * D] = qkv_ref[...]
        first_ref[:, 3 * D : 4 * D] = out_ref[...]
        first_ref[:, 4 * D :] = table.T.astype(BF)
        if stacked:
            rest_ref = refs[13]
            for b in range(4):
                rest_ref[b * rows : (b + 1) * rows, :] = up_ref[:, b * D : (b + 1) * D]
            rest_ref[4 * rows :, :] = down_ref[...]

    return kernel


def marks_kernel(len_ref, blocks_ref, key_ref, query_ref):
    for i in range(blocks_ref.shape[0]):
        line = blocks_ref[i : i + 1, :].astype(F32)
        block = jnp.broadcast_to(line, (128, line.shape[1])).T
        slot = lax.broadcasted_iota(jnp.int32, block.shape, 0)
        lane = lax.broadcasted_iota(jnp.int32, block.shape, 1)
        mark = (lane - MARK).astype(F32)
        own = jnp.where(slot < len_ref[i], block, float(BLOCKS))
        key_ref[i] = jnp.where((lane < 48) | (mark == own), 1.0, 0.0).astype(BF)
        barred = (mark > block) & (mark <= BLOCKS)
        query_ref[i] = jnp.where(barred, MASKED, 0.0).astype(BF)


def mask_marks(lengths, blocks):
    items, slots = blocks.shape
    shapes = [jax.ShapeDtypeStruct((items, slots, 128), BF)] * 2
    return pl.pallas_call(
        marks_kernel,
        grid_spec=pltpu.PrefetchScalarGridSpec(
            num_scalar_prefetch=1,
            grid=(1,),
            in_specs=[whole_block(blocks)],
            out_specs=[whole_block(v) for v in shapes],
        ),
        out_shape=shapes,
        compiler_params=pltpu.CompilerParams(vmem_limit_bytes=60 * MIB),
        cost_estimate=pl.CostEstimate(flops=1, bytes_accessed=MIB, transcendentals=0),
        name="mask_marks",
    )(lengths, blocks)


def pack_parameters(vectors, qkv, out, up, down, stacked):
    rows = qkv.shape[0]
    shapes = [jax.ShapeDtypeStruct((rows, 4 * D + SMALL), BF)]
    if stacked:
        shapes.append(jax.ShapeDtypeStruct((8 * rows, D), BF))
    values = [v.reshape(1, -1) for v in vectors] + [qkv, out, up, down]
    return pl.pallas_call(
        pack_kernel(stacked),
        grid=(1,),
        in_specs=[whole_block(v) for v in values],
        out_specs=[whole_block(v) for v in shapes],
        out_shape=shapes,
        compiler_params=pltpu.CompilerParams(vmem_limit_bytes=60 * MIB),
        name="pack_parameters",
    )(*values)


def from_table(lines, count, rows, start, pick_rows):
    lane = lax.broadcasted_iota(jnp.int32, (1, D), 1) + start
    first = start // count // 128 * 128
    place = lax.broadcasted_iota(jnp.int32, (pick_rows, D), 0) + first
    at = lax.broadcasted_iota(jnp.int32, (pick_rows, D), 1) + start
    pick = (place == rows * (at // (count * rows)) + at % rows).astype(F32).astype(BF)
    lines = mm(lines[:, first : first + pick_rows].astype(BF), pick)
    which = lane % (count * rows) // rows
    line = lines[0:1, :]
    for j in range(1, count):
        line = jnp.where(which == j, lines[j : j + 1, :], line)
    return line


def unpack(table, vec_ref, rows):
    lines = table.astype(F32).T
    vec_ref[0:2, :] = lines[0:2, :]
    vec_ref[2:3, :] = from_table(lines[2:4, :], 2, rows, 0, D // 2)
    vec_ref[3:4, :] = from_table(lines[2:4, :], 2, rows, D, D // 2)
    vec_ref[4:7, :] = lines[4:7, :]
    vec_ref[7:8, :] = lines[11:12, :]
    for b in range(4):
        vec_ref[8 + b : 9 + b, :] = from_table(lines[7:11, :], 4, rows, b * D, 256)
    vec_ref[12:16, :] = jnp.zeros((4, D), F32)


def to_table(line, count, rows, start, pick_rows, column):
    row = lax.broadcasted_iota(jnp.int32, (SMALL, D), 0)
    at = lax.broadcasted_iota(jnp.int32, (SMALL, D), 1) + start
    spread = jnp.where(row - column == at % (count * rows) // rows, line, 0.0).astype(BF)
    place = lax.broadcasted_iota(jnp.int32, (pick_rows, D), 0) + start // count
    lane = lax.broadcasted_iota(jnp.int32, (pick_rows, D), 1) + start
    pick = (place == rows * (lane // (count * rows)) + lane % rows).astype(F32).astype(BF)
    return mm_nt(pick, spread)


def small_table(norms, lines, mid_sums, up_sums, down_sums, rows):
    row = lax.broadcasted_iota(jnp.int32, (SMALL, D), 0)
    plain = jnp.zeros((SMALL, D), F32)
    for at, line in (
        (4, mid_sums[2:3, :]), (5, mid_sums[0:1, :]), (6, mid_sums[1:2, :]), (11, down_sums),
    ):
        plain = jnp.where(row == at, line, plain)
    halves = []
    for part, which in enumerate((0, 2)):
        line = jnp.concatenate(
            [
                lines[:, g * D + which * GROUP : g * D + (which + 1) * GROUP]
                for g in range(GROUPS)
            ],
            axis=1,
        )
        halves.append(to_table(line, 2, rows, part * D, D // 2, 2))
    quarters = [
        to_table(up_sums[:, b * D : (b + 1) * D], 4, rows, b * D, D // 4, 7) for b in range(4)
    ]
    return (
        plain.T + norms + jnp.concatenate(halves, axis=0) + jnp.concatenate(quarters, axis=0)
    )


def two_heads(x, value):
    return jnp.concatenate([x * lane_mask(0, value), x * lane_mask(1, value)], axis=0)


def whole_rows(refs, me, x_first):
    if len(refs) == 1:
        return refs[0][...]
    mine, other = refs[0][...].astype(F32), refs[1][...].astype(F32)
    even = jnp.where(me == 0, mine, other)
    odd = jnp.where(me == 0, other, mine)
    pieces = []
    for owner in range(even.shape[0]):
        zz, y, x = owner // 4, owner // 2 % 2, owner % 2
        at = (8 * x + 4 * y if x_first else 8 * y + 4 * x) + zz
        pieces += [even[at], odd[at]]
    return jnp.concatenate(pieces, axis=0).astype(BF)


def forward_kernel(len_ref, tok_ref, key_ref, query_ref, *refs, rows, items, parts):
    weights, refs = refs[: 5 * parts], refs[5 * parts :]
    scaled_ref, q_ref, k_ref, v_ref, mixed_ref, lse_ref, vec_ref, *whole, n1 = refs
    wq_ref, wk_ref, wv_ref, wout_ref, table_ref = whole
    g = pl.program_id(0)
    i = pl.program_id(1)
    slots = tok_ref.shape[1]
    go = len_ref[0] > 0
    own = pl.ds(pl.multiple_of(g * GROUP, GROUP), GROUP)

    @pl.when(i == 0)
    def _():
        for n, ref in enumerate((wq_ref, wk_ref, wv_ref, wout_ref)):
            ref[...] = whole_rows(weights[n * parts : (n + 1) * parts], len_ref[items], n < 2)

    @pl.when((g == 0) & (i == 0))
    def _():
        table_ref[...] = whole_rows(weights[4 * parts :], len_ref[items], False)
        unpack(table_ref[...], vec_ref, rows)

    @pl.when(g == 0)
    def _():
        scaled, _inverse = norm_parts(tok_ref[0].astype(F32))
        scaled_ref[0] = scaled.astype(BF)
        n1[i] = (scaled * vec_ref[0:1, :] + vec_ref[1:2, :]).astype(BF)

    @pl.when(go)
    def _():
        q_ref[0] = (mm(n1[i], wq_ref[...]) + vec_ref[2:3, own]).astype(BF)

    @pl.when(go)
    def _():
        k_ref[0] = mm(n1[i], wk_ref[...]).astype(BF)

    @pl.when(go)
    def _():
        v_ref[0] = (mm(n1[i], wv_ref[...]) + vec_ref[3:4, own]).astype(BF)

    lane = lax.broadcasted_iota(jnp.int32, (1, 128), 1)
    ones = jnp.ones((slots, 128), BF)
    marks = jnp.concatenate([query_ref[0], query_ref[0]], axis=0)

    def scores_of(pair):
        cols = slice(pair * 128, (pair + 1) * 128)
        queries = two_heads(q_ref[0, :, cols], HEAD ** -0.5)
        return mm_nt(
            jnp.concatenate([queries, marks], axis=1),
            jnp.concatenate([k_ref[0, :, cols], key_ref[0]], axis=1),
        )

    def exponents_of(scores):
        parts, peaks = [], []
        for half in range(2):
            own = scores[half * slots : (half + 1) * slots]
            peak = jnp.max(own, axis=-1, keepdims=True)
            parts.append(jnp.exp(own - peak).astype(BF))
            peaks.append(peak)
        return jnp.concatenate(parts, axis=0), peaks

    def finish(pair, exponents, peaks, lse_lanes):
        cols = slice(pair * 128, (pair + 1) * 128)
        both = mm(exponents, jnp.concatenate([v_ref[0, :, cols], ones], axis=1))
        first, second = both[:slots], both[slots:]
        total = jnp.where(lane < HEAD, first[:, 128:], second[:, 128:])
        values = jnp.where(lane < HEAD, first[:, :128], second[:, :128])
        mixed_ref[0, :, cols] = (values * (1.0 / total)).astype(BF)
        for half, part in ((0, first), (1, second)):
            lse = peaks[half] + jnp.log(part[:, 128:])
            lse_lanes = jnp.where(lane == 2 * pair + half, lse, lse_lanes)
        return lse_lanes

    lse_lanes = jnp.zeros((slots, 128), F32)
    tables = [scores_of(pair) for pair in range(PAIRS)]
    for pair in range(PAIRS):
        exponents, peaks = exponents_of(tables[pair])
        lse_lanes = finish(pair, exponents, peaks, lse_lanes)
    lse_ref[0] = in_three(lse_lanes)


def attention_forward(scalars, tokens, first, key_marks, query_marks, rows):
    items, slots, _ = tokens.shape
    early = lambda g, i, *_: (jnp.where(g == 0, i, items - 1), 0, 0)
    cols = lambda g, i, *_: (i, 0, g)
    fixed = lambda g, i, *_: (0, 0)

    parts = len(first[0])

    def given(width, index):
        if parts == 1:
            return [pl.BlockSpec((D, width), lambda g, i, *_: (0, index(g)))]
        shape = (first[0][0].shape[0], rows, width)
        return [pl.BlockSpec(shape, lambda g, i, *_: (0, 0, index(g)))] * parts

    specs = []
    for n in range(4):
        specs += given(GROUP, lambda g, n=n: n % 2 * GROUPS + g)
    specs += given(SMALL, lambda g: 2 * D // SMALL)
    sources = [*first[0] * 2, *first[1] * 3]
    weight = pl.BlockSpec((D, GROUP), lambda g, i, *_: (0, g))
    return pl.pallas_call(
        functools.partial(forward_kernel, rows=rows, items=items, parts=parts),
        grid_spec=pltpu.PrefetchScalarGridSpec(
            num_scalar_prefetch=1,
            grid=(GROUPS, items),
            in_specs=[
                pl.BlockSpec((1, slots, D), early),
                pl.BlockSpec((1, slots, 128), lambda g, i, *_: (i, 0, 0)),
                pl.BlockSpec((1, slots, 128), lambda g, i, *_: (i, 0, 0)),
                *specs,
            ],
            out_specs=[pl.BlockSpec((1, slots, D), early)]
            + [pl.BlockSpec((1, slots, GROUP), cols)] * 4
            + [
                pl.BlockSpec((1, slots, 128), cols),
                pl.BlockSpec((VEC_ROWS, D), fixed),
                weight, weight, weight, weight,
                pl.BlockSpec((D, SMALL), fixed),
            ],
            scratch_shapes=[pltpu.VMEM((items, slots, D), BF)],
        ),
        out_shape=[jax.ShapeDtypeStruct((items, slots, D), BF)] * 5
        + [
            jax.ShapeDtypeStruct((items, slots, 128 * GROUPS), BF),
            jax.ShapeDtypeStruct((VEC_ROWS, D), F32),
        ]
        + [jax.ShapeDtypeStruct((D, D), BF)] * 4
        + [jax.ShapeDtypeStruct((D, SMALL), BF)],
        compiler_params=pltpu.CompilerParams(vmem_limit_bytes=60 * MIB),
        cost_estimate=pl.CostEstimate(
            flops=2 * items * slots * D * 3 * D + 16 * items * HEADS * slots * slots * HEAD,
            bytes_accessed=20 * MIB,
            transcendentals=items * HEADS * slots * slots,
        ),
        name="attention_forward",
    )(scalars, tokens, key_marks, query_marks, *sources)


GELU_SCALE = 0.7978845608028654
GELU_CUBE = 0.044715
STEPS = 4
PARTS = 3


def row_valid(len_ref, start, rows, slots, items):
    index = lax.broadcasted_iota(jnp.int32, (rows, 1), 0) + start
    valid = index < len_ref[0]
    for item in range(1, items):
        valid = valid | ((index >= item * slots) & (index < item * slots + len_ref[item]))
    return jnp.where(valid, 1.0, 0.0).astype(F32)


def middle_forward_kernel(items, slots):
    tile = items * slots // PARTS

    def kernel(
        len_ref, mixed_ref, tok_ref, cot_ref, wout_ref, vec_ref,
        middle_ref, n2_ref, dlow_ref, gbd_ref,
    ):
        part = pl.program_id(0)
        middle = (tok_ref[...].astype(F32) + mm(mixed_ref[...], wout_ref[...])) + vec_ref[4:5, :]
        middle_ref[...] = middle
        scaled, _inverse = norm_parts(middle)
        n2_ref[...] = (scaled * vec_ref[5:6, :] + vec_ref[6:7, :]).astype(BF)
        lower = cot_ref[...].astype(F32) * row_valid(len_ref, part * tile, tile, slots, items)
        dlow_ref[...] = lower.astype(BF)
        sums = jnp.sum(lower, axis=0, keepdims=True)
        gbd_ref[...] = jnp.where(part == 0, 0.0, gbd_ref[...]) + sums

    return kernel


def middle_forward(lengths, mixed, tokens, cotangent, w_all, vec, items, slots):
    row_count = items * slots
    tile = row_count // PARTS
    block = pl.BlockSpec((tile, D), lambda p, *_: (p, 0))
    fixed = lambda p, *_: (0, 0)
    return pl.pallas_call(
        middle_forward_kernel(items, slots),
        grid_spec=pltpu.PrefetchScalarGridSpec(
            num_scalar_prefetch=1,
            grid=(PARTS,),
            in_specs=[
                block, block, block,
                pl.BlockSpec((D, D), fixed),
                pl.BlockSpec((VEC_ROWS, D), fixed),
            ],
            out_specs=[block, block, block, pl.BlockSpec((8, D), fixed)],
        ),
        out_shape=[
            jax.ShapeDtypeStruct((row_count, D), F32),
            jax.ShapeDtypeStruct((row_count, D), BF),
            jax.ShapeDtypeStruct((row_count, D), BF),
            jax.ShapeDtypeStruct((8, D), F32),
        ],
        compiler_params=pltpu.CompilerParams(vmem_limit_bytes=60 * MIB),
        cost_estimate=pl.CostEstimate(
            flops=2 * row_count * D * D, bytes_accessed=14 * MIB, transcendentals=0
        ),
        name="middle_forward",
    )(lengths, mixed, tokens, cotangent, w_all, vec)


def mlp_kernel(stacked, items, slots):
    tile = items * slots // PARTS

    def kernel(
        len_ref, n2, dlow, vec_ref, up_ref, down_ref, act, dn2_ref, gbu_ref, *rest
    ):
        outs = rest[:-5]
        dpre, pre_all, gu, gd, sems = rest[-5:]
        b = pl.program_id(0)
        slot = lax.rem(b, 2)
        go = len_ref[0] > 0

        def send(step, act_on):
            where = lax.rem(step, 2)
            if stacked:
                per, pairs = gu.shape[3], gd.shape[1]
                me = len_ref[items]
                up_rows = pl.ds(pl.multiple_of(per * step, 8), per)
                for n, half in ((1, 1 - me), (2, me)):
                    act_on(
                        pltpu.make_async_copy(
                            gu.at[where, :, half],
                            outs[n].at[:, up_rows, :],
                            sems.at[n, where],
                        )
                    )
                owners = pl.ds(pairs * step, pairs)
                act_on(
                    pltpu.make_async_copy(gd.at[where], outs[0].at[owners], sems.at[0, where])
                )
            else:
                at = pl.ds(pl.multiple_of(D * step, D), D)
                act_on(pltpu.make_async_copy(gu.at[where], outs[0].at[:, at], sems.at[0, where]))
                act_on(pltpu.make_async_copy(gd.at[where], outs[1].at[at, :], sems.at[1, where]))

        @pl.when(b == 0)
        def _():
            dn2_ref[...] = jnp.zeros_like(dn2_ref)

        gbu_ref[...] = jnp.zeros_like(gbu_ref)
        bias = vec_ref[pl.ds(8 + b, 1), :]
        parts = [slice(part * tile, (part + 1) * tile) for part in range(PARTS)]
        for at in parts:

            @pl.when(go)
            def _():
                pre_all[at, :] = mm(n2[at, :], up_ref[...].reshape(D, D)) + bias

        for at in parts:

            @pl.when(go)
            def _():
                pre = pre_all[at, :]
                square = pre * pre
                turned = jnp.tanh(pre * (GELU_SCALE + (GELU_CUBE * GELU_SCALE) * square))
                double = 1.0 + turned
                half = 0.5 * pre
                act[at, :] = (half * double).astype(BF)
                slope = 0.5 * double + half * (1.0 - turned * turned) * (
                    GELU_SCALE + (3.0 * GELU_CUBE * GELU_SCALE) * square
                )
                d_pre = (mm_nt(dlow[at, :], down_ref[...].reshape(D, D)) * slope).astype(BF)
                dpre[at, :] = d_pre
                gbu_ref[0:1, :] += jnp.sum(d_pre.astype(F32), axis=0, keepdims=True)

        for at in parts:

            @pl.when(go)
            def _():
                dn2_ref[at, :] += mm_nt(dpre[at, :], up_ref[...].reshape(D, D))

        @pl.when(b >= 2)
        def _():
            send(b - 2, lambda copy: copy.wait())

        @pl.when(go)
        def _():
            gu[slot] = mm_tn(n2[...], dpre[...]).reshape(gu.shape[1:]).astype(BF)

        @pl.when(go)
        def _():
            gd[slot] = mm_tn(act[...], dlow[...]).reshape(gd.shape[1:]).astype(BF)

        send(b, lambda copy: copy.start())

        @pl.when(b == STEPS - 1)
        def _():
            send(b - 1, lambda copy: copy.wait())
            send(b, lambda copy: copy.wait())

    return kernel


def feed_forward(lengths, normed, d_lower, vec, up, down, stacked, items, slots):
    row_count = items * slots
    once = pl.Buffered(1)
    fixed = lambda b, *_: (0, 0)
    if stacked:
        devices, stack, _ = up.shape
        per = stack // 8
        up_spec = pl.BlockSpec((devices, per, D), lambda b, *_: (0, b, 0))
        down_spec = pl.BlockSpec((devices // 4, 4 * per, D), lambda b, *_: (b, 1, 0))
        grad_shapes = [
            jax.ShapeDtypeStruct((devices // 2, 2, 4 * per, D), BF)
        ] + [jax.ShapeDtypeStruct((devices // 2, 4 * per, D), BF)] * 2
        gu_shape, gd_shape = (devices // 2, 2, per, D), (devices // 8, 2, 4 * per, D)
    else:
        up_spec = pl.BlockSpec((D, D), lambda b, *_: (0, b))
        down_spec = pl.BlockSpec((D, D), lambda b, *_: (b, 0))
        grad_shapes = [
            jax.ShapeDtypeStruct((D, STEPS * D), BF),
            jax.ShapeDtypeStruct((STEPS * D, D), BF),
        ]
        gu_shape = gd_shape = (D, D)
    whole = pl.BlockSpec((row_count, D), fixed, pipeline_mode=once)
    return pl.pallas_call(
        mlp_kernel(stacked, items, slots),
        grid_spec=pltpu.PrefetchScalarGridSpec(
            num_scalar_prefetch=1,
            grid=(STEPS,),
            in_specs=[
                whole, whole,
                pl.BlockSpec((VEC_ROWS, D), fixed),
                up_spec,
                down_spec,
            ],
            out_specs=[
                pl.BlockSpec((row_count, D), lambda b, *_: (0, b)),
                whole,
                pl.BlockSpec((8, D), lambda b, *_: (0, b)),
            ]
            + [pl.BlockSpec(memory_space=pl.ANY)] * len(grad_shapes),
            scratch_shapes=[
                pltpu.VMEM((row_count, D), BF),
                pltpu.VMEM((row_count, D), F32),
                pltpu.VMEM((2,) + gu_shape, BF),
                pltpu.VMEM((2,) + gd_shape, BF),
                pltpu.SemaphoreType.DMA((3, 2)),
            ],
        ),
        out_shape=[
            jax.ShapeDtypeStruct((row_count, STEPS * D), BF),
            jax.ShapeDtypeStruct((row_count, D), F32),
            jax.ShapeDtypeStruct((8, STEPS * D), F32),
        ]
        + grad_shapes,
        compiler_params=pltpu.CompilerParams(vmem_limit_bytes=60 * MIB),
        cost_estimate=pl.CostEstimate(
            flops=2 * row_count * D * D * 20,
            bytes_accessed=36 * MIB,
            transcendentals=row_count * 4 * D,
        ),
        name="feed_forward",
    )(lengths, normed, d_lower, vec, up, down)


def output_kernel(first, items, slots):
    tile = items * slots // PARTS

    def kernel(len_ref, middle_ref, act_ref, down_ref, vec_ref, *refs):
        part = pl.program_id(0) + first
        valid = row_valid(len_ref, part * tile, tile, slots, items)
        down = down_ref[...].reshape(STEPS * D, D)
        whole = middle_ref[...] + (mm(act_ref[...], down) + vec_ref[7:8, :])
        refs[-1][...] = (whole * valid).astype(BF)

    return kernel


def feed_forward_output(first, count, lengths, middle, active, down, vec, stacked, items, slots, so_far, after):
    tile = items * slots // PARTS
    vec, _after = lax.optimization_barrier((vec, after))
    once = pl.Buffered(1)
    if stacked:
        devices, stack, _ = down.shape
        spec = pl.BlockSpec(
            (devices, stack // 2, D), lambda p, *_: (0, 1, 0), pipeline_mode=once
        )
    else:
        spec = pl.BlockSpec((STEPS * D, D), lambda p, *_: (0, 0), pipeline_mode=once)
    block = lambda width: pl.BlockSpec((tile, width), lambda p, *_: (first + p, 0))
    return pl.pallas_call(
        output_kernel(first, items, slots),
        grid_spec=pltpu.PrefetchScalarGridSpec(
            num_scalar_prefetch=1,
            grid=(count,),
            in_specs=[
                block(D), block(STEPS * D), spec,
                pl.BlockSpec((VEC_ROWS, D), lambda p, *_: (0, 0)),
            ]
            + [pl.BlockSpec(memory_space=pl.ANY)] * len(so_far),
            out_specs=block(D),
        ),
        out_shape=jax.ShapeDtypeStruct((items * slots, D), BF),
        input_output_aliases={5: 0} if so_far else {},
        compiler_params=pltpu.CompilerParams(vmem_limit_bytes=60 * MIB),
        cost_estimate=pl.CostEstimate(
            flops=4 * count * items * slots * D * D, bytes_accessed=4 * MIB, transcendentals=0
        ),
        name="feed_forward_output",
    )(lengths, middle, active, down, vec, *so_far)


MIDDLE_PARTS = 3


def middle_kernel(tile, slots, items):
    def kernel(
        len_ref, dn2_ref, middle_ref, cot_ref, mixed_ref, wout_ref, vec_ref,
        dmid_ref, dmix_ref, delta_ref, sums_ref, *rest,
    ):
        gouts, (acc, branch) = rest[:-2], rest[-2:]
        part = pl.program_id(0)
        go = len_ref[0] > 0

        @pl.when(part == 0)
        def _():
            sums_ref[...] = jnp.zeros_like(sums_ref)
            acc[...] = jnp.zeros_like(acc)

        scaled, inverse = norm_parts(middle_ref[...])
        d_n2 = dn2_ref[...]
        valid = row_valid(len_ref, part * tile, tile, slots, items)
        d_middle = cot_ref[...].astype(F32) * valid + norm_back(
            d_n2, scaled, inverse, vec_ref[5:6, :]
        )
        dmid_ref[...] = d_middle
        low = d_middle.astype(BF)
        branch[...] = low
        sums_ref[...] += jnp.concatenate(
            [
                jnp.sum(d_n2 * scaled, axis=0, keepdims=True),
                jnp.sum(d_n2, axis=0, keepdims=True),
                jnp.sum(low.astype(F32), axis=0, keepdims=True),
                jnp.zeros((5, D), F32),
            ],
            axis=0,
        )

        @pl.when(go)
        def _():
            dmix_ref[...] = mm_nt(branch[...], wout_ref[...]).astype(BF)

        @pl.when(go)
        def _():
            acc[...] += mm_tn(mixed_ref[...], branch[...])

        @pl.when(go)
        def _():
            product = dmix_ref[...].astype(F32) * mixed_ref[...].astype(F32)
            row = lax.broadcasted_iota(jnp.int32, (D, 128), 0)
            lane = lax.broadcasted_iota(jnp.int32, (D, 128), 1)
            pick = jnp.where(row // HEAD == lane, 1.0, 0.0).astype(BF)
            delta_ref[...] = in_three(mm(product.astype(BF), pick))

        @pl.when(part == MIDDLE_PARTS - 1)
        def _():
            store_halves(gouts, acc[...], len_ref[items], slice(None))

    return kernel


def middle_backward(scalars, d_n2, middle, cotangent, mixed, w_all, vec, fast, items, slots, devices):
    row_count = items * slots
    tile = row_count // MIDDLE_PARTS
    fixed = lambda p, *_: (0, 0)
    block = pl.BlockSpec((tile, D), lambda p, *_: (p, 0))
    outs = split_shapes(fast, devices, D)
    return pl.pallas_call(
        middle_kernel(tile, slots, items),
        grid_spec=pltpu.PrefetchScalarGridSpec(
            num_scalar_prefetch=1,
            grid=(MIDDLE_PARTS,),
            in_specs=[
                block, block, block, block,
                pl.BlockSpec((D, D), fixed),
                pl.BlockSpec((VEC_ROWS, D), fixed),
            ],
            out_specs=[
                block, block,
                pl.BlockSpec((tile, 128), lambda p, *_: (p, 0)),
                pl.BlockSpec((8, D), fixed),
            ]
            + [whole_block(v) for v in outs],
            scratch_shapes=[pltpu.VMEM((D, D), F32), pltpu.VMEM((tile, D), BF)],
        ),
        out_shape=[
            jax.ShapeDtypeStruct((row_count, D), F32),
            jax.ShapeDtypeStruct((row_count, D), BF),
            jax.ShapeDtypeStruct((row_count, 128), BF),
            jax.ShapeDtypeStruct((8, D), F32),
        ]
        + outs,
        compiler_params=pltpu.CompilerParams(vmem_limit_bytes=60 * MIB),
        cost_estimate=pl.CostEstimate(
            flops=10 * row_count * D * D, bytes_accessed=8 * MIB, transcendentals=0
        ),
        name="middle_backward",
    )(scalars, d_n2, middle, cotangent, mixed, w_all, vec)


def backward_kernel(
    len_ref, q_ref, k_ref, v_ref, dmix_ref, lse_ref, delta_ref, key_ref, query_ref, scaled_ref,
    wq_ref, wk_ref, wv_ref, table_ref, *rest, base, so_far, rows,
):
    given, rest = rest[:so_far], rest[so_far:]
    dqkv_ref, gbias_ref, norm_ref, *gws, acc = rest
    g = pl.program_id(0)
    i = pl.program_id(1)
    items = pl.num_programs(1)
    last_item = items - 1
    slots = q_ref.shape[1]
    go = len_ref[0] > 0
    beside = lambda x, y: jnp.concatenate([x, y], axis=1)
    fronts = []
    for pair in range(PAIRS):
        cols = slice(pair * 128, (pair + 1) * 128)
        queries = two_heads(q_ref[0, :, cols], HEAD ** -0.5)
        upstream = two_heads(dmix_ref[0, :, cols], 1.0)
        heads = (2 * pair, 2 * pair + 1)
        marks = jnp.concatenate(
            [lse_ref[0] * offset_lanes(head) + query_ref[0] for head in heads], axis=0
        )
        offsets = jnp.concatenate(
            [delta_ref[0] * offset_lanes(4 * (base + g) + head) for head in heads], axis=0
        )
        fronts.append(
            (
                queries,
                upstream,
                mm_nt(beside(k_ref[0, :, cols], key_ref[0]), beside(queries, marks)),
                mm_nt(beside(v_ref[0, :, cols], key_ref[0]), beside(upstream, offsets)),
            )
        )
    for pair in range(PAIRS):
        queries, upstream, scores, d_probs = fronts[pair]
        dv = dk = None
        turned = []
        flipped = k_ref[0, :, pair * 128 : (pair + 1) * 128].T
        for half in range(2):
            at = slice(half * slots, (half + 1) * slots)
            probs = jnp.exp(scores[:, at])
            d_scores = (probs * d_probs[:, at]).astype(BF)
            dv_half = mm(probs.astype(BF), upstream[at])
            dk_half = mm(d_scores, queries[at])
            dv = dv_half if dv is None else dv + dv_half
            dk = dk_half if dk is None else dk + dk_half
            turned.append(mm(flipped, d_scores))
        row = lax.broadcasted_iota(jnp.int32, (128, 1), 0)
        dq = jnp.where(row < HEAD, turned[0], turned[1]).T * HEAD ** -0.5
        for which, part in ((0, dq), (1, dk), (2, dv)):
            start = which * GROUP + pair * 128
            dqkv_ref[0, :, start : start + 128] = part.astype(BF)

    @pl.when(go)
    def _():
        bias = jnp.sum(dqkv_ref[0].astype(F32), axis=0, keepdims=True)
        before = jnp.where(i == 0, 0.0, gbias_ref[...])
        gbias_ref[...] = before + bias

    @pl.when(i == 0)
    def _():
        acc[...] = mm_tn(scaled_ref[0], dqkv_ref[0])

    @pl.when(i > 0)
    def _():
        acc[...] += mm_tn(scaled_ref[0], dqkv_ref[0])

    @pl.when(i == last_item)
    def _():
        gain = table_ref[:, 0:1].astype(F32)
        shift = table_ref[:, 1:2].astype(F32)
        lane = lax.broadcasted_iota(jnp.int32, (1, SMALL), 1)
        gains = jnp.zeros((D, 1), F32)
        shifts = jnp.zeros((D, 1), F32)
        for which, ref in ((0, wq_ref), (1, wk_ref), (2, wv_ref)):
            cols = slice(which * GROUP, (which + 1) * GROUP)
            total = acc[:, cols]
            sums = gbias_ref[0:1, cols]
            weight = ref[...].astype(F32)
            store_halves(gws, gain * total + shift * sums, len_ref[items], cols)
            gains = gains + jnp.sum(weight * total, axis=-1, keepdims=True)
            shifts = shifts + jnp.sum(weight * sums, axis=-1, keepdims=True)
        new = jnp.where(lane == 0, gains, jnp.where(lane == 1, shifts, 0.0))
        norm_ref[...] = jnp.where(g == 0, 0.0, norm_ref[...]) + new
        if so_far:
            mid_ref, up_ref, down_ref, *before = given
            norms, lines = norm_ref[...], gbias_ref[0:1, :]
            if before:
                norms = norms + before[0][...]
                lines = jnp.concatenate([before[1][0:1, :], lines], axis=1)
            table = small_table(
                norms, lines, mid_ref[...], up_ref[0:1, :], down_ref[0:1, :], rows
            )
            store_halves(gws, table, len_ref[items], slice(D, D + SMALL))


def attention_backward(
    base, count, scalars, q, k, v, d_mixed, lse, delta, key_marks, query_marks, scaled, weights,
    fast, devices, so_far,
):
    items, slots, _ = q.shape
    rows = lambda g, i, *_: (i, 0, 0)
    block = pl.BlockSpec((1, slots, GROUP), lambda g, i, *_: (i, 0, base + g))
    weight = pl.BlockSpec((D, GROUP), lambda g, i, *_: (0, base + g))
    outs = split_shapes(fast, devices, count * D + (SMALL if so_far else 0))
    kernel = functools.partial(
        backward_kernel, base=base, so_far=len(so_far), rows=D // devices
    )
    return pl.pallas_call(
        kernel,
        grid_spec=pltpu.PrefetchScalarGridSpec(
            num_scalar_prefetch=1,
            grid=(count, items),
            in_specs=[
                block, block, block, block,
                pl.BlockSpec((1, slots, 128), lambda g, i, *_: (i, 0, base + g)),
                pl.BlockSpec((1, slots, 128), rows),
                pl.BlockSpec((1, slots, 128), rows),
                pl.BlockSpec((1, slots, 128), rows),
                pl.BlockSpec((1, slots, D), rows),
                weight, weight, weight,
                pl.BlockSpec((D, SMALL), lambda g, i, *_: (0, 0)),
                *[whole_block(v) for v in so_far],
            ],
            out_specs=[
                pl.BlockSpec((1, slots, D), lambda g, i, *_: (i, 0, g)),
                pl.BlockSpec((8, D), lambda g, i, *_: (0, g)),
                pl.BlockSpec((D, SMALL), lambda g, i, *_: (0, 0)),
            ]
            + [
                pl.BlockSpec(
                    v.shape[:-1] + ((D + SMALL) if so_far else D,),
                    lambda g, i, *_, n=len(v.shape): (0,) * (n - 1) + (g,),
                )
                for v in outs
            ],
            scratch_shapes=[pltpu.VMEM((D, D), F32)],
        ),
        out_shape=[
            jax.ShapeDtypeStruct((items, slots, count * D), BF),
            jax.ShapeDtypeStruct((8, count * D), F32),
            jax.ShapeDtypeStruct((D, SMALL), F32),
        ]
        + outs,
        compiler_params=pltpu.CompilerParams(vmem_limit_bytes=60 * MIB),
        cost_estimate=pl.CostEstimate(
            flops=14 * count * items * slots * D * D,
            bytes_accessed=8 * count * MIB,
            transcendentals=count * items * 4 * slots * slots,
        ),
        name="attention_backward",
    )(
        scalars, q, k, v, d_mixed, lse, delta, key_marks, query_marks, scaled,
        *weights, *so_far,
    )


def input_kernel(*refs):
    parts, (*weights, tok_ref, dmid_ref, vec_ref, grad_ref) = refs[:-7], refs[-7:]
    places = [(ref, n) for ref in parts for n in range(ref.shape[2] // D)]
    total = None
    for g in range(GROUPS):
        for which in range(3):
            weight = weights[which][:, g * GROUP : (g + 1) * GROUP]
            ref, n = places[g]
            start = n * D + which * GROUP
            part = mm_nt(ref[0, :, start : start + GROUP], weight)
            total = part if total is None else total + part
    scaled, inverse = norm_parts(tok_ref[0].astype(F32))
    grad_ref[0] = dmid_ref[0] + norm_back(total, scaled, inverse, vec_ref[0:1, :])


def input_backward(d_qkv, weights, tokens, d_middle, vec, after):
    items, slots, _ = tokens.shape
    vec, _after = lax.optimization_barrier((vec, after))
    rows = lambda i: (i, 0, 0)
    fixed = lambda i: (0, 0)
    block = pl.BlockSpec((1, slots, D), rows)
    return pl.pallas_call(
        input_kernel,
        grid=(items,),
        in_specs=[
            *[pl.BlockSpec((1, slots, part.shape[2]), rows) for part in d_qkv],
            *[pl.BlockSpec((D, D), fixed)] * 3,
            block, block,
            pl.BlockSpec((VEC_ROWS, D), fixed),
        ],
        out_specs=block,
        out_shape=jax.ShapeDtypeStruct((items, slots, D), F32),
        compiler_params=pltpu.CompilerParams(vmem_limit_bytes=60 * MIB),
        cost_estimate=pl.CostEstimate(
            flops=10 * items * slots * D * D, bytes_accessed=8 * MIB, transcendentals=0
        ),
        name="input_backward",
    )(*d_qkv, *weights, tokens, d_middle, vec)


def own_kernel(keep_ref, got_ref, *refs):
    rows = keep_ref.shape[0]
    up = refs[:3] if len(refs) > 10 else ()
    qkv_ref, out_ref, *refs = refs[len(up) :]
    total = keep_ref[...] + got_ref[...].astype(F32)
    for which in range(3):
        for g in range(GROUPS):
            start = g * D + which * GROUP
            qkv_ref[:, which * D + g * GROUP : which * D + (g + 1) * GROUP] = total[
                :, start : start + GROUP
            ]
    out_ref[...] = total[:, 3 * D + SMALL :]
    lines = total[:, 3 * D : 3 * D + SMALL].T
    at = 0
    for ref, (_name, count) in zip(refs, COLUMNS):
        ref[...] = jnp.concatenate([lines[at + j : at + j + 1, :] for j in range(count)], axis=1)
        at += count
    for n, ref in enumerate(up[:2]):
        for half in range(2):
            b = 2 * n + half
            own = ref[half * rows : (half + 1) * rows, :]
            got = up[2][b * rows : (b + 1) * rows, :].astype(F32)
            refs[-1][:, b * D : (b + 1) * D] = own + got


def own_grads(keep, got, *up):
    rows = keep.shape[0]
    shapes = [(rows, 3 * D), (rows, D)] + [(1, count * rows) for _name, count in COLUMNS]
    if up:
        shapes.append((rows, STEPS * D))
    return pl.pallas_call(
        own_kernel,
        out_shape=[jax.ShapeDtypeStruct(shape, F32) for shape in shapes],
        compiler_params=pltpu.CompilerParams(vmem_limit_bytes=16 * MIB),
        name="own_grads",
    )(keep, got, *up)


def swap(x, axis, bit, size):
    return lax.ppermute(x, axis, [(i, i ^ (1 << bit)) for i in range(size)])


def own_bit(axis, bit):
    return (lax.axis_index(axis) >> bit) & 1


def doubled(x, axis, bit, size, at):
    other = jnp.expand_dims(swap(x, axis, bit, size), at)
    mine = jnp.expand_dims(x, at)
    return jnp.where(
        own_bit(axis, bit) == 0,
        jnp.concatenate([mine, other], at),
        jnp.concatenate([other, mine], at),
    )


def gather_rows(x, cut, sizes):
    rows = x.shape[0]
    wide, narrow = sizes
    if sizes != (8, 4):
        whole = lax.all_gather(x, AXES, axis=0, tiled=True)
        return [whole[:, :cut]], [whole[:, cut:]]

    def ordered(mine, other, axis, bit, at):
        mine, other = jnp.expand_dims(mine, at), jnp.expand_dims(other, at)
        return jnp.where(
            own_bit(axis, bit) == 0,
            jnp.concatenate([mine, other], at),
            jnp.concatenate([other, mine], at),
        )

    away = lambda mask: lax.ppermute(x, "wide", [(i, i ^ mask) for i in range(wide)])
    near, far, both = away(2), away(4), away(6)
    x = ordered(ordered(x, near, "wide", 1, 0), ordered(far, both, "wide", 1, 0), "wide", 2, 0)
    a, b = x[..., :cut], x[..., cut:]
    a = doubled(a, "wide", 0, wide, 0)
    b = doubled(b, "narrow", 1, narrow, 0)
    a = doubled(a, "narrow", 1, narrow, 0)
    b = doubled(b, "wide", 0, wide, 0)
    flat = lambda t: t.reshape(wide * narrow // 2, rows, -1)
    return [[flat(t), flat(swap(t, "narrow", 0, narrow))] for t in (a, b)]


def fold_kernel(_bits_ref, *refs):
    keeps, gots, outs = refs[:4], refs[4:8], refs[8:]
    for keep, got, out in zip(keeps, gots, outs):
        out[...] = (keep[...].astype(F32) + got[...].astype(F32)).astype(BF)


def fold(scalars, keep, got, cut, items):
    parts, rows, _ = keep.shape
    quads = parts // 4
    side = lambda bits, n, mine: bits[items + n] if mine else 1 - bits[items + n]
    by_x = lambda mine: pl.BlockSpec(
        (1, 2, 1, cut, D), lambda p, bits: (p, 0, side(bits, 1, mine), 0, 0)
    )
    by_y = lambda mine: pl.BlockSpec(
        (1, 1, 2, cut, D), lambda p, bits: (p, side(bits, 2, mine), 0, 1, 0)
    )
    specs = [by_x(False), by_x(True), by_y(False), by_y(True)]
    shapes = [jax.ShapeDtypeStruct((quads, 2, 1, cut, D), BF)] * 2
    shapes += [jax.ShapeDtypeStruct((quads, 1, 2, cut, D), BF)] * 2
    at = lambda p, *_: (p, 0, 0, 0, 0)
    keep, got = (t.reshape(quads, 2, 2, rows, D) for t in (keep, got))
    return pl.pallas_call(
        fold_kernel,
        grid_spec=pltpu.PrefetchScalarGridSpec(
            num_scalar_prefetch=1,
            grid=(quads,),
            in_specs=specs * 2,
            out_specs=[pl.BlockSpec((1,) + v.shape[1:], at) for v in shapes],
        ),
        out_shape=shapes,
        compiler_params=pltpu.CompilerParams(vmem_limit_bytes=60 * MIB),
        cost_estimate=pl.CostEstimate(flops=1, bytes_accessed=14 * MIB, transcendentals=0),
        name="fold",
    )(scalars, *[keep] * 4, *[got] * 4)


def together(*values):
    return lax.optimization_barrier(values)


def halves(keep, got, axis, bit, at, kind=F32):
    me = own_bit(axis, bit)

    def half(which):
        part = lambda x: lax.dynamic_index_in_dim(x, which, at, keepdims=False).astype(F32)
        return part(keep) if got is None else part(keep) + part(got)

    return half(1 - me).astype(BF), half(me).astype(kind)


def body(sizes):
    def run(
        tokens, lengths, blocks, ln1_gain, ln1_bias, qkv_weight, qv_bias, out_weight, out_bias,
        ln2_gain, ln2_bias, up_weight, up_bias, down_weight, down_bias, cotangent,
    ):
        items, slots, _ = tokens.shape
        row_count = items * slots
        rows = qkv_weight.shape[0]
        devices = sizes[0] * sizes[1]
        stacked = sizes == (8, 4)

        vectors = (
            ln1_gain, ln1_bias, qv_bias, out_bias, ln2_gain, ln2_bias, up_bias, down_bias,
        )
        first, *rest = pack_parameters(
            vectors, qkv_weight, out_weight, up_weight, down_weight, stacked
        )
        first, later_blocks = lax.optimization_barrier((first, blocks))
        key_marks, query_marks = mask_marks(lengths, later_blocks)
        if stacked:
            whole = lax.all_gather(rest[0], AXES, axis=0, tiled=True)
            up = down = whole.reshape(devices, 8 * rows, D)
        else:
            up = lax.all_gather(up_weight, AXES, axis=0, tiled=True)
            down = lax.all_gather(down_weight, AXES, axis=0, tiled=True)
        bits = [own_bit("narrow", 0), own_bit("narrow", 1), own_bit("wide", 0)]
        scalars = jnp.concatenate([lengths, jnp.stack(bits).astype(lengths.dtype)])
        first = gather_rows(first, 2 * D, sizes)

        scaled, q, k, v, mixed, lse, vec, w_q, w_k, w_v, w_out, table = attention_forward(
            scalars, tokens, first, key_marks, query_marks, rows
        )
        flat = lambda t: t.reshape(row_count, D)
        cube = lambda t: t.reshape(items, slots, D)
        middle, normed, d_lower, gb_down = middle_forward(
            lengths, flat(mixed), flat(tokens), flat(cotangent), w_out, vec, items, slots
        )
        wide, narrow = sizes
        fast = sizes == (8, 4)
        active, d_n2, gb_up, *ffn = feed_forward(
            scalars, normed, d_lower, vec, up, down, fast, items, slots
        )

        def middle_part():
            return middle_backward(
                scalars, d_n2, middle, flat(cotangent), flat(mixed), w_out, vec, fast, items,
                slots, devices,
            )

        def attention_part(base, count, d_mixed, delta, so_far=()):
            d_qkv, sums, norms, *grads = attention_backward(
                base, count, scalars, q, k, v, cube(d_mixed), lse,
                delta.reshape(items, slots, 128), key_marks, query_marks, scaled,
                (w_q, w_k, w_v, table), fast, devices, so_far,
            )
            return d_qkv, sums, norms, grads

        def input_part(d_qkv, d_middle, after):
            return input_backward(
                d_qkv, (w_q, w_k, w_v), tokens, cube(d_middle), vec, after
            )

        def output_part(after):
            return feed_forward_output(
                0, PARTS, lengths, middle, active, down, vec, fast, items, slots, (), after
            )

        def rest_of_backward():
            core = ("narrow", 0, narrow)
            x_link, y_link = ("narrow", 1), ("wide", 0)
            z_near, z_far = ("wide", 1), ("wide", 2)
            size = {"wide": wide, "narrow": narrow}
            move = lambda value, link: swap(value, *link, size[link[0]])
            beside = lambda *parts: jnp.concatenate(parts, axis=-1)
            cut = 2 * rows

            up_got = swap(ffn[1], *core)
            d_middle, d_mixed, delta, mid_sums, *g_out = middle_part()
            up_got, d_mixed, *g_out = together(up_got, d_mixed, *g_out)
            out_got = swap(g_out[0], *core)
            c_send, c_keep, d_send, d_keep = fold(scalars, ffn[2], up_got, cut, items)
            c_send, d_send, d_mixed = together(c_send, d_send, d_mixed)
            c_got, d_got = move(c_send, x_link), move(d_send, y_link)
            d_qkv, sums, norms, grads = attention_part(0, 2, d_mixed, delta)
            c_got, d_got, out_got, c_keep, d_keep, d_mixed, grads[0], norms = together(
                c_got, d_got, out_got, c_keep, d_keep, d_mixed, grads[0], norms
            )
            shaped = lambda t: t.reshape((2, 2, 2, cut, D))
            c_send, c_keep = halves(shaped(c_keep), shaped(c_got), *y_link, 2, BF)
            d_send, d_keep = halves(shaped(d_keep), shaped(d_got), *x_link, 2, BF)
            c_send, d_send, c_keep, d_keep, d_mixed, out_got = together(
                c_send, d_send, c_keep, d_keep, d_mixed, out_got
            )
            c_got, d_got = move(c_send, y_link), move(d_send, x_link)
            a_got = swap(grads[0], *core)
            d_qkv_2, _sums, _norms, grads_2 = attention_part(
                2, 1, d_mixed, delta, (mid_sums, gb_up, gb_down, norms, sums)
            )
            c_got, d_got, a_got, c_keep, d_keep, out_got, grads_2[0] = together(
                c_got, d_got, a_got, c_keep, d_keep, out_got, grads_2[0]
            )

            shaped = lambda t: t.reshape((2, 2, 2, 2, rows, -1))
            b_got = swap(grads_2[0], *core)
            c_send, c_keep = halves(c_keep, c_got, *z_near, 1)
            d_send, d_keep = halves(d_keep, d_got, *z_near, 1)
            send = jnp.concatenate([c_send, d_send], axis=-2)
            up_got = move(send, z_near)
            a_send, a_keep = halves(shaped(grads[1]), shaped(a_got), *x_link, 3)
            out_send, out_keep = halves(shaped(g_out[1]), shaped(out_got), *y_link, 2)
            b_got, a_send, out_send, send = together(b_got, a_send, out_send, send)
            b_send, b_keep = halves(
                shaped(grads_2[1]), shaped(b_got), *y_link, 2
            )
            b_send, b_keep = beside(b_send, out_send), beside(b_keep, out_keep)
            a_send, b_send = together(a_send, b_send)
            a_got, b_got = move(a_send, x_link), move(b_send, y_link)
            input_grad = input_part([d_qkv, d_qkv_2], d_middle, (a_send, b_send))
            a_got, b_got, up_got, input_grad = together(a_got, b_got, up_got, input_grad)
            a_send, a_keep = halves(a_keep, a_got, *y_link, 2)
            b_send, b_keep = halves(b_keep, b_got, *x_link, 2)
            c_send, c_keep = halves(c_keep, up_got[:, :cut], *z_far, 0)
            d_send, d_keep = halves(d_keep, up_got[:, cut:], *z_far, 0)
            send = jnp.concatenate([c_send, d_send], axis=-2)
            a_send, b_send, send = together(a_send, b_send, send)
            a_got, b_got = move(a_send, y_link), move(b_send, x_link)
            up_got = move(send, z_far)
            output = output_part((a_send, b_send))
            a_got, b_got, up_got, output = together(a_got, b_got, up_got, output)
            send, keep = halves(beside(a_keep, b_keep), beside(a_got, b_got), *z_near, 1)
            got = move(send, z_near)
            send, keep = halves(keep, got, *z_far, 0)
            got = move(send, z_far)
            return [input_grad, output, *own_grads(keep, got, c_keep, d_keep, up_got)]

        if not fast:
            scatter = lambda x: lax.psum_scatter(
                x.astype(F32), AXES, scatter_dimension=0, tiled=True
            )
            grad_up, grad_down = scatter(ffn[0]), scatter(ffn[1])
            d_middle, d_mixed, delta, mid_sums, *g_out = middle_part()
            d_qkv, sums, norms, grads = attention_part(0, 2, d_mixed, delta)
            d_qkv_2, _sums, _norms, grads_2 = attention_part(
                2, 1, d_mixed, delta, (mid_sums, gb_up, gb_down, norms, sums)
            )
            input_grad = input_part([d_qkv, d_qkv_2], d_middle, ())
            output = output_part(())
            keep = scatter(jnp.concatenate([grads[0], grads_2[0], g_out[0]], axis=1))
            own_qkv, own_out, *own_small = own_grads(keep, jnp.zeros(keep.shape, BF))
        else:
            grad_down = lax.psum_scatter(
                ffn[0].reshape(STEPS * D, D), AXES, scatter_dimension=0, tiled=True
            ).astype(F32)
            shapes = jax.eval_shape(rest_of_backward)
            input_grad, output, own_qkv, own_out, *own_small, grad_up = lax.cond(
                scalars[0] > 0,
                rest_of_backward,
                lambda: [jnp.zeros(v.shape, v.dtype) for v in shapes],
            )
        ln1_g, ln1_b, qv_b, out_b, ln2_g, ln2_b, up_b, down_b = [v.reshape(-1) for v in own_small]
        return (
            cube(output), input_grad, ln1_g, ln1_b, own_qkv, qv_b, own_out, out_b, ln2_g, ln2_b,
            grad_up, up_b, grad_down, down_b,
        )

    return run


def solution(mesh):
    sizes = (mesh.shape["wide"], mesh.shape["narrow"])
    one = P(AXES)
    two = P(AXES, None)
    three = P(AXES, None, None)
    return jax.shard_map(
        body(sizes),
        mesh=mesh,
        in_specs=(
            three, one, two, one, one, two, one, two, one, one, one, two, one, two, one, three,
        ),
        out_specs=(
            three, three, one, one, two, one, two, one, one, one, two, one, two, one,
        ),
        check_vma=False,
    )
```
